128 devices in a mesh: row: 8 (over x, z_hi), col: 16 (over y, z_lo, core).
Axes of the slice: x: 4, y: 4, z: 4 (z_hi: 2, z_lo: 2; z = z_hi * 2 + z_lo), core: 2. Of those that a mesh axis runs over, the one named last changes fastest.
Arguments:
- amplitudes: float32 [12800, 12800], P('row', 'col'), may hold values from -0.0546875 to 0.0546875
- aux_left: float32 [12800, 1280], P('col'), may hold values from -12 to 12
- aux_right: float32 [12800, 1280], P('col'), may hold values from -0.3125 to 0.3125
- left_rotation: float32 [320, 320], replicated, may hold values from -0.3125 to 0.3125
- right_rotation: float32 [320, 320], replicated, may hold values from -0.3125 to 0.3125
- occ_energy: float32 [40], replicated, may hold values from -2 to -0.5
- vir_energy: float32 [320], replicated, may hold values from 0.5 to 4
Outputs:
- residual_update: float32 [320, 40, 40, 320], P('col', 'row')
The draws below stay inside these ranges and needn't reach their ends.
All inputs are finite; a program needn't handle non-finite values.
Results may differ from the reference program's by a relative error of at most 0.00007.
Values sent between devices are 32-bit elements; how exact they have to be, the bound alone decides.
A program may use at most 192 MiB of HBM per device.

```python
import math
import jax
import jax.numpy as jnp
from jax import lax

NOCC = 40
NVIR = 320
NAUX = 1280


def steps_of(stream_key, shape, cuts, least, high):
    factor_of, own = 1.0, jax.random.fold_in(stream_key, 6)
    for position, parts in cuts:
        draws = jnp.exp(jax.random.uniform(jax.random.fold_in(own, position), (parts,), jnp.float32, least / len(cuts), high / len(cuts)))
        factor_of = factor_of * jnp.repeat(draws, shape[position] // parts).reshape([-1 if axis == position else 1 for axis in range(len(shape))])
    return factor_of


def gaussian(rng, extent, spread, bound, cuts=(), held_as=jnp.bfloat16):
    result = spread * jax.random.normal(rng, extent, jnp.float32)
    if cuts:
        result = result * steps_of(rng, extent, cuts, -0.22, 0.18)
    return jnp.clip(result, -bound, bound).astype(held_as)


def setup_inputs(seed: int = 0) -> dict:
    arg_keys = jax.random.split(jax.random.key(seed), 8)
    return {
        "amplitudes": gaussian(arg_keys[0], (NVIR * NOCC, NVIR * NOCC), (NVIR * NOCC) ** -0.5, 0.0546875, ((0, 8), (1, 16)), jnp.float32),
        "aux_left": gaussian(arg_keys[1], (NVIR * NOCC, NAUX), 2.0, 12.0, ((0, 16),), jnp.float32),
        "aux_right": gaussian(arg_keys[2], (NVIR * NOCC, NAUX), (NAUX // 4) ** -0.5, 0.3125, ((0, 16),), jnp.float32),
        "left_rotation": gaussian(arg_keys[3], (NVIR, NVIR), NVIR ** -0.5, 0.3125, (), jnp.float32),
        "right_rotation": gaussian(arg_keys[4], (NVIR, NVIR), NVIR ** -0.5, 0.3125, (), jnp.float32),
        "occ_energy": jnp.clip(jax.random.uniform(arg_keys[5], (NOCC,), jnp.float32, -2.0, -0.5), -2.0, -0.5),
        "vir_energy": jnp.clip(jnp.exp(jax.random.uniform(arg_keys[6], (NVIR,), jnp.float32, math.log(0.5), math.log(4.0))), 0.5, 4.0),
    }


def reference(amplitudes, aux_left, aux_right, left_rotation, right_rotation, occ_energy, vir_energy):
    highest = lax.Precision.HIGHEST
    fitted = jnp.dot(amplitudes, aux_left, precision=highest, preferred_element_type=jnp.float32)
    paired = lax.dot_general(fitted, aux_right, (((1,), (1,)), ((), ())), precision=highest, preferred_element_type=jnp.float32)
    summed = paired + paired.T
    half_rot = jnp.dot(left_rotation, summed.reshape(NVIR, NOCC * NVIR * NOCC), precision=highest, preferred_element_type=jnp.float32)
    rotated = jnp.einsum("aibj,Bb->aijB", half_rot.reshape(NVIR, NOCC, NVIR, NOCC), right_rotation, precision=highest)
    denominator = (vir_energy[:, None, None, None] + vir_energy[None, None, None, :]
                   - occ_energy[None, :, None, None] - occ_energy[None, None, :, None])
    return rotated / denominator
```

```python
import functools

import jax
import jax.numpy as jnp
from jax import lax
from jax.experimental import pallas as pl
from jax.experimental.pallas import tpu as pltpu
from jax.sharding import PartitionSpec as P

MESH = pl.DeviceIdType.MESH
F32 = jnp.float32
BF16 = jnp.bfloat16
WIDE = 256


def halves(x):
    hi = x.astype(BF16)
    return hi, (x - hi.astype(F32)).astype(BF16)


def dot3(xh, xl, yh, yl, dims):
    def dot(a, b):
        return lax.dot_general(a, b, (dims, ((), ())), preferred_element_type=F32)

    return dot(xl, yh) + dot(xh, yl) + dot(xh, yh)


def up(n, unit):
    return -(-n // unit) * unit


def planes(src, dst):
    width, rows = src.shape[1], 40 if src.shape[0] % 40 == 0 else src.shape[0]

    def one(g, _):
        at = pl.ds(pl.multiple_of(g * rows, 8), rows)
        for p in range(dst.shape[0]):
            n = min(128, width - p * 128)
            dst[p, at, :n] = src[at, p * 128 : p * 128 + n]
        return 0

    lax.fori_loop(0, src.shape[0] // rows, one, 0)


def every(src, start, count, stride, width):
    parts = [src[p, pl.ds(start, count, stride=stride), :] for p in range(src.shape[0])]
    return jnp.concatenate(parts, axis=1)[:, :width]


def gather_kernel(
    nr, occ,
    t_ref, b_ref, z_ref,
    fg_ref, zg_ref,
    tp, zp, bh, bl, sib_send, sib_recv, own, rs_recv, fp, zs_send, zs_recv, zc,
    sib_s, sib_r, rs_s, rs_r, zs_s, zs_r, za_s, za_r, fa_s, fa_r, loc,
):
    r, c = lax.axis_index("row"), lax.axis_index("col")
    t, k = c // 2, lax.rem(c, 2)
    sib = c + 1 - 2 * k
    og = occ // nr
    va = t_ref.shape[0] // occ
    vc = z_ref.shape[0] // occ
    half = b_ref.shape[1] // 2
    blk = lax.rem(t - r + nr, nr)
    is_own = lax.rem(r + r, nr) == t

    barrier = pltpu.get_barrier_semaphore()
    pl.semaphore_signal(barrier, inc=1, device_id=(r, sib), device_id_type=MESH)

    def greet(s, _):
        peer = lax.rem(t + 1 + s, nr)
        pl.semaphore_signal(barrier, inc=1, device_id=(r, 2 * peer + k), device_id_type=MESH)
        return 0

    lax.fori_loop(0, nr - 1, greet, 0)

    def greet_sources(s, _):
        @pl.when(jnp.logical_not(jnp.logical_and(is_own, s == t)))
        def _():
            pl.semaphore_signal(barrier, inc=1, device_id=(blk, 2 * s + k), device_id_type=MESH)

        return 0

    lax.fori_loop(0, nr, greet_sources, 0)

    planes(t_ref, tp)
    planes(z_ref, zp)
    mine, other = pl.ds(pl.multiple_of(k * half, half), half), pl.ds(pl.multiple_of((1 - k) * half, half), half)
    for at, cols in ((0, other), (half, mine)):
        hi, lo = halves(b_ref[:, cols])
        bh[:, at : at + half] = hi
        bl[:, at : at + half] = lo

    first = k == 0
    kept = []
    for jj in range(og):
        z = every(zp, r * og + jj, vc, occ, z_ref.shape[1])
        z0, z1 = z[:, :half], z[:, half:]
        zs_send[jj] = jnp.where(first, z1, z0)
        kept.append(jnp.where(first, z0, z1))
        zc[jj * va : jj * va + vc, :] = kept[-1]

    @pl.when(is_own)
    def _():
        pl.semaphore_wait(barrier, 2 * nr - 1)

    @pl.when(jnp.logical_not(is_own))
    def _():
        pl.semaphore_wait(barrier, 2 * nr)

    z_swap = pltpu.make_async_remote_copy(
        src_ref=zs_send, dst_ref=zs_recv, send_sem=zs_s, recv_sem=zs_r,
        device_id=(r, sib), device_id_type=MESH,
    )
    z_swap.start()
    z_swap.wait()
    for jj in range(og):
        z_mine = zc[jj * va : jj * va + vc, :]
        z_sib = zs_recv[jj]
        zc[jj * va : (jj + 1) * va, :] = jnp.concatenate(
            [jnp.where(first, z_mine, z_sib), jnp.where(first, z_sib, z_mine)], axis=0
        )

    def spread(src, dst, slot, send, recv, s):
        peer = lax.rem(t + 1 + s, nr)
        return pltpu.make_async_remote_copy(
            src_ref=src, dst_ref=dst.at[slot], send_sem=send.at[s], recv_sem=recv.at[slot],
            device_id=(r, 2 * peer + k), device_id_type=MESH,
        )

    def z_start(s, _):
        spread(zc, zg_ref, t, za_s, za_r, s).start()
        return 0

    lax.fori_loop(0, nr - 1, z_start, 0)
    z_own = pltpu.make_async_copy(zc, zg_ref.at[t], loc.at[0])
    z_own.start()

    def to_sibling(s):
        return pltpu.make_async_remote_copy(
            src_ref=sib_send.at[s], dst_ref=sib_recv.at[s], send_sem=sib_s.at[s], recv_sem=sib_r.at[s],
            device_id=(r, sib), device_id_type=MESH,
        )

    def to_owner(s):
        dst = lax.rem(r + 1 + s, nr)
        return pltpu.make_async_remote_copy(
            src_ref=own.at[s], dst_ref=rs_recv.at[t], send_sem=rs_s.at[s], recv_sem=rs_r.at[t],
            device_id=(dst, 2 * lax.rem(r + dst, nr) + k), device_id_type=MESH,
        )

    last_is_own = is_own

    def finish(s):
        to_sibling(s).wait_recv()
        own[s] = own[s] + sib_recv[s]
        here = jnp.logical_and(s == nr - 1, last_is_own)

        @pl.when(here)
        def _():
            rs_recv[t] = own[s]

        @pl.when(jnp.logical_not(here))
        def _():
            to_owner(s).start()

    def step(s, _):
        dst = lax.rem(r + 1 + s, nr)
        x = jnp.concatenate(
            [every(tp, dst * og + ii, va, occ, t_ref.shape[1]) for ii in range(og)], axis=0
        )
        xh, xl = halves(x)
        part = dot3(xh, xl, bh[...], bl[...], ((1,), (0,)))
        sib_send[s] = part[:, :half]
        own[s] = part[:, half:]
        to_sibling(s).start()

        @pl.when(s > 0)
        def _():
            finish(s - 1)

        return 0

    lax.fori_loop(0, nr, step, 0)
    finish(nr - 1)

    def arrived(s, _):
        @pl.when(jnp.logical_not(jnp.logical_and(is_own, s == t)))
        def _():
            pltpu.make_async_remote_copy(
                src_ref=own.at[0], dst_ref=rs_recv.at[s], send_sem=rs_s.at[0], recv_sem=rs_r.at[s],
                device_id=(r, sib), device_id_type=MESH,
            ).wait_recv()

        return 0

    lax.fori_loop(0, nr, arrived, 0)

    def add_up(g, _):
        rows = pl.ds(pl.multiple_of(g * 8, 8), 8)
        total = rs_recv[0, rows, :]
        for s in range(1, nr):
            total = total + rs_recv[s, rows, :]
        fp[rows, :] = total
        return 0

    lax.fori_loop(0, fp.shape[0] // 8, add_up, 0)

    def f_start(s, _):
        spread(fp, fg_ref, blk, fa_s, fa_r, s).start()
        return 0

    lax.fori_loop(0, nr - 1, f_start, 0)
    f_own = pltpu.make_async_copy(fp, fg_ref.at[blk], loc.at[1])
    f_own.start()

    def settle(s, _):
        peer = lax.rem(t + 1 + s, nr)
        spread(zc, zg_ref, peer, za_s, za_r, s).wait()
        spread(fp, fg_ref, lax.rem(peer - r + nr, nr), fa_s, fa_r, s).wait()
        return 0

    lax.fori_loop(0, nr - 1, settle, 0)

    def sent(s, _):
        to_sibling(s).wait_send()

        @pl.when(jnp.logical_not(jnp.logical_and(s == nr - 1, last_is_own)))
        def _():
            to_owner(s).wait_send()

        return 0

    lax.fori_loop(0, nr, sent, 0)
    z_own.wait()
    f_own.wait()


def tile_kernel(
    nr, og, vc, tiles,
    fg_ref, zg_ref, l_ref, r_ref, rowd_ref, cold_ref,
    out_ref,
    rh, rl, yh, yl, xp, xo, xg, xh, xl, s_send, s_recv, own,
    xs, xr, ss, sr, os_, or_, loc,
):
    r, c = lax.axis_index("row"), lax.axis_index("col")
    t, k = c // 2, lax.rem(c, 2)
    sib = c + 1 - 2 * k
    half = fg_ref.shape[2]
    vir = r_ref.shape[0]
    va = vir // nr
    pad = xo.shape[1] // 2
    wide_pad = xh.shape[1] // nr

    barrier = pltpu.get_barrier_semaphore()
    pl.semaphore_signal(barrier, inc=1, device_id=(r, sib), device_id_type=MESH)

    def greet(s, _):
        pl.semaphore_signal(barrier, inc=1, device_id=(lax.rem(r + 1 + s, nr), c), device_id_type=MESH)
        return 0

    lax.fori_loop(0, nr - 1, greet, 0)

    hi, lo = halves(r_ref[...])
    rh[...] = hi
    rl[...] = lo
    lh, ll = halves(l_ref[pl.ds(pl.multiple_of(t * va, 8), va), :])
    xp[...] = jnp.zeros_like(xp)
    pl.semaphore_wait(barrier, nr)

    def x_copy(q, s):
        return pltpu.make_async_remote_copy(
            src_ref=xo.at[q], dst_ref=xg.at[r, q], send_sem=xs.at[q, s], recv_sem=xr.at[q, r],
            device_id=(lax.rem(r + 1 + s, nr), c), device_id_type=MESH,
        )

    def x_wait(q, s):
        src = lax.rem(r + 1 + s, nr)
        return pltpu.make_async_remote_copy(
            src_ref=xo.at[q], dst_ref=xg.at[src, q], send_sem=xs.at[q, s], recv_sem=xr.at[q, src],
            device_id=(src, c), device_id_type=MESH,
        )

    for q, g_ref in ((1, zg_ref), (0, fg_ref)):
        y_at = (1 - q) * half
        for ii in range(og):
            gh, gl = halves(g_ref[:, ii * va : (ii + 1) * va, :].reshape(vir, half))
            x = dot3(lh, ll, gh, gl, ((1,), (0,)))
            for par in range(2):
                for p in range(half // 128):
                    xp[p, pl.ds(par * pad + ii, vc, stride=og), :] = x[
                        par * vc : (par + 1) * vc, p * 128 : (p + 1) * 128
                    ]
            y = dot3(rh[...], rl[...], gh, gl, ((1,), (0,)))
            hi, lo = halves(y)
            yh[ii * vir : (ii + 1) * vir, y_at : y_at + half] = hi
            yl[ii * vir : (ii + 1) * vir, y_at : y_at + half] = lo

        for p in range(half // 128):
            xo[q, :, p * 128 : (p + 1) * 128] = xp[p]

        def x_start(s, _, q=q):
            x_copy(q, s).start()
            return 0

        lax.fori_loop(0, nr - 1, x_start, 0)

    def take(src, q, load):
        x_at = q * half
        at = pl.multiple_of(src * wide_pad, 16)
        for par in range(2):
            hi, lo = halves(load(par))
            xh[par, pl.ds(at, pad), x_at : x_at + half] = hi
            xl[par, pl.ds(at, pad), x_at : x_at + half] = lo

    for q in (1, 0):
        take(r, q, lambda par, q=q: xo[q, par * pad : (par + 1) * pad, :])

        def x_take(s, _, q=q):
            src = lax.rem(r + 1 + s, nr)
            x_wait(q, s).wait_recv()
            take(src, q, lambda par: xg[src, q, par * pad : (par + 1) * pad, :])
            return 0

        lax.fori_loop(0, nr - 1, x_take, 0)

    def to_sibling(n, width):
        return pltpu.make_async_remote_copy(
            src_ref=s_send.at[lax.rem(n, 2), :, pl.ds(0, width)], dst_ref=s_recv.at[n, :, pl.ds(0, width)],
            send_sem=ss.at[lax.rem(n, 2)], recv_sem=sr.at[n],
            device_id=(r, sib), device_id_type=MESH,
        )

    def to_row(n, width, s, src):
        dst = lax.rem(r + 1 + s, nr)
        cols = pl.ds(pl.multiple_of(n * WIDE, 128), width)
        return pltpu.make_async_remote_copy(
            src_ref=own.at[pl.ds(pl.multiple_of(dst * wide_pad, 8), pad), cols],
            dst_ref=out_ref.at[src, :, cols],
            send_sem=os_.at[n, s], recv_sem=or_.at[n, src],
            device_id=(dst, c), device_id_type=MESH,
        )

    def stay(n, width):
        cols = pl.ds(pl.multiple_of(n * WIDE, 128), width)
        return pltpu.make_async_copy(
            own.at[pl.ds(pl.multiple_of(r * wide_pad, 8), pad), cols], out_ref.at[r, :, cols], loc.at[n]
        )

    def tile(n, width, slot_used):
        rows = pl.ds(pl.multiple_of(n * WIDE, 128), width)
        wh, wl = yh[rows, :], yl[rows, :]

        def product(par):
            return dot3(xh[par], xl[par], wh, wl, ((1,), (1,)))

        @pl.when(slot_used)
        def _():
            to_sibling(n - 2, WIDE).wait_send()

        s_send[lax.rem(n, 2), :, 0:width] = product(1 - k)
        to_sibling(n, width).start()
        own[:, rows] = product(k)
        to_sibling(n, width).wait_recv()
        reps = width // 128

        def close(g, _):
            at = pl.ds(pl.multiple_of(g * 8, 8), 8)
            rowd = rowd_ref[at, :]
            for m in range(reps):
                cols = pl.ds(pl.multiple_of(n * WIDE + m * 128, 128), 128)
                here = own[at, cols] + s_recv[n, at, m * 128 : (m + 1) * 128]
                own[at, cols] = here / (rowd + cold_ref[:, cols])
            return 0

        lax.fori_loop(0, own.shape[0] // 8, close, 0)

        def send(s, _):
            to_row(n, width, s, r).start()
            return 0

        lax.fori_loop(0, nr - 1, send, 0)
        stay(n, width).start()

    tail = yh.shape[0] - (tiles - 1) * WIDE

    def full(n, _):
        tile(n, WIDE, n > 1)
        return 0

    lax.fori_loop(0, tiles - 1, full, 0)
    tile(jnp.int32(tiles - 1), tail, tiles > 2)

    def settle(n, width):
        def one(s, _):
            src = lax.rem(r + 1 + s, nr)
            to_row(n, width, s, src).wait()
            return 0

        lax.fori_loop(0, nr - 1, one, 0)
        stay(n, width).wait()

    def settle_full(n, _):
        settle(n, WIDE)
        return 0

    lax.fori_loop(0, tiles - 1, settle_full, 0)
    settle(jnp.int32(tiles - 1), tail)
    to_sibling(jnp.int32(tiles - 2), WIDE).wait_send()
    to_sibling(jnp.int32(tiles - 1), tail).wait_send()
    for q in (1, 0):
        def x_sent(s, _, q=q):
            x_copy(q, s).wait_send()
            return 0

        lax.fori_loop(0, nr - 1, x_sent, 0)


def lay_kernel(nr, og, vir, occ, in_ref, out_ref, op):
    count, wide = op.shape[0], in_ref.shape[2]
    for src in range(nr):
        for jj in range(og):
            for p in range(count):
                start = jj * vir + p * 128
                n = min(128, wide - start)
                v = in_ref[src, :, start : start + n]
                if n < 128:
                    v = jnp.concatenate([v, jnp.zeros((8, 128 - n), F32)], axis=1)
                op[p, pl.ds(src * og + jj, 8, stride=occ), :] = v
    for p in range(count):
        n = min(128, vir - p * 128)
        out_ref[:, p * 128 : p * 128 + n] = op[p, :, :n]


def shards(amplitudes, aux_left, aux_right, left_rotation, right_rotation, occ_energy, vir_energy):
    nr, nc = lax.axis_size("row"), lax.axis_size("col")
    occ, vir = occ_energy.shape[0], vir_energy.shape[0]
    naux = aux_left.shape[1]
    half = naux // 2
    og, va, vc = occ // nr, vir // nr, vir // nc
    piece = og * va
    dma = pltpu.SemaphoreType.DMA
    vmem = pl.BlockSpec(memory_space=pltpu.VMEM)
    hbm = pl.BlockSpec(memory_space=pl.ANY)
    limit = 60 * 1024 * 1024

    fg, zg = pl.pallas_call(
        functools.partial(gather_kernel, nr, occ),
        out_shape=[jax.ShapeDtypeStruct((nr, piece, half), F32)] * 2,
        in_specs=[vmem] * 3,
        out_specs=[hbm] * 2,
        scratch_shapes=[
            pltpu.VMEM((up(amplitudes.shape[1], 128) // 128, amplitudes.shape[0], 128), F32),
            pltpu.VMEM((up(naux, 128) // 128, aux_right.shape[0], 128), F32),
            pltpu.VMEM((aux_left.shape[0], naux), BF16),
            pltpu.VMEM((aux_left.shape[0], naux), BF16),
            pltpu.VMEM((nr, piece, half), F32),
            pltpu.VMEM((nr, piece, half), F32),
            pltpu.VMEM((nr, piece, half), F32),
            pltpu.VMEM((nr, piece, half), F32),
            pltpu.VMEM((piece, half), F32),
            pltpu.VMEM((og, vc, half), F32),
            pltpu.VMEM((og, vc, half), F32),
            pltpu.VMEM((piece, half), F32),
            dma((nr,)), dma((nr,)), dma((nr,)), dma((nr,)), dma, dma,
            dma((nr,)), dma((nr,)), dma((nr,)), dma((nr,)), dma((2,)),
        ],
        compiler_params=pltpu.CompilerParams(collective_id=0, has_side_effects=True, vmem_limit_bytes=limit),
        name="fit_gather",
    )(amplitudes, aux_left, aux_right)

    rows = vc * og
    pad, wide_pad = up(rows, 8), up(rows, 16)
    cols = og * vir
    cols_pad = up(cols, 128)
    tiles = up(cols_pad, WIDE) // WIDE
    r, c = lax.axis_index("row"), lax.axis_index("col")
    vir_here = lax.dynamic_slice_in_dim(vir_energy, c * vc, vc)
    occ_here = lax.dynamic_slice_in_dim(occ_energy, r * og, og)
    rowd = (vir_here[None, :, None] - occ_energy.reshape(nr, 1, og)).reshape(nr, rows)
    rowd = jnp.pad(rowd, ((0, 0), (0, wide_pad - rows)), constant_values=1.0).reshape(nr * wide_pad, 1)
    rowd = jnp.broadcast_to(rowd, (nr * wide_pad, 128))
    cold = (vir_energy[None, :] - occ_here[:, None]).reshape(1, cols)
    cold = jnp.pad(cold, ((0, 0), (0, cols_pad - cols)), constant_values=1.0)
    cold = jnp.broadcast_to(cold, (8, cols_pad))

    moved = pl.pallas_call(
        functools.partial(tile_kernel, nr, og, vc, tiles),
        out_shape=jax.ShapeDtypeStruct((nr, pad, cols_pad), F32),
        in_specs=[vmem] * 6,
        out_specs=hbm,
        scratch_shapes=[
            pltpu.VMEM((vir, vir), BF16),
            pltpu.VMEM((vir, vir), BF16),
            pltpu.VMEM((cols_pad, naux), BF16),
            pltpu.VMEM((cols_pad, naux), BF16),
            pltpu.VMEM((half // 128, 2 * pad, 128), F32),
            pltpu.VMEM((2, 2 * pad, half), F32),
            pltpu.VMEM((nr, 2, 2 * pad, half), F32),
            pltpu.VMEM((2, nr * wide_pad, naux), BF16),
            pltpu.VMEM((2, nr * wide_pad, naux), BF16),
            pltpu.VMEM((2, nr * wide_pad, WIDE), F32),
            pltpu.VMEM((tiles, nr * wide_pad, WIDE), F32),
            pltpu.VMEM((nr * wide_pad, cols_pad), F32),
            dma((2, nr)), dma((2, nr)), dma((2,)), dma((tiles,)),
            dma((tiles, nr)), dma((tiles, nr)), dma((tiles,)),
        ],
        compiler_params=pltpu.CompilerParams(collective_id=1, has_side_effects=True, vmem_limit_bytes=limit),
        name="tile_exchange",
    )(fg, zg, left_rotation, right_rotation, rowd, cold)

    out = pl.pallas_call(
        functools.partial(lay_kernel, nr, og, vir, occ),
        grid=(pad // 8,),
        out_shape=jax.ShapeDtypeStruct((rows * occ, vir), F32),
        in_specs=[pl.BlockSpec((nr, 8, cols_pad), lambda g: (0, g, 0))],
        out_specs=pl.BlockSpec((8 * occ, vir), lambda g: (g, 0)),
        scratch_shapes=[pltpu.VMEM((up(vir, 128) // 128, 8 * occ, 128), F32)],
        compiler_params=pltpu.CompilerParams(vmem_limit_bytes=limit),
        name="lay_out",
    )(moved)
    return out.reshape(vc, og, occ, vir)


def solution(mesh):
    placed = (P("row", "col"), P("col", None), P("col", None), P(), P(), P(), P())
    return jax.shard_map(
        shards, mesh=mesh, in_specs=placed, out_specs=P("col", "row", None, None), check_vma=False
    )
```

```python
import functools

import jax
import jax.numpy as jnp
from jax import lax
from jax.experimental import pallas as pl
from jax.experimental.pallas import tpu as pltpu
from jax.sharding import PartitionSpec as P

MESH = pl.DeviceIdType.MESH
F32 = jnp.float32
BF16 = jnp.bfloat16
WIDE = 256


def halves(x):
    hi = x.astype(BF16)
    return hi, (x - hi.astype(F32)).astype(BF16)


def dot3(xh, xl, yh, yl, dims):
    def dot(a, b):
        return lax.dot_general(a, b, (dims, ((), ())), preferred_element_type=F32)

    return dot(xl, yh) + dot(xh, yl) + dot(xh, yh)


def up(n, unit):
    return -(-n // unit) * unit


def planes(src, dst):
    width, rows = src.shape[1], 40 if src.shape[0] % 40 == 0 else src.shape[0]

    def one(g, _):
        at = pl.ds(pl.multiple_of(g * rows, 8), rows)
        for p in range(dst.shape[0]):
            n = min(128, width - p * 128)
            dst[p, at, :n] = src[at, p * 128 : p * 128 + n]
        return 0

    lax.fori_loop(0, src.shape[0] // rows, one, 0)


def every(src, start, count, stride, width):
    parts = [src[p, pl.ds(start, count, stride=stride), :] for p in range(src.shape[0])]
    return jnp.concatenate(parts, axis=1)[:, :width]


def gather_kernel(
    nr, occ,
    t_ref, b_ref, z_ref,
    fp_ref, zg_ref,
    tp, zp, bh, bl, sib_send, sib_recv, own, rs_recv, zs_send, zs_recv, zc,
    sib_s, sib_r, rs_s, rs_r, zs_s, zs_r, za_s, za_r, loc,
):
    r, c = lax.axis_index("row"), lax.axis_index("col")
    t, k = c // 2, lax.rem(c, 2)
    sib = c + 1 - 2 * k
    og = occ // nr
    va = t_ref.shape[0] // occ
    vc = z_ref.shape[0] // occ
    half = b_ref.shape[1] // 2
    blk = lax.rem(t - r + nr, nr)
    is_own = lax.rem(r + r, nr) == t

    barrier = pltpu.get_barrier_semaphore()
    pl.semaphore_signal(barrier, inc=1, device_id=(r, sib), device_id_type=MESH)

    def greet(s, _):
        peer = lax.rem(t + 1 + s, nr)
        pl.semaphore_signal(barrier, inc=1, device_id=(r, 2 * peer + k), device_id_type=MESH)
        return 0

    lax.fori_loop(0, nr - 1, greet, 0)

    def greet_sources(s, _):
        @pl.when(jnp.logical_not(jnp.logical_and(is_own, s == t)))
        def _():
            pl.semaphore_signal(barrier, inc=1, device_id=(blk, 2 * s + k), device_id_type=MESH)

        return 0

    lax.fori_loop(0, nr, greet_sources, 0)

    planes(t_ref, tp)
    planes(z_ref, zp)
    mine, other = pl.ds(pl.multiple_of(k * half, half), half), pl.ds(pl.multiple_of((1 - k) * half, half), half)
    for at, cols in ((0, other), (half, mine)):
        hi, lo = halves(b_ref[:, cols])
        bh[:, at : at + half] = hi
        bl[:, at : at + half] = lo

    first = k == 0
    kept = []
    for jj in range(og):
        z = every(zp, r * og + jj, vc, occ, z_ref.shape[1])
        z0, z1 = z[:, :half], z[:, half:]
        zs_send[jj] = jnp.where(first, z1, z0)
        kept.append(jnp.where(first, z0, z1))
        zc[jj * va : jj * va + vc, :] = kept[-1]

    @pl.when(is_own)
    def _():
        pl.semaphore_wait(barrier, 2 * nr - 1)

    @pl.when(jnp.logical_not(is_own))
    def _():
        pl.semaphore_wait(barrier, 2 * nr)

    z_swap = pltpu.make_async_remote_copy(
        src_ref=zs_send, dst_ref=zs_recv, send_sem=zs_s, recv_sem=zs_r,
        device_id=(r, sib), device_id_type=MESH,
    )
    z_swap.start()
    z_swap.wait()
    for jj in range(og):
        z_mine = zc[jj * va : jj * va + vc, :]
        z_sib = zs_recv[jj]
        zc[jj * va : (jj + 1) * va, :] = jnp.concatenate(
            [jnp.where(first, z_mine, z_sib), jnp.where(first, z_sib, z_mine)], axis=0
        )

    def spread(src, dst, slot, send, recv, s):
        peer = lax.rem(t + 1 + s, nr)
        return pltpu.make_async_remote_copy(
            src_ref=src, dst_ref=dst.at[slot], send_sem=send.at[s], recv_sem=recv.at[slot],
            device_id=(r, 2 * peer + k), device_id_type=MESH,
        )

    def z_start(s, _):
        spread(zc, zg_ref, t, za_s, za_r, s).start()
        return 0

    lax.fori_loop(0, nr - 1, z_start, 0)
    z_own = pltpu.make_async_copy(zc, zg_ref.at[t], loc)
    z_own.start()

    def to_sibling(s):
        return pltpu.make_async_remote_copy(
            src_ref=sib_send.at[s], dst_ref=sib_recv.at[s], send_sem=sib_s.at[s], recv_sem=sib_r.at[s],
            device_id=(r, sib), device_id_type=MESH,
        )

    def to_owner(s):
        dst = lax.rem(r + t + 1 + s, nr)
        return pltpu.make_async_remote_copy(
            src_ref=own.at[s], dst_ref=rs_recv.at[t], send_sem=rs_s.at[s], recv_sem=rs_r.at[t],
            device_id=(dst, 2 * lax.rem(r + dst, nr) + k), device_id_type=MESH,
        )

    own_step = nr - 1 - t

    def finish(s):
        to_sibling(s).wait_recv()
        own[s] = own[s] + sib_recv[s]
        here = jnp.logical_and(s == own_step, is_own)

        @pl.when(here)
        def _():
            rs_recv[t] = own[s]

        @pl.when(jnp.logical_not(here))
        def _():
            to_owner(s).start()

    def step(s, _):
        dst = lax.rem(r + t + 1 + s, nr)
        x = jnp.concatenate(
            [every(tp, dst * og + ii, va, occ, t_ref.shape[1]) for ii in range(og)], axis=0
        )
        xh, xl = halves(x)
        part = dot3(xh, xl, bh[...], bl[...], ((1,), (0,)))
        sib_send[s] = part[:, :half]
        own[s] = part[:, half:]
        to_sibling(s).start()

        @pl.when(s > 0)
        def _():
            finish(s - 1)

        return 0

    lax.fori_loop(0, nr, step, 0)
    finish(nr - 1)

    def arrived(s, _):
        @pl.when(jnp.logical_not(jnp.logical_and(is_own, s == t)))
        def _():
            pltpu.make_async_remote_copy(
                src_ref=own.at[0], dst_ref=rs_recv.at[s], send_sem=rs_s.at[0], recv_sem=rs_r.at[s],
                device_id=(r, sib), device_id_type=MESH,
            ).wait_recv()

        return 0

    lax.fori_loop(0, nr, arrived, 0)

    def add_up(g, _):
        rows = pl.ds(pl.multiple_of(g * 8, 8), 8)
        total = rs_recv[0, rows, :]
        for s in range(1, nr):
            total = total + rs_recv[s, rows, :]
        fp_ref[rows, :] = total
        return 0

    lax.fori_loop(0, fp_ref.shape[0] // 8, add_up, 0)

    def settle(s, _):
        peer = lax.rem(t + 1 + s, nr)
        spread(zc, zg_ref, peer, za_s, za_r, s).wait()
        return 0

    lax.fori_loop(0, nr - 1, settle, 0)

    def sent(s, _):
        to_sibling(s).wait_send()

        @pl.when(jnp.logical_not(jnp.logical_and(s == own_step, is_own)))
        def _():
            to_owner(s).wait_send()

        return 0

    lax.fori_loop(0, nr, sent, 0)
    z_own.wait()


def tile_kernel(
    nr, og, vc, tiles, cuts,
    fp_ref, zg_ref, l_ref, r_ref, rowd_ref, cold_ref,
    out_ref,
    fg, rh, rl, yh, yl, xp, xo, xg, xh, xl, s_send, s_recv, own,
    fs, fr, xs, xr, ss, sr, os_, or_, loc,
):
    r, c = lax.axis_index("row"), lax.axis_index("col")
    t, k = c // 2, lax.rem(c, 2)
    sib = c + 1 - 2 * k
    half = fp_ref.shape[1]
    vir = r_ref.shape[0]
    va = vir // nr
    pad = xo.shape[1] // 2
    wide_pad = xh.shape[1] // nr
    blk = lax.rem(t - r + nr, nr)
    far = r + 1 - 2 * lax.rem(r, 2)
    near = nr // 2 - 1

    barrier = pltpu.get_barrier_semaphore()
    pl.semaphore_signal(barrier, inc=1, device_id=(r, sib), device_id_type=MESH)

    def greet(s, _):
        pl.semaphore_signal(barrier, inc=1, device_id=(lax.rem(r + 1 + s, nr), c), device_id_type=MESH)
        pl.semaphore_signal(
            barrier, inc=1, device_id=(r, 2 * lax.rem(t + 1 + s, nr) + k), device_id_type=MESH
        )
        return 0

    lax.fori_loop(0, nr - 1, greet, 0)

    hi, lo = halves(r_ref[...])
    rh[:vir, :] = hi
    rl[:vir, :] = lo
    hi, lo = halves(l_ref[pl.ds(pl.multiple_of(t * va, 8), va), :])
    rh[vir:, :] = hi
    rl[vir:, :] = lo
    xp[...] = jnp.zeros_like(xp)
    fg[blk] = fp_ref[...]
    pl.semaphore_wait(barrier, 2 * nr - 1)

    def f_copy(m, s):
        at, width = cuts[m]
        cols = pl.ds(at, width)
        return pltpu.make_async_remote_copy(
            src_ref=fp_ref.at[:, cols], dst_ref=fg.at[blk, :, cols],
            send_sem=fs.at[m, s], recv_sem=fr.at[m, blk],
            device_id=(r, 2 * lax.rem(t + 1 + s, nr) + k), device_id_type=MESH,
        )

    def f_wait(m, s):
        at, width = cuts[m]
        cols = pl.ds(at, width)
        peer = lax.rem(t + 1 + s, nr)
        slot = lax.rem(peer - r + nr, nr)
        return pltpu.make_async_remote_copy(
            src_ref=fp_ref.at[:, cols], dst_ref=fg.at[slot, :, cols],
            send_sem=fs.at[m, s], recv_sem=fr.at[m, slot],
            device_id=(r, 2 * peer + k), device_id_type=MESH,
        )

    def each(count, body):
        def one(s, _):
            body(s)
            return 0

        lax.fori_loop(0, count, one, 0)

    for m in range(len(cuts)):
        each(nr - 1, lambda s, m=m: f_copy(m, s).start())

    def x_cut(m):
        return (1, 0, half) if m == len(cuts) else (0,) + cuts[m]

    def x_push(m, src_ref, slot, dst, sem):
        return pltpu.make_async_remote_copy(
            src_ref=src_ref, dst_ref=xg.at[slot, x_cut(m)[0], :, pl.ds(*x_cut(m)[1:])],
            send_sem=xs.at[m, sem], recv_sem=xr.at[m, slot],
            device_id=(dst, c), device_id_type=MESH,
        )

    def x_mine(m):
        q, at, width = x_cut(m)
        return xo.at[q, :, pl.ds(at, width)]

    def x_far(m):
        q, at, width = x_cut(m)
        return xg.at[far, q, :, pl.ds(at, width)]

    def beside(s):
        return lax.rem(r + 2 * (s + 1), nr)

    def x_start(m):
        x_push(m, x_mine(m), r, far, near).start()
        each(near, lambda s: x_push(m, x_mine(m), r, beside(s), s).start())

    def x_arrive(m, slot):
        x_push(m, x_mine(m), slot, far, near).wait_recv()

    def x_forward(m):
        x_arrive(m, far)
        each(near, lambda s: x_push(m, x_far(m), far, beside(s), near + 1 + s).start())

    def rotate(g_ref, q, at, width):
        y_at = (1 - q) * half + at
        for ii in range(og):
            gh, gl = halves(g_ref[:, ii * va : (ii + 1) * va, at : at + width].reshape(vir, width))
            both = dot3(rh[...], rl[...], gh, gl, ((1,), (0,)))
            hi, lo = halves(both[:vir])
            yh[ii * vir : (ii + 1) * vir, y_at : y_at + width] = hi
            yl[ii * vir : (ii + 1) * vir, y_at : y_at + width] = lo
            for par in range(2):
                rows = both[vir + par * vc : vir + (par + 1) * vc]
                for p in range(width // 128):
                    xp[p, pl.ds(par * pad + ii, vc, stride=og), :] = rows[:, p * 128 : (p + 1) * 128]
        for p in range(width // 128):
            xo[q, :, at + p * 128 : at + (p + 1) * 128] = xp[p]

    def take(m, src, load):
        q, at, width = x_cut(m)
        x_at = q * half + at
        rows = pl.ds(pl.multiple_of(src * wide_pad, 16), pad)
        for par in range(2):
            hi, lo = halves(load(q, par * pad, at, width))
            xh[par, rows, x_at : x_at + width] = hi
            xl[par, rows, x_at : x_at + width] = lo

    def take_own(m):
        take(m, r, lambda q, row, at, width: xo[q, row : row + pad, at : at + width])

    def take_from(m, src):
        take(m, src, lambda q, row, at, width: xg[src, q, row : row + pad, at : at + width])

    def take_near(m, base):
        def one(s):
            src = lax.rem(base + 2 * (s + 1), nr)
            x_arrive(m, src)
            take_from(m, src)

        each(near, one)

    zm = len(cuts)
    rotate(zg_ref, 1, 0, half)
    x_start(zm)
    order = [zm] + list(range(zm))
    for m, (at, width) in enumerate(cuts):
        each(nr - 1, lambda s, m=m: f_wait(m, s).wait_recv())
        rotate(fg, 0, at, width)
        x_start(m)
        x_forward(order[m])
    x_forward(order[-1])
    for m in order:
        take_own(m)
        take_from(m, far)
        take_near(m, r)
        take_near(m, far)

    def to_sibling(n, width):
        return pltpu.make_async_remote_copy(
            src_ref=s_send.at[lax.rem(n, 2), :, pl.ds(0, width)], dst_ref=s_recv.at[n, :, pl.ds(0, width)],
            send_sem=ss.at[lax.rem(n, 2)], recv_sem=sr.at[n],
            device_id=(r, sib), device_id_type=MESH,
        )

    def to_row(n, width, s, src):
        dst = lax.rem(r + 1 + s, nr)
        cols = pl.ds(pl.multiple_of(n * WIDE, 128), width)
        return pltpu.make_async_remote_copy(
            src_ref=own.at[pl.ds(pl.multiple_of(dst * wide_pad, 8), pad), cols],
            dst_ref=out_ref.at[src, :, cols],
            send_sem=os_.at[n, s], recv_sem=or_.at[n, src],
            device_id=(dst, c), device_id_type=MESH,
        )

    def stay(n, width):
        cols = pl.ds(pl.multiple_of(n * WIDE, 128), width)
        return pltpu.make_async_copy(
            own.at[pl.ds(pl.multiple_of(r * wide_pad, 8), pad), cols], out_ref.at[r, :, cols], loc.at[n]
        )

    def tile(n, width, slot_used):
        rows = pl.ds(pl.multiple_of(n * WIDE, 128), width)
        wh, wl = yh[rows, :], yl[rows, :]

        def product(par):
            return dot3(xh[par], xl[par], wh, wl, ((1,), (1,)))

        @pl.when(slot_used)
        def _():
            to_sibling(n - 2, WIDE).wait_send()

        s_send[lax.rem(n, 2), :, 0:width] = product(1 - k)
        to_sibling(n, width).start()
        own[:, rows] = product(k)
        to_sibling(n, width).wait_recv()
        reps = width // 128

        def close(g, _):
            at = pl.ds(pl.multiple_of(g * wide_pad, 8), wide_pad)
            rowd = rowd_ref[at, :]
            for m in range(reps):
                cols = pl.ds(pl.multiple_of(n * WIDE + m * 128, 128), 128)
                here = own[at, cols] + s_recv[n, at, m * 128 : (m + 1) * 128]
                own[at, cols] = here / (rowd + cold_ref[0:1, cols])
            return 0

        lax.fori_loop(0, nr, close, 0)

        def send(s, _):
            to_row(n, width, s, r).start()
            return 0

        lax.fori_loop(0, nr - 1, send, 0)
        stay(n, width).start()

    tail = yh.shape[0] - (tiles - 1) * WIDE

    def full(n, _):
        tile(n, WIDE, n > 1)
        return 0

    lax.fori_loop(0, tiles - 1, full, 0)
    tile(jnp.int32(tiles - 1), tail, tiles > 2)

    def settle(n, width):
        def one(s, _):
            src = lax.rem(r + 1 + s, nr)
            to_row(n, width, s, src).wait()
            return 0

        lax.fori_loop(0, nr - 1, one, 0)
        stay(n, width).wait()

    def settle_full(n, _):
        settle(n, WIDE)
        return 0

    lax.fori_loop(0, tiles - 1, settle_full, 0)
    settle(jnp.int32(tiles - 1), tail)
    to_sibling(jnp.int32(tiles - 2), WIDE).wait_send()
    to_sibling(jnp.int32(tiles - 1), tail).wait_send()
    for m in order:
        x_push(m, x_mine(m), r, far, near).wait_send()
        each(near, lambda s, m=m: x_push(m, x_mine(m), r, beside(s), s).wait_send())
        each(near, lambda s, m=m: x_push(m, x_far(m), far, beside(s), near + 1 + s).wait_send())
    for m in range(zm):
        each(nr - 1, lambda s, m=m: f_copy(m, s).wait_send())


def lay_kernel(nr, og, vir, occ, in_ref, out_ref, op):
    count, wide = op.shape[0], in_ref.shape[2]
    for src in range(nr):
        for jj in range(og):
            for p in range(count):
                start = jj * vir + p * 128
                n = min(128, wide - start)
                v = in_ref[src, :, start : start + n]
                if n < 128:
                    v = jnp.concatenate([v, jnp.zeros((8, 128 - n), F32)], axis=1)
                op[p, pl.ds(src * og + jj, 8, stride=occ), :] = v
    for p in range(count):
        n = min(128, vir - p * 128)
        out_ref[:, p * 128 : p * 128 + n] = op[p, :, :n]


def shards(amplitudes, aux_left, aux_right, left_rotation, right_rotation, occ_energy, vir_energy):
    nr, nc = lax.axis_size("row"), lax.axis_size("col")
    occ, vir = occ_energy.shape[0], vir_energy.shape[0]
    naux = aux_left.shape[1]
    half = naux // 2
    og, va, vc = occ // nr, vir // nr, vir // nc
    piece = og * va
    dma = pltpu.SemaphoreType.DMA
    vmem = pl.BlockSpec(memory_space=pltpu.VMEM)
    hbm = pl.BlockSpec(memory_space=pl.ANY)
    limit = 60 * 1024 * 1024

    fp, zg = pl.pallas_call(
        functools.partial(gather_kernel, nr, occ),
        out_shape=[
            jax.ShapeDtypeStruct((piece, half), F32),
            jax.ShapeDtypeStruct((nr, piece, half), F32),
        ],
        in_specs=[vmem] * 3,
        out_specs=[vmem, hbm],
        scratch_shapes=[
            pltpu.VMEM((up(amplitudes.shape[1], 128) // 128, amplitudes.shape[0], 128), F32),
            pltpu.VMEM((up(naux, 128) // 128, aux_right.shape[0], 128), F32),
            pltpu.VMEM((aux_left.shape[0], naux), BF16),
            pltpu.VMEM((aux_left.shape[0], naux), BF16),
            pltpu.VMEM((nr, piece, half), F32),
            pltpu.VMEM((nr, piece, half), F32),
            pltpu.VMEM((nr, piece, half), F32),
            pltpu.VMEM((nr, piece, half), F32),
            pltpu.VMEM((og, vc, half), F32),
            pltpu.VMEM((og, vc, half), F32),
            pltpu.VMEM((piece, half), F32),
            dma((nr,)), dma((nr,)), dma((nr,)), dma((nr,)), dma, dma,
            dma((nr,)), dma((nr,)), dma,
        ],
        compiler_params=pltpu.CompilerParams(collective_id=0, has_side_effects=True, vmem_limit_bytes=limit),
        name="fit_gather",
    )(amplitudes, aux_left, aux_right)

    rows = vc * og
    pad, wide_pad = up(rows, 8), up(rows, 16)
    cols = og * vir
    cols_pad = up(cols, 128)
    tiles = up(cols_pad, WIDE) // WIDE
    cuts = [(at, min(256, half - at)) for at in range(0, half, 256)]
    r, c = lax.axis_index("row"), lax.axis_index("col")
    vir_here = lax.dynamic_slice_in_dim(vir_energy, c * vc, vc)
    occ_here = lax.dynamic_slice_in_dim(occ_energy, r * og, og)
    rowd = (vir_here[None, :, None] - occ_energy.reshape(nr, 1, og)).reshape(nr, rows)
    rowd = jnp.pad(rowd, ((0, 0), (0, wide_pad - rows)), constant_values=1.0).reshape(nr * wide_pad, 1)
    rowd = jnp.broadcast_to(rowd, (nr * wide_pad, 128))
    cold = (vir_energy[None, :] - occ_here[:, None]).reshape(1, cols)
    cold = jnp.pad(cold, ((0, 0), (0, cols_pad - cols)), constant_values=1.0)
    cold = jnp.broadcast_to(cold, (8, cols_pad))

    moved = pl.pallas_call(
        functools.partial(tile_kernel, nr, og, vc, tiles, cuts),
        out_shape=jax.ShapeDtypeStruct((nr, pad, cols_pad), F32),
        in_specs=[vmem] * 6,
        out_specs=hbm,
        scratch_shapes=[
            pltpu.VMEM((nr, piece, half), F32),
            pltpu.VMEM((vir + va, vir), BF16),
            pltpu.VMEM((vir + va, vir), BF16),
            pltpu.VMEM((cols_pad, naux), BF16),
            pltpu.VMEM((cols_pad, naux), BF16),
            pltpu.VMEM((half // 128, 2 * pad, 128), F32),
            pltpu.VMEM((2, 2 * pad, half), F32),
            pltpu.VMEM((nr, 2, 2 * pad, half), F32),
            pltpu.VMEM((2, nr * wide_pad, naux), BF16),
            pltpu.VMEM((2, nr * wide_pad, naux), BF16),
            pltpu.VMEM((2, nr * wide_pad, WIDE), F32),
            pltpu.VMEM((tiles, nr * wide_pad, WIDE), F32),
            pltpu.VMEM((nr * wide_pad, cols_pad), F32),
            dma((len(cuts), nr)), dma((len(cuts), nr)),
            dma((len(cuts) + 1, nr)), dma((len(cuts) + 1, nr)), dma((2,)), dma((tiles,)),
            dma((tiles, nr)), dma((tiles, nr)), dma((tiles,)),
        ],
        compiler_params=pltpu.CompilerParams(collective_id=1, has_side_effects=True, vmem_limit_bytes=limit),
        name="tile_exchange",
    )(fp, zg, left_rotation, right_rotation, rowd, cold)

    out = pl.pallas_call(
        functools.partial(lay_kernel, nr, og, vir, occ),
        grid=(pad // 8,),
        out_shape=jax.ShapeDtypeStruct((rows * occ, vir), F32),
        in_specs=[pl.BlockSpec((nr, 8, cols_pad), lambda g: (0, g, 0))],
        out_specs=pl.BlockSpec((8 * occ, vir), lambda g: (g, 0)),
        scratch_shapes=[pltpu.VMEM((up(vir, 128) // 128, 8 * occ, 128), F32)],
        compiler_params=pltpu.CompilerParams(vmem_limit_bytes=limit),
        name="lay_out",
    )(moved)
    return out.reshape(vc, og, occ, vir)


def solution(mesh):
    placed = (P("row", "col"), P("col", None), P("col", None), P(), P(), P(), P())
    return jax.shard_map(
        shards, mesh=mesh, in_specs=placed, out_specs=P("col", "row", None, None), check_vma=False
    )
```

```python
import functools

import jax
import jax.numpy as jnp
from jax import lax
from jax.experimental import pallas as pl
from jax.experimental.pallas import tpu as pltpu
from jax.sharding import PartitionSpec as P

MESH = pl.DeviceIdType.MESH
F32 = jnp.float32
BF16 = jnp.bfloat16
WIDE = 256


def halves(x):
    hi = x.astype(BF16)
    return hi, (x - hi.astype(F32)).astype(BF16)


def dot3(xh, xl, yh, yl, dims):
    def dot(a, b):
        return lax.dot_general(a, b, (dims, ((), ())), preferred_element_type=F32)

    return dot(xl, yh) + dot(xh, yl) + dot(xh, yh)


def up(n, unit):
    return -(-n // unit) * unit


def planes(src, dst):
    width, rows = src.shape[1], 40 if src.shape[0] % 40 == 0 else src.shape[0]

    def one(g, _):
        at = pl.ds(pl.multiple_of(g * rows, 8), rows)
        for p in range(dst.shape[0]):
            n = min(128, width - p * 128)
            dst[p, at, :n] = src[at, p * 128 : p * 128 + n]
        return 0

    lax.fori_loop(0, src.shape[0] // rows, one, 0)


def every(src, start, count, stride, width):
    parts = [src[p, pl.ds(start, count, stride=stride), :] for p in range(src.shape[0])]
    return jnp.concatenate(parts, axis=1)[:, :width]


def gather_kernel(
    nr, occ,
    t_ref, b_ref, z_ref,
    fp_ref, zg_ref,
    tp, zp, bh, bl, sib_send, sib_recv, own, z_recv, rs_recv, zs_send, zs_recv, zc,
    sib_s, sib_r, zz_s, zz_r, rs_s, rs_r, zs_s, zs_r, za_s, za_r, loc,
):
    r, c = lax.axis_index("row"), lax.axis_index("col")
    t, k = c // 2, lax.rem(c, 2)
    sib = c + 1 - 2 * k
    og = occ // nr
    va = t_ref.shape[0] // occ
    vc = z_ref.shape[0] // occ
    half = b_ref.shape[1] // 2
    blk = lax.rem(t - r + nr, nr)
    is_own = lax.rem(r + r, nr) == t
    ny = nr // 2
    y, low = t // 2, lax.rem(t, 2)
    pair = t + 1 - 2 * low

    barrier = pltpu.get_barrier_semaphore()
    pl.semaphore_signal(barrier, inc=1, device_id=(r, sib), device_id_type=MESH)

    pl.semaphore_signal(barrier, inc=1, device_id=(r, 2 * pair + k), device_id_type=MESH)

    def along(s):
        return 2 * lax.rem(y + 1 + s, ny) + low

    def each(count, body):
        def one(s, _):
            body(s)
            return 0

        lax.fori_loop(0, count, one, 0)

    each(
        ny - 1,
        lambda s: pl.semaphore_signal(
            barrier, inc=1, device_id=(r, 2 * along(s) + k), device_id_type=MESH
        ),
    )

    def greet_source(s):
        @pl.when(jnp.logical_not(jnp.logical_and(is_own, s == y)))
        def _():
            pl.semaphore_signal(
                barrier, inc=1, device_id=(blk, 2 * (2 * s + low) + k), device_id_type=MESH
            )

    each(ny, greet_source)

    planes(t_ref, tp)
    planes(z_ref, zp)
    mine, other = pl.ds(pl.multiple_of(k * half, half), half), pl.ds(pl.multiple_of((1 - k) * half, half), half)
    for at, cols in ((0, other), (half, mine)):
        hi, lo = halves(b_ref[:, cols])
        bh[:, at : at + half] = hi
        bl[:, at : at + half] = lo

    first = k == 0
    kept = []
    for jj in range(og):
        z = every(zp, r * og + jj, vc, occ, z_ref.shape[1])
        z0, z1 = z[:, :half], z[:, half:]
        zs_send[jj] = jnp.where(first, z1, z0)
        kept.append(jnp.where(first, z0, z1))
        zc[jj * va : jj * va + vc, :] = kept[-1]

    @pl.when(is_own)
    def _():
        pl.semaphore_wait(barrier, nr)

    @pl.when(jnp.logical_not(is_own))
    def _():
        pl.semaphore_wait(barrier, nr + 1)

    z_swap = pltpu.make_async_remote_copy(
        src_ref=zs_send, dst_ref=zs_recv, send_sem=zs_s, recv_sem=zs_r,
        device_id=(r, sib), device_id_type=MESH,
    )
    z_swap.start()
    z_swap.wait()
    for jj in range(og):
        z_mine = zc[jj * va : jj * va + vc, :]
        z_sib = zs_recv[jj]
        zc[jj * va : (jj + 1) * va, :] = jnp.concatenate(
            [jnp.where(first, z_mine, z_sib), jnp.where(first, z_sib, z_mine)], axis=0
        )

    def z_push(src_ref, slot, peer, sem):
        return pltpu.make_async_remote_copy(
            src_ref=src_ref, dst_ref=zg_ref.at[slot], send_sem=za_s.at[sem], recv_sem=za_r.at[slot],
            device_id=(r, 2 * peer + k), device_id_type=MESH,
        )

    z_push(zc, t, pair, ny - 1).start()
    each(ny - 1, lambda s: z_push(zc, t, along(s), s).start())
    z_own = pltpu.make_async_copy(zc, zg_ref.at[t], loc)
    z_own.start()

    def to_sibling(s):
        return pltpu.make_async_remote_copy(
            src_ref=sib_send.at[s], dst_ref=sib_recv.at[s], send_sem=sib_s.at[s], recv_sem=sib_r.at[s],
            device_id=(r, sib), device_id_type=MESH,
        )

    def owner(s):
        stays = s // ny
        side = stays * low + (1 - stays) * (1 - low)
        return 2 * lax.rem(y + 1 + lax.rem(s, ny), ny) + side

    def to_pair(s):
        return pltpu.make_async_remote_copy(
            src_ref=own.at[s], dst_ref=z_recv.at[s], send_sem=zz_s.at[s], recv_sem=zz_r.at[s],
            device_id=(r, 2 * pair + k), device_id_type=MESH,
        )

    def to_owner(s):
        ot = owner(ny + s)
        return pltpu.make_async_remote_copy(
            src_ref=own.at[ny + s], dst_ref=rs_recv.at[y], send_sem=rs_s.at[s], recv_sem=rs_r.at[y],
            device_id=(lax.rem(ot - r + nr, nr), 2 * ot + k), device_id_type=MESH,
        )

    def finish(s):
        to_sibling(s).wait_recv()
        own[s] = own[s] + sib_recv[s]

        @pl.when(s < ny)
        def _():
            to_pair(s).start()

    def step(s):
        dst = lax.rem(owner(s) - r + nr, nr)
        x = jnp.concatenate(
            [every(tp, dst * og + ii, va, occ, t_ref.shape[1]) for ii in range(og)], axis=0
        )
        xh, xl = halves(x)
        part = dot3(xh, xl, bh[...], bl[...], ((1,), (0,)))
        sib_send[s] = part[:, :half]
        own[s] = part[:, half:]
        to_sibling(s).start()

        @pl.when(s > 0)
        def _():
            finish(s - 1)

    each(nr, step)
    finish(nr - 1)

    z_push(zc, pair, pair, ny - 1).wait_recv()
    each(ny - 1, lambda s: z_push(zg_ref.at[pair], pair, along(s), ny + s).start())

    def deliver(s):
        to_pair(s).wait_recv()
        own[ny + s] = own[ny + s] + z_recv[s]
        here = jnp.logical_and(s == ny - 1, is_own)

        @pl.when(here)
        def _():
            rs_recv[y] = own[ny + s]

        @pl.when(jnp.logical_not(here))
        def _():
            to_owner(s).start()

    each(ny, deliver)

    def arrived(s):
        @pl.when(jnp.logical_not(jnp.logical_and(is_own, s == y)))
        def _():
            pltpu.make_async_remote_copy(
                src_ref=own.at[0], dst_ref=rs_recv.at[s], send_sem=rs_s.at[0], recv_sem=rs_r.at[s],
                device_id=(r, sib), device_id_type=MESH,
            ).wait_recv()

    each(ny, arrived)

    def add_up(g, _):
        rows = pl.ds(pl.multiple_of(g * 8, 8), 8)
        total = rs_recv[0, rows, :]
        for s in range(1, ny):
            total = total + rs_recv[s, rows, :]
        fp_ref[rows, :] = total
        return 0

    lax.fori_loop(0, fp_ref.shape[0] // 8, add_up, 0)

    z_push(zc, t, pair, ny - 1).wait_send()

    def settle(s):
        z_push(zc, t, along(s), s).wait_send()
        z_push(zc, along(s), along(s), s).wait_recv()
        z_push(zg_ref.at[pair], pair, along(s), ny + s).wait_send()
        z_push(zc, along(s) + pair - t, pair, s).wait_recv()

    each(ny - 1, settle)
    each(nr, lambda s: to_sibling(s).wait_send())

    def sent(s):
        to_pair(s).wait_send()

        @pl.when(jnp.logical_not(jnp.logical_and(s == ny - 1, is_own)))
        def _():
            to_owner(s).wait_send()

    each(ny, sent)
    z_own.wait()


def tile_kernel(
    nr, og, vc, tiles, cuts,
    fp_ref, zg_ref, l_ref, r_ref, rowd_ref, cold_ref,
    out_ref,
    fg, rh, rl, yh, yl, xp, xo, xg, xh, xl, s_send, s_recv, own,
    fs, fr, xs, xr, ss, sr, os_, or_, loc,
):
    r, c = lax.axis_index("row"), lax.axis_index("col")
    t, k = c // 2, lax.rem(c, 2)
    sib = c + 1 - 2 * k
    half = fp_ref.shape[1]
    vir = r_ref.shape[0]
    va = vir // nr
    pad = xo.shape[1] // 2
    wide_pad = xh.shape[1] // nr
    blk = lax.rem(t - r + nr, nr)
    far = r + 1 - 2 * lax.rem(r, 2)
    near = nr // 2 - 1

    barrier = pltpu.get_barrier_semaphore()
    pl.semaphore_signal(barrier, inc=1, device_id=(r, sib), device_id_type=MESH)

    def greet(s, _):
        pl.semaphore_signal(barrier, inc=1, device_id=(lax.rem(r + 1 + s, nr), c), device_id_type=MESH)
        pl.semaphore_signal(
            barrier, inc=1, device_id=(r, 2 * lax.rem(t + 1 + s, nr) + k), device_id_type=MESH
        )
        return 0

    lax.fori_loop(0, nr - 1, greet, 0)

    hi, lo = halves(r_ref[...])
    rh[:vir, :] = hi
    rl[:vir, :] = lo
    hi, lo = halves(l_ref[pl.ds(pl.multiple_of(t * va, 8), va), :])
    rh[vir:, :] = hi
    rl[vir:, :] = lo
    xp[...] = jnp.zeros_like(xp)
    fg[blk] = fp_ref[...]
    pl.semaphore_wait(barrier, 2 * nr - 1)

    ny = nr // 2
    y, low = t // 2, lax.rem(t, 2)
    pair = t + 1 - 2 * low

    def along(s):
        return 2 * lax.rem(y + 1 + s, ny) + low

    def slot_of(other):
        return lax.rem(other - r + nr, nr)

    def f_push(m, src_ref, slot, peer, sem):
        at, width = cuts[m]
        cols = pl.ds(at, width)
        return pltpu.make_async_remote_copy(
            src_ref=src_ref.at[:, cols], dst_ref=fg.at[slot, :, cols],
            send_sem=fs.at[m, sem], recv_sem=fr.at[m, slot],
            device_id=(r, 2 * peer + k), device_id_type=MESH,
        )

    def each(count, body):
        def one(s, _):
            body(s)
            return 0

        lax.fori_loop(0, count, one, 0)

    def f_start(m):
        f_push(m, fp_ref, blk, pair, ny - 1).start()
        each(ny - 1, lambda s: f_push(m, fp_ref, blk, along(s), s).start())

    def f_forward(m):
        f_push(m, fp_ref, slot_of(pair), pair, ny - 1).wait_recv()
        each(
            ny - 1,
            lambda s: f_push(m, fg.at[slot_of(pair)], slot_of(pair), along(s), ny + s).start(),
        )

    def f_rest(m):
        def one(s):
            f_push(m, fp_ref, slot_of(along(s)), pair, ny - 1).wait_recv()
            f_push(m, fp_ref, slot_of(along(s) + pair - t), pair, ny - 1).wait_recv()

        each(ny - 1, one)

    for m in range(len(cuts)):
        f_start(m)

    def x_cut(m):
        return (1, 0, half) if m == len(cuts) else (0,) + cuts[m]

    def x_push(m, src_ref, slot, dst, sem):
        return pltpu.make_async_remote_copy(
            src_ref=src_ref, dst_ref=xg.at[slot, x_cut(m)[0], :, pl.ds(*x_cut(m)[1:])],
            send_sem=xs.at[m, sem], recv_sem=xr.at[m, slot],
            device_id=(dst, c), device_id_type=MESH,
        )

    def x_mine(m):
        q, at, width = x_cut(m)
        return xo.at[q, :, pl.ds(at, width)]

    def x_far(m):
        q, at, width = x_cut(m)
        return xg.at[far, q, :, pl.ds(at, width)]

    def beside(s):
        return lax.rem(r + 2 * (s + 1), nr)

    def x_start(m):
        x_push(m, x_mine(m), r, far, near).start()
        each(near, lambda s: x_push(m, x_mine(m), r, beside(s), s).start())

    def x_arrive(m, slot):
        x_push(m, x_mine(m), slot, far, near).wait_recv()

    def x_forward(m):
        x_arrive(m, far)
        each(near, lambda s: x_push(m, x_far(m), far, beside(s), near + 1 + s).start())

    def rotate(g_ref, q, at, width):
        y_at = (1 - q) * half + at
        for ii in range(og):
            gh, gl = halves(g_ref[:, ii * va : (ii + 1) * va, at : at + width].reshape(vir, width))
            both = dot3(rh[...], rl[...], gh, gl, ((1,), (0,)))
            hi, lo = halves(both[:vir])
            yh[ii * vir : (ii + 1) * vir, y_at : y_at + width] = hi
            yl[ii * vir : (ii + 1) * vir, y_at : y_at + width] = lo
            for par in range(2):
                rows = both[vir + par * vc : vir + (par + 1) * vc]
                for p in range(width // 128):
                    xp[p, pl.ds(par * pad + ii, vc, stride=og), :] = rows[:, p * 128 : (p + 1) * 128]
        for p in range(width // 128):
            xo[q, :, at + p * 128 : at + (p + 1) * 128] = xp[p]

    def take(m, src, load):
        q, at, width = x_cut(m)
        x_at = q * half + at
        rows = pl.ds(pl.multiple_of(src * wide_pad, 16), pad)
        for par in range(2):
            hi, lo = halves(load(q, par * pad, at, width))
            xh[par, rows, x_at : x_at + width] = hi
            xl[par, rows, x_at : x_at + width] = lo

    def take_own(m):
        take(m, r, lambda q, row, at, width: xo[q, row : row + pad, at : at + width])

    def take_from(m, src):
        take(m, src, lambda q, row, at, width: xg[src, q, row : row + pad, at : at + width])

    def take_near(m, base):
        def one(s):
            src = lax.rem(base + 2 * (s + 1), nr)
            x_arrive(m, src)
            take_from(m, src)

        each(near, one)

    zm = len(cuts)
    rotate(zg_ref, 1, 0, half)
    x_start(zm)
    for m in range(zm):
        f_forward(m)
    order = [zm] + list(range(zm))
    for m, (at, width) in enumerate(cuts):
        f_rest(m)
        rotate(fg, 0, at, width)
        x_start(m)
        x_forward(order[m])
    x_forward(order[-1])
    for m in order:
        take_own(m)
        take_from(m, far)
        take_near(m, r)
        take_near(m, far)

    def to_sibling(n, width):
        return pltpu.make_async_remote_copy(
            src_ref=s_send.at[lax.rem(n, 2), :, pl.ds(0, width)], dst_ref=s_recv.at[n, :, pl.ds(0, width)],
            send_sem=ss.at[lax.rem(n, 2)], recv_sem=sr.at[n],
            device_id=(r, sib), device_id_type=MESH,
        )

    def to_row(n, width, s, src):
        dst = lax.rem(r + 1 + s, nr)
        cols = pl.ds(pl.multiple_of(n * WIDE, 128), width)
        return pltpu.make_async_remote_copy(
            src_ref=own.at[pl.ds(pl.multiple_of(dst * wide_pad, 8), pad), cols],
            dst_ref=out_ref.at[src, :, cols],
            send_sem=os_.at[n, s], recv_sem=or_.at[n, src],
            device_id=(dst, c), device_id_type=MESH,
        )

    def stay(n, width):
        cols = pl.ds(pl.multiple_of(n * WIDE, 128), width)
        return pltpu.make_async_copy(
            own.at[pl.ds(pl.multiple_of(r * wide_pad, 8), pad), cols], out_ref.at[r, :, cols], loc.at[n]
        )

    def tile(n, width, slot_used):
        rows = pl.ds(pl.multiple_of(n * WIDE, 128), width)
        wh, wl = yh[rows, :], yl[rows, :]

        def product(par):
            return dot3(xh[par], xl[par], wh, wl, ((1,), (1,)))

        @pl.when(slot_used)
        def _():
            to_sibling(n - 2, WIDE).wait_send()

        s_send[lax.rem(n, 2), :, 0:width] = product(1 - k)
        to_sibling(n, width).start()
        own[:, rows] = product(k)
        to_sibling(n, width).wait_recv()
        reps = width // 128

        def close(g, _):
            at = pl.ds(pl.multiple_of(g * wide_pad, 8), wide_pad)
            rowd = rowd_ref[at, :]
            for m in range(reps):
                cols = pl.ds(pl.multiple_of(n * WIDE + m * 128, 128), 128)
                here = own[at, cols] + s_recv[n, at, m * 128 : (m + 1) * 128]
                own[at, cols] = here / (rowd + cold_ref[0:1, cols])
            return 0

        lax.fori_loop(0, nr, close, 0)

        def send(s, _):
            to_row(n, width, s, r).start()
            return 0

        lax.fori_loop(0, nr - 1, send, 0)
        stay(n, width).start()

    tail = yh.shape[0] - (tiles - 1) * WIDE

    def full(n, _):
        tile(n, WIDE, n > 1)
        return 0

    lax.fori_loop(0, tiles - 1, full, 0)
    tile(jnp.int32(tiles - 1), tail, tiles > 2)

    def settle(n, width):
        def one(s, _):
            src = lax.rem(r + 1 + s, nr)
            to_row(n, width, s, src).wait()
            return 0

        lax.fori_loop(0, nr - 1, one, 0)
        stay(n, width).wait()

    def settle_full(n, _):
        settle(n, WIDE)
        return 0

    lax.fori_loop(0, tiles - 1, settle_full, 0)
    settle(jnp.int32(tiles - 1), tail)
    to_sibling(jnp.int32(tiles - 2), WIDE).wait_send()
    to_sibling(jnp.int32(tiles - 1), tail).wait_send()
    for m in order:
        x_push(m, x_mine(m), r, far, near).wait_send()
        each(near, lambda s, m=m: x_push(m, x_mine(m), r, beside(s), s).wait_send())
        each(near, lambda s, m=m: x_push(m, x_far(m), far, beside(s), near + 1 + s).wait_send())
    for m in range(zm):
        f_push(m, fp_ref, blk, pair, ny - 1).wait_send()
        each(ny - 1, lambda s, m=m: f_push(m, fp_ref, blk, along(s), s).wait_send())
        each(ny - 1, lambda s, m=m: f_push(m, fp_ref, blk, along(s), ny + s).wait_send())


def lay_kernel(nr, og, vir, occ, in_ref, out_ref, op):
    count, wide = op.shape[0], in_ref.shape[2]
    for src in range(nr):
        for jj in range(og):
            for p in range(count):
                start = jj * vir + p * 128
                n = min(128, wide - start)
                v = in_ref[src, :, start : start + n]
                if n < 128:
                    v = jnp.concatenate([v, jnp.zeros((8, 128 - n), F32)], axis=1)
                op[p, pl.ds(src * og + jj, 8, stride=occ), :] = v
    for p in range(count):
        n = min(128, vir - p * 128)
        out_ref[:, p * 128 : p * 128 + n] = op[p, :, :n]


def shards(amplitudes, aux_left, aux_right, left_rotation, right_rotation, occ_energy, vir_energy):
    nr, nc = lax.axis_size("row"), lax.axis_size("col")
    occ, vir = occ_energy.shape[0], vir_energy.shape[0]
    naux = aux_left.shape[1]
    half = naux // 2
    og, va, vc = occ // nr, vir // nr, vir // nc
    piece = og * va
    dma = pltpu.SemaphoreType.DMA
    vmem = pl.BlockSpec(memory_space=pltpu.VMEM)
    hbm = pl.BlockSpec(memory_space=pl.ANY)
    limit = 60 * 1024 * 1024

    fp, zg = pl.pallas_call(
        functools.partial(gather_kernel, nr, occ),
        out_shape=[
            jax.ShapeDtypeStruct((piece, half), F32),
            jax.ShapeDtypeStruct((nr, piece, half), F32),
        ],
        in_specs=[vmem] * 3,
        out_specs=[vmem, hbm],
        scratch_shapes=[
            pltpu.VMEM((up(amplitudes.shape[1], 128) // 128, amplitudes.shape[0], 128), F32),
            pltpu.VMEM((up(naux, 128) // 128, aux_right.shape[0], 128), F32),
            pltpu.VMEM((aux_left.shape[0], naux), BF16),
            pltpu.VMEM((aux_left.shape[0], naux), BF16),
            pltpu.VMEM((nr, piece, half), F32),
            pltpu.VMEM((nr, piece, half), F32),
            pltpu.VMEM((nr, piece, half), F32),
            pltpu.VMEM((nr // 2, piece, half), F32),
            pltpu.VMEM((nr // 2, piece, half), F32),
            pltpu.VMEM((og, vc, half), F32),
            pltpu.VMEM((og, vc, half), F32),
            pltpu.VMEM((piece, half), F32),
            dma((nr,)), dma((nr,)), dma((nr,)), dma((nr,)), dma((nr,)), dma((nr,)), dma, dma,
            dma((nr,)), dma((nr,)), dma,
        ],
        compiler_params=pltpu.CompilerParams(collective_id=0, has_side_effects=True, vmem_limit_bytes=limit),
        name="fit_gather",
    )(amplitudes, aux_left, aux_right)

    rows = vc * og
    pad, wide_pad = up(rows, 8), up(rows, 16)
    cols = og * vir
    cols_pad = up(cols, 128)
    tiles = up(cols_pad, WIDE) // WIDE
    cuts = [(at, min(256, half - at)) for at in range(0, half, 256)]
    r, c = lax.axis_index("row"), lax.axis_index("col")
    vir_here = lax.dynamic_slice_in_dim(vir_energy, c * vc, vc)
    occ_here = lax.dynamic_slice_in_dim(occ_energy, r * og, og)
    rowd = (vir_here[None, :, None] - occ_energy.reshape(nr, 1, og)).reshape(nr, rows)
    rowd = jnp.pad(rowd, ((0, 0), (0, wide_pad - rows)), constant_values=1.0).reshape(nr * wide_pad, 1)
    rowd = jnp.broadcast_to(rowd, (nr * wide_pad, 128))
    cold = (vir_energy[None, :] - occ_here[:, None]).reshape(1, cols)
    cold = jnp.pad(cold, ((0, 0), (0, cols_pad - cols)), constant_values=1.0)
    cold = jnp.broadcast_to(cold, (8, cols_pad))

    moved = pl.pallas_call(
        functools.partial(tile_kernel, nr, og, vc, tiles, cuts),
        out_shape=jax.ShapeDtypeStruct((nr, pad, cols_pad), F32),
        in_specs=[vmem] * 6,
        out_specs=hbm,
        scratch_shapes=[
            pltpu.VMEM((nr, piece, half), F32),
            pltpu.VMEM((vir + va, vir), BF16),
            pltpu.VMEM((vir + va, vir), BF16),
            pltpu.VMEM((cols_pad, naux), BF16),
            pltpu.VMEM((cols_pad, naux), BF16),
            pltpu.VMEM((half // 128, 2 * pad, 128), F32),
            pltpu.VMEM((2, 2 * pad, half), F32),
            pltpu.VMEM((nr, 2, 2 * pad, half), F32),
            pltpu.VMEM((2, nr * wide_pad, naux), BF16),
            pltpu.VMEM((2, nr * wide_pad, naux), BF16),
            pltpu.VMEM((2, nr * wide_pad, WIDE), F32),
            pltpu.VMEM((tiles, nr * wide_pad, WIDE), F32),
            pltpu.VMEM((nr * wide_pad, cols_pad), F32),
            dma((len(cuts), nr)), dma((len(cuts), nr)),
            dma((len(cuts) + 1, nr)), dma((len(cuts) + 1, nr)), dma((2,)), dma((tiles,)),
            dma((tiles, nr)), dma((tiles, nr)), dma((tiles,)),
        ],
        compiler_params=pltpu.CompilerParams(collective_id=1, has_side_effects=True, vmem_limit_bytes=limit),
        name="tile_exchange",
    )(fp, zg, left_rotation, right_rotation, rowd, cold)

    out = pl.pallas_call(
        functools.partial(lay_kernel, nr, og, vir, occ),
        grid=(pad // 8,),
        out_shape=jax.ShapeDtypeStruct((rows * occ, vir), F32),
        in_specs=[pl.BlockSpec((nr, 8, cols_pad), lambda g: (0, g, 0))],
        out_specs=pl.BlockSpec((8 * occ, vir), lambda g: (g, 0)),
        scratch_shapes=[pltpu.VMEM((up(vir, 128) // 128, 8 * occ, 128), F32)],
        compiler_params=pltpu.CompilerParams(vmem_limit_bytes=limit),
        name="lay_out",
    )(moved)
    return out.reshape(vc, og, occ, vir)


def solution(mesh):
    placed = (P("row", "col"), P("col", None), P("col", None), P(), P(), P(), P())
    return jax.shard_map(
        shards, mesh=mesh, in_specs=placed, out_specs=P("col", "row", None, None), check_vma=False
    )
```

```python
import functools

import jax
import jax.numpy as jnp
from jax import lax
from jax.experimental import pallas as pl
from jax.experimental.pallas import tpu as pltpu
from jax.sharding import PartitionSpec as P

MESH = pl.DeviceIdType.MESH
F32 = jnp.float32
BF16 = jnp.bfloat16
WIDE = 256


def halves(x):
    hi = x.astype(BF16)
    return hi, (x - hi.astype(F32)).astype(BF16)


def dot3(xh, xl, yh, yl, dims):
    def dot(a, b):
        return lax.dot_general(a, b, (dims, ((), ())), preferred_element_type=F32)

    return dot(xl, yh) + dot(xh, yl) + dot(xh, yh)


def up(n, unit):
    return -(-n // unit) * unit


def planes(src, dst):
    width, rows = src.shape[1], 40 if src.shape[0] % 40 == 0 else src.shape[0]

    def one(g, _):
        at = pl.ds(pl.multiple_of(g * rows, 8), rows)
        for p in range(dst.shape[0]):
            n = min(128, width - p * 128)
            dst[p, at, :n] = src[at, p * 128 : p * 128 + n]
        return 0

    lax.fori_loop(0, src.shape[0] // rows, one, 0)


def every(src, start, count, stride, width):
    parts = [src[p, pl.ds(start, count, stride=stride), :] for p in range(src.shape[0])]
    return jnp.concatenate(parts, axis=1)[:, :width]


def gather_kernel(
    nr, occ,
    t_ref, b_ref, z_ref, l_ref,
    fp_ref, zg_ref, xz_ref,
    tp, zp, bh, bl, sib_send, sib_recv, own, z_recv, rs_recv, zs_send, zs_recv, zc, xp, xo,
    sib_s, sib_r, zz_s, zz_r, rs_s, rs_r, zs_s, zs_r, za_s, za_r, xs, xr, loc,
):
    r, c = lax.axis_index("row"), lax.axis_index("col")
    t, k = c // 2, lax.rem(c, 2)
    sib = c + 1 - 2 * k
    og = occ // nr
    va = t_ref.shape[0] // occ
    vc = z_ref.shape[0] // occ
    half = b_ref.shape[1] // 2
    blk = lax.rem(t - r + nr, nr)
    is_own = lax.rem(r + r, nr) == t
    ny = nr // 2
    y, low = t // 2, lax.rem(t, 2)
    pair = t + 1 - 2 * low

    far = r + 1 - 2 * lax.rem(r, 2)
    vir = va * nr
    pad = xo.shape[0] // 2

    barrier = pltpu.get_barrier_semaphore()
    pl.semaphore_signal(barrier, inc=1, device_id=(r, sib), device_id_type=MESH)

    pl.semaphore_signal(barrier, inc=1, device_id=(r, 2 * pair + k), device_id_type=MESH)

    def along(s):
        return 2 * lax.rem(y + 1 + s, ny) + low

    def each(count, body):
        def one(s, _):
            body(s)
            return 0

        lax.fori_loop(0, count, one, 0)

    def beside(s):
        return lax.rem(r + 2 * (s + 1), nr)

    pl.semaphore_signal(barrier, inc=1, device_id=(far, c), device_id_type=MESH)

    def greet(s):
        pl.semaphore_signal(barrier, inc=1, device_id=(r, 2 * along(s) + k), device_id_type=MESH)
        pl.semaphore_signal(barrier, inc=1, device_id=(beside(s), c), device_id_type=MESH)

    each(ny - 1, greet)

    def greet_source(s):
        @pl.when(jnp.logical_not(jnp.logical_and(is_own, s == y)))
        def _():
            pl.semaphore_signal(
                barrier, inc=1, device_id=(blk, 2 * (2 * s + low) + k), device_id_type=MESH
            )

    each(ny, greet_source)

    planes(t_ref, tp)
    planes(z_ref, zp)
    mine, other = pl.ds(pl.multiple_of(k * half, half), half), pl.ds(pl.multiple_of((1 - k) * half, half), half)
    for at, cols in ((0, other), (half, mine)):
        hi, lo = halves(b_ref[:, cols])
        bh[:, at : at + half] = hi
        bl[:, at : at + half] = lo

    first = k == 0
    kept = []
    for jj in range(og):
        z = every(zp, r * og + jj, vc, occ, z_ref.shape[1])
        z0, z1 = z[:, :half], z[:, half:]
        zs_send[jj] = jnp.where(first, z1, z0)
        kept.append(jnp.where(first, z0, z1))
        zc[jj * va : jj * va + vc, :] = kept[-1]

    @pl.when(is_own)
    def _():
        pl.semaphore_wait(barrier, nr + ny)

    @pl.when(jnp.logical_not(is_own))
    def _():
        pl.semaphore_wait(barrier, nr + ny + 1)

    z_swap = pltpu.make_async_remote_copy(
        src_ref=zs_send, dst_ref=zs_recv, send_sem=zs_s, recv_sem=zs_r,
        device_id=(r, sib), device_id_type=MESH,
    )
    z_swap.start()
    z_swap.wait()
    for jj in range(og):
        z_mine = zc[jj * va : jj * va + vc, :]
        z_sib = zs_recv[jj]
        zc[jj * va : (jj + 1) * va, :] = jnp.concatenate(
            [jnp.where(first, z_mine, z_sib), jnp.where(first, z_sib, z_mine)], axis=0
        )

    def z_push(src_ref, slot, peer, sem):
        return pltpu.make_async_remote_copy(
            src_ref=src_ref, dst_ref=zg_ref.at[slot], send_sem=za_s.at[sem], recv_sem=za_r.at[slot],
            device_id=(r, 2 * peer + k), device_id_type=MESH,
        )

    z_push(zc, t, pair, ny - 1).start()
    each(ny - 1, lambda s: z_push(zc, t, along(s), s).start())
    zg_ref[t] = zc[...]

    def to_sibling(s):
        return pltpu.make_async_remote_copy(
            src_ref=sib_send.at[s], dst_ref=sib_recv.at[s], send_sem=sib_s.at[s], recv_sem=sib_r.at[s],
            device_id=(r, sib), device_id_type=MESH,
        )

    def owner(s):
        stays = s // ny
        side = stays * low + (1 - stays) * (1 - low)
        return 2 * lax.rem(y + 1 + lax.rem(s, ny), ny) + side

    def to_pair(s):
        return pltpu.make_async_remote_copy(
            src_ref=own.at[s], dst_ref=z_recv.at[s], send_sem=zz_s.at[s], recv_sem=zz_r.at[s],
            device_id=(r, 2 * pair + k), device_id_type=MESH,
        )

    def to_owner(s):
        ot = owner(ny + s)
        return pltpu.make_async_remote_copy(
            src_ref=own.at[ny + s], dst_ref=rs_recv.at[y], send_sem=rs_s.at[s], recv_sem=rs_r.at[y],
            device_id=(lax.rem(ot - r + nr, nr), 2 * ot + k), device_id_type=MESH,
        )

    def finish(s):
        to_sibling(s).wait_recv()
        own[s] = own[s] + sib_recv[s]

        @pl.when(s < ny)
        def _():
            to_pair(s).start()

    def step(s):
        dst = lax.rem(owner(s) - r + nr, nr)
        x = jnp.concatenate(
            [every(tp, dst * og + ii, va, occ, t_ref.shape[1]) for ii in range(og)], axis=0
        )
        xh, xl = halves(x)
        part = dot3(xh, xl, bh[...], bl[...], ((1,), (0,)))
        sib_send[s] = part[:, :half]
        own[s] = part[:, half:]
        to_sibling(s).start()

        @pl.when(s > 0)
        def _():
            finish(s - 1)

        @pl.when(s == ny)
        def _():
            z_push(zc, pair, pair, ny - 1).wait_recv()
            each(ny - 1, lambda j: z_push(zg_ref.at[pair], pair, along(j), ny + j).start())

    each(nr, step)
    finish(nr - 1)

    def deliver(s):
        to_pair(s).wait_recv()
        own[ny + s] = own[ny + s] + z_recv[s]
        here = jnp.logical_and(s == ny - 1, is_own)

        @pl.when(here)
        def _():
            rs_recv[y] = own[ny + s]

        @pl.when(jnp.logical_not(here))
        def _():
            to_owner(s).start()

    def x_push(src_ref, slot, dst, sem):
        return pltpu.make_async_remote_copy(
            src_ref=src_ref, dst_ref=xz_ref.at[slot], send_sem=xs.at[sem], recv_sem=xr.at[slot],
            device_id=(dst, c), device_id_type=MESH,
        )

    def deliver_early(s):
        deliver(s)

    early = ny // 2
    each(early, deliver_early)

    def z_rest(s):
        z_push(zc, along(s), along(s), s).wait_recv()
        z_push(zc, along(s) + pair - t, pair, s).wait_recv()

    each(ny - 1, z_rest)
    lh, ll = halves(l_ref[pl.ds(pl.multiple_of(t * va, 8), va), :])
    xp[...] = jnp.zeros_like(xp)
    for ii in range(og):
        gh, gl = halves(zg_ref[:, ii * va : (ii + 1) * va, :].reshape(vir, half))
        x = dot3(lh, ll, gh, gl, ((1,), (0,)))
        for par in range(2):
            for p in range(half // 128):
                xp[p, pl.ds(par * pad + ii, vc, stride=og), :] = x[
                    par * vc : (par + 1) * vc, p * 128 : (p + 1) * 128
                ]
    for p in range(half // 128):
        xo[:, p * 128 : (p + 1) * 128] = xp[p]
    x_push(xo, r, far, ny - 1).start()
    each(ny - 1, lambda s: x_push(xo, r, beside(s), s).start())
    x_own = pltpu.make_async_copy(xo, xz_ref.at[r], loc)
    x_own.start()

    each(ny - early, lambda s: deliver(early + s))
    x_push(xo, far, far, ny - 1).wait_recv()
    each(ny - 1, lambda s: x_push(xz_ref.at[far], far, beside(s), ny + s).start())

    def arrived(s):
        @pl.when(jnp.logical_not(jnp.logical_and(is_own, s == y)))
        def _():
            pltpu.make_async_remote_copy(
                src_ref=own.at[0], dst_ref=rs_recv.at[s], send_sem=rs_s.at[0], recv_sem=rs_r.at[s],
                device_id=(r, sib), device_id_type=MESH,
            ).wait_recv()

    each(ny, arrived)

    def add_up(g, _):
        rows = pl.ds(pl.multiple_of(g * 8, 8), 8)
        total = rs_recv[0, rows, :]
        for s in range(1, ny):
            total = total + rs_recv[s, rows, :]
        fp_ref[rows, :] = total
        return 0

    lax.fori_loop(0, fp_ref.shape[0] // 8, add_up, 0)

    z_push(zc, t, pair, ny - 1).wait_send()

    def settle(s):
        z_push(zc, t, along(s), s).wait_send()
        z_push(zg_ref.at[pair], pair, along(s), ny + s).wait_send()
        x_push(xo, r, beside(s), s).wait_send()
        x_push(xz_ref.at[far], far, beside(s), ny + s).wait_send()
        x_push(xo, beside(s), far, s).wait_recv()
        x_push(xo, lax.rem(far + 2 * (s + 1), nr), far, s).wait_recv()

    each(ny - 1, settle)
    each(nr, lambda s: to_sibling(s).wait_send())

    def sent(s):
        to_pair(s).wait_send()

        @pl.when(jnp.logical_not(jnp.logical_and(s == ny - 1, is_own)))
        def _():
            to_owner(s).wait_send()

    each(ny, sent)
    x_push(xo, r, far, ny - 1).wait_send()
    x_own.wait()


def tile_kernel(
    nr, og, vc, tiles, cuts,
    fp_ref, zg_ref, xz_ref, l_ref, r_ref, rowd_ref, cold_ref,
    out_ref,
    fg, rh, rl, yh, yl, xp, xo, xg, xh, xl, s_send, s_recv, own,
    fs, fr, xs, xr, ss, sr, os_, or_, loc,
):
    r, c = lax.axis_index("row"), lax.axis_index("col")
    t, k = c // 2, lax.rem(c, 2)
    sib = c + 1 - 2 * k
    half = fp_ref.shape[1]
    vir = r_ref.shape[0]
    va = vir // nr
    pad = xo.shape[0] // 2
    wide_pad = xh.shape[1] // nr
    blk = lax.rem(t - r + nr, nr)
    far = r + 1 - 2 * lax.rem(r, 2)
    near = nr // 2 - 1

    barrier = pltpu.get_barrier_semaphore()
    pl.semaphore_signal(barrier, inc=1, device_id=(r, sib), device_id_type=MESH)

    def greet(s, _):
        pl.semaphore_signal(barrier, inc=1, device_id=(lax.rem(r + 1 + s, nr), c), device_id_type=MESH)
        pl.semaphore_signal(
            barrier, inc=1, device_id=(r, 2 * lax.rem(t + 1 + s, nr) + k), device_id_type=MESH
        )
        return 0

    lax.fori_loop(0, nr - 1, greet, 0)

    hi, lo = halves(r_ref[...])
    rh[:vir, :] = hi
    rl[:vir, :] = lo
    hi, lo = halves(l_ref[pl.ds(pl.multiple_of(t * va, 8), va), :])
    rh[vir:, :] = hi
    rl[vir:, :] = lo
    xp[...] = jnp.zeros_like(xp)
    fg[blk] = fp_ref[...]
    pl.semaphore_wait(barrier, 2 * nr - 1)

    ny = nr // 2
    y, low = t // 2, lax.rem(t, 2)
    pair = t + 1 - 2 * low

    def along(s):
        return 2 * lax.rem(y + 1 + s, ny) + low

    def slot_of(other):
        return lax.rem(other - r + nr, nr)

    def f_push(m, src_ref, slot, peer, sem):
        at, width = cuts[m]
        cols = pl.ds(at, width)
        return pltpu.make_async_remote_copy(
            src_ref=src_ref.at[:, cols], dst_ref=fg.at[slot, :, cols],
            send_sem=fs.at[m, sem], recv_sem=fr.at[m, slot],
            device_id=(r, 2 * peer + k), device_id_type=MESH,
        )

    def each(count, body):
        def one(s, _):
            body(s)
            return 0

        lax.fori_loop(0, count, one, 0)

    def f_start(m):
        f_push(m, fp_ref, blk, pair, ny - 1).start()
        each(ny - 1, lambda s: f_push(m, fp_ref, blk, along(s), s).start())

    def f_forward(m):
        f_push(m, fp_ref, slot_of(pair), pair, ny - 1).wait_recv()
        each(
            ny - 1,
            lambda s: f_push(m, fg.at[slot_of(pair)], slot_of(pair), along(s), ny + s).start(),
        )

    def f_rest(m):
        def one(s):
            f_push(m, fp_ref, slot_of(along(s)), pair, ny - 1).wait_recv()
            f_push(m, fp_ref, slot_of(along(s) + pair - t), pair, ny - 1).wait_recv()

        each(ny - 1, one)

    last = len(cuts) - 1
    for m in range(last):
        f_start(m)

    def x_push(m, src_ref, slot, dst, sem):
        return pltpu.make_async_remote_copy(
            src_ref=src_ref, dst_ref=xg.at[slot, :, pl.ds(*cuts[m])],
            send_sem=xs.at[m, sem], recv_sem=xr.at[m, slot],
            device_id=(dst, c), device_id_type=MESH,
        )

    def x_mine(m):
        return xo.at[:, pl.ds(*cuts[m])]

    def x_far(m):
        return xg.at[far, :, pl.ds(*cuts[m])]

    def beside(s):
        return lax.rem(r + 2 * (s + 1), nr)

    def x_start(m):
        x_push(m, x_mine(m), r, far, near).start()
        each(near, lambda s: x_push(m, x_mine(m), r, beside(s), s).start())

    def x_arrive(m, slot):
        x_push(m, x_mine(m), slot, far, near).wait_recv()

    def x_forward(m):
        x_arrive(m, far)
        each(near, lambda s: x_push(m, x_far(m), far, beside(s), near + 1 + s).start())

    def rotate(g_ref, fitted, at, width):
        y_at = half * fitted + at
        count = vir + va * fitted
        for ii in range(og):
            gh, gl = halves(g_ref[:, ii * va : (ii + 1) * va, at : at + width].reshape(vir, width))
            both = dot3(rh[:count], rl[:count], gh, gl, ((1,), (0,)))
            hi, lo = halves(both[:vir])
            yh[ii * vir : (ii + 1) * vir, y_at : y_at + width] = hi
            yl[ii * vir : (ii + 1) * vir, y_at : y_at + width] = lo
            if fitted:
                for par in range(2):
                    rows = both[vir + par * vc : vir + (par + 1) * vc]
                    for p in range(width // 128):
                        xp[p, pl.ds(par * pad + ii, vc, stride=og), :] = rows[:, p * 128 : (p + 1) * 128]
        if fitted:
            for p in range(width // 128):
                xo[:, at + p * 128 : at + (p + 1) * 128] = xp[p]

    def take(src, load, x_at, width):
        rows = pl.ds(pl.multiple_of(src * wide_pad, 16), pad)
        for par in range(2):
            hi, lo = halves(load(par * pad))
            xh[par, rows, x_at : x_at + width] = hi
            xl[par, rows, x_at : x_at + width] = lo

    def take_own(m):
        at, width = cuts[m]
        take(r, lambda row: xo[row : row + pad, at : at + width], at, width)

    def take_from(m, src):
        at, width = cuts[m]
        take(src, lambda row: xg[src, row : row + pad, at : at + width], at, width)

    def take_near(m, base):
        def one(s):
            src = lax.rem(base + 2 * (s + 1), nr)
            x_arrive(m, src)
            take_from(m, src)

        each(near, one)

    f_forward(0)
    if last:
        f_start(last)
    each(nr, lambda src: take(src, lambda row: xz_ref[src, row : row + pad, :], half, half))
    rotate(zg_ref, 0, 0, half)
    if last > 1:
        f_forward(1)
    for m, (at, width) in enumerate(cuts):
        f_rest(m)
        rotate(fg, 1, at, width)
        x_start(m)
        if m == 0 and last:
            f_forward(last)
        if m:
            x_forward(m - 1)
    x_forward(last)
    for m in range(len(cuts)):
        take_own(m)
        take_from(m, far)
        take_near(m, r)
        take_near(m, far)

    def to_sibling(n, width):
        return pltpu.make_async_remote_copy(
            src_ref=s_send.at[lax.rem(n, 2), :, pl.ds(0, width)], dst_ref=s_recv.at[n, :, pl.ds(0, width)],
            send_sem=ss.at[lax.rem(n, 2)], recv_sem=sr.at[n],
            device_id=(r, sib), device_id_type=MESH,
        )

    def to_row(n, width, s, src):
        dst = lax.rem(r + 1 + s, nr)
        cols = pl.ds(pl.multiple_of(n * WIDE, 128), width)
        return pltpu.make_async_remote_copy(
            src_ref=own.at[pl.ds(pl.multiple_of(dst * wide_pad, 8), pad), cols],
            dst_ref=out_ref.at[src, :, cols],
            send_sem=os_.at[n, s], recv_sem=or_.at[n, src],
            device_id=(dst, c), device_id_type=MESH,
        )

    def stay(n, width):
        cols = pl.ds(pl.multiple_of(n * WIDE, 128), width)
        return pltpu.make_async_copy(
            own.at[pl.ds(pl.multiple_of(r * wide_pad, 8), pad), cols], out_ref.at[r, :, cols], loc.at[n]
        )

    def tile(n, width, slot_used):
        rows = pl.ds(pl.multiple_of(n * WIDE, 128), width)
        wh, wl = yh[rows, :], yl[rows, :]

        def product(par):
            return dot3(xh[par], xl[par], wh, wl, ((1,), (1,)))

        @pl.when(slot_used)
        def _():
            to_sibling(n - 2, WIDE).wait_send()

        s_send[lax.rem(n, 2), :, 0:width] = product(1 - k)
        to_sibling(n, width).start()
        own[:, rows] = product(k)
        to_sibling(n, width).wait_recv()
        reps = width // 128

        def close(g, _):
            at = pl.ds(pl.multiple_of(g * wide_pad, 8), wide_pad)
            rowd = rowd_ref[at, :]
            for m in range(reps):
                cols = pl.ds(pl.multiple_of(n * WIDE + m * 128, 128), 128)
                here = own[at, cols] + s_recv[n, at, m * 128 : (m + 1) * 128]
                own[at, cols] = here / (rowd + cold_ref[0:1, cols])
            return 0

        lax.fori_loop(0, nr, close, 0)

        def send(s, _):
            to_row(n, width, s, r).start()
            return 0

        lax.fori_loop(0, nr - 1, send, 0)
        stay(n, width).start()

    tail = yh.shape[0] - (tiles - 1) * WIDE

    def full(n, _):
        tile(n, WIDE, n > 1)
        return 0

    lax.fori_loop(0, tiles - 1, full, 0)
    tile(jnp.int32(tiles - 1), tail, tiles > 2)

    def settle(n, width):
        def one(s, _):
            src = lax.rem(r + 1 + s, nr)
            to_row(n, width, s, src).wait()
            return 0

        lax.fori_loop(0, nr - 1, one, 0)
        stay(n, width).wait()

    def settle_full(n, _):
        settle(n, WIDE)
        return 0

    lax.fori_loop(0, tiles - 1, settle_full, 0)
    settle(jnp.int32(tiles - 1), tail)
    to_sibling(jnp.int32(tiles - 2), WIDE).wait_send()
    to_sibling(jnp.int32(tiles - 1), tail).wait_send()
    for m in range(len(cuts)):
        x_push(m, x_mine(m), r, far, near).wait_send()
        each(near, lambda s, m=m: x_push(m, x_mine(m), r, beside(s), s).wait_send())
        each(near, lambda s, m=m: x_push(m, x_far(m), far, beside(s), near + 1 + s).wait_send())
    for m in range(len(cuts)):
        f_push(m, fp_ref, blk, pair, ny - 1).wait_send()
        each(ny - 1, lambda s, m=m: f_push(m, fp_ref, blk, along(s), s).wait_send())
        each(ny - 1, lambda s, m=m: f_push(m, fp_ref, blk, along(s), ny + s).wait_send())


def lay_kernel(nr, og, vir, occ, in_ref, out_ref, op):
    count, wide = op.shape[0], in_ref.shape[2]
    for src in range(nr):
        for jj in range(og):
            for p in range(count):
                start = jj * vir + p * 128
                n = min(128, wide - start)
                v = in_ref[src, :, start : start + n]
                if n < 128:
                    v = jnp.concatenate([v, jnp.zeros((8, 128 - n), F32)], axis=1)
                op[p, pl.ds(src * og + jj, 8, stride=occ), :] = v
    for p in range(count):
        n = min(128, vir - p * 128)
        out_ref[:, p * 128 : p * 128 + n] = op[p, :, :n]


def shards(amplitudes, aux_left, aux_right, left_rotation, right_rotation, occ_energy, vir_energy):
    nr, nc = lax.axis_size("row"), lax.axis_size("col")
    occ, vir = occ_energy.shape[0], vir_energy.shape[0]
    naux = aux_left.shape[1]
    half = naux // 2
    og, va, vc = occ // nr, vir // nr, vir // nc
    piece = og * va
    rows = vc * og
    pad, wide_pad = up(rows, 8), up(rows, 16)
    dma = pltpu.SemaphoreType.DMA
    vmem = pl.BlockSpec(memory_space=pltpu.VMEM)
    hbm = pl.BlockSpec(memory_space=pl.ANY)
    limit = 60 * 1024 * 1024

    fp, zg, xz = pl.pallas_call(
        functools.partial(gather_kernel, nr, occ),
        out_shape=[
            jax.ShapeDtypeStruct((piece, half), F32),
            jax.ShapeDtypeStruct((nr, piece, half), F32),
            jax.ShapeDtypeStruct((nr, 2 * pad, half), F32),
        ],
        in_specs=[vmem] * 4,
        out_specs=[vmem, vmem, hbm],
        scratch_shapes=[
            pltpu.VMEM((up(amplitudes.shape[1], 128) // 128, amplitudes.shape[0], 128), F32),
            pltpu.VMEM((up(naux, 128) // 128, aux_right.shape[0], 128), F32),
            pltpu.VMEM((aux_left.shape[0], naux), BF16),
            pltpu.VMEM((aux_left.shape[0], naux), BF16),
            pltpu.VMEM((nr, piece, half), F32),
            pltpu.VMEM((nr, piece, half), F32),
            pltpu.VMEM((nr, piece, half), F32),
            pltpu.VMEM((nr // 2, piece, half), F32),
            pltpu.VMEM((nr // 2, piece, half), F32),
            pltpu.VMEM((og, vc, half), F32),
            pltpu.VMEM((og, vc, half), F32),
            pltpu.VMEM((piece, half), F32),
            pltpu.VMEM((half // 128, 2 * pad, 128), F32),
            pltpu.VMEM((2 * pad, half), F32),
            dma((nr,)), dma((nr,)), dma((nr,)), dma((nr,)), dma((nr,)), dma((nr,)), dma, dma,
            dma((nr,)), dma((nr,)), dma((nr,)), dma((nr,)), dma,
        ],
        compiler_params=pltpu.CompilerParams(collective_id=0, has_side_effects=True, vmem_limit_bytes=limit),
        name="fit_gather",
    )(amplitudes, aux_left, aux_right, left_rotation)

    cols = og * vir
    cols_pad = up(cols, 128)
    tiles = up(cols_pad, WIDE) // WIDE
    cuts = [(at, min(256, half - at)) for at in range(0, half, 256)]
    r, c = lax.axis_index("row"), lax.axis_index("col")
    vir_here = lax.dynamic_slice_in_dim(vir_energy, c * vc, vc)
    occ_here = lax.dynamic_slice_in_dim(occ_energy, r * og, og)
    rowd = (vir_here[None, :, None] - occ_energy.reshape(nr, 1, og)).reshape(nr, rows)
    rowd = jnp.pad(rowd, ((0, 0), (0, wide_pad - rows)), constant_values=1.0).reshape(nr * wide_pad, 1)
    rowd = jnp.broadcast_to(rowd, (nr * wide_pad, 128))
    cold = (vir_energy[None, :] - occ_here[:, None]).reshape(1, cols)
    cold = jnp.pad(cold, ((0, 0), (0, cols_pad - cols)), constant_values=1.0)
    cold = jnp.broadcast_to(cold, (8, cols_pad))

    moved = pl.pallas_call(
        functools.partial(tile_kernel, nr, og, vc, tiles, cuts),
        out_shape=jax.ShapeDtypeStruct((nr, pad, cols_pad), F32),
        in_specs=[vmem] * 7,
        out_specs=hbm,
        scratch_shapes=[
            pltpu.VMEM((nr, piece, half), F32),
            pltpu.VMEM((vir + va, vir), BF16),
            pltpu.VMEM((vir + va, vir), BF16),
            pltpu.VMEM((cols_pad, naux), BF16),
            pltpu.VMEM((cols_pad, naux), BF16),
            pltpu.VMEM((half // 128, 2 * pad, 128), F32),
            pltpu.VMEM((2 * pad, half), F32),
            pltpu.VMEM((nr, 2 * pad, half), F32),
            pltpu.VMEM((2, nr * wide_pad, naux), BF16),
            pltpu.VMEM((2, nr * wide_pad, naux), BF16),
            pltpu.VMEM((2, nr * wide_pad, WIDE), F32),
            pltpu.VMEM((tiles, nr * wide_pad, WIDE), F32),
            pltpu.VMEM((nr * wide_pad, cols_pad), F32),
            dma((len(cuts), nr)), dma((len(cuts), nr)),
            dma((len(cuts), nr)), dma((len(cuts), nr)), dma((2,)), dma((tiles,)),
            dma((tiles, nr)), dma((tiles, nr)), dma((tiles,)),
        ],
        compiler_params=pltpu.CompilerParams(collective_id=1, has_side_effects=True, vmem_limit_bytes=limit),
        name="tile_exchange",
    )(fp, zg, xz, left_rotation, right_rotation, rowd, cold)

    out = pl.pallas_call(
        functools.partial(lay_kernel, nr, og, vir, occ),
        grid=(pad // 8,),
        out_shape=jax.ShapeDtypeStruct((rows * occ, vir), F32),
        in_specs=[pl.BlockSpec((nr, 8, cols_pad), lambda g: (0, g, 0))],
        out_specs=pl.BlockSpec((8 * occ, vir), lambda g: (g, 0)),
        scratch_shapes=[pltpu.VMEM((up(vir, 128) // 128, 8 * occ, 128), F32)],
        compiler_params=pltpu.CompilerParams(vmem_limit_bytes=limit),
        name="lay_out",
    )(moved)
    return out.reshape(vc, og, occ, vir)


def solution(mesh):
    placed = (P("row", "col"), P("col", None), P("col", None), P(), P(), P(), P())
    return jax.shard_map(
        shards, mesh=mesh, in_specs=placed, out_specs=P("col", "row", None, None), check_vma=False
    )
```

```python
import functools

import jax
import jax.numpy as jnp
from jax import lax
from jax.experimental import pallas as pl
from jax.experimental.pallas import tpu as pltpu
from jax.sharding import PartitionSpec as P

MESH = pl.DeviceIdType.MESH
F32 = jnp.float32
BF16 = jnp.bfloat16
WIDE = 256


def halves(x):
    hi = x.astype(BF16)
    return hi, (x - hi.astype(F32)).astype(BF16)


def dot3(xh, xl, yh, yl, dims):
    def dot(a, b):
        return lax.dot_general(a, b, (dims, ((), ())), preferred_element_type=F32)

    return dot(xl, yh) + dot(xh, yl) + dot(xh, yh)


def up(n, unit):
    return -(-n // unit) * unit


def planes(src, dst):
    width, rows = src.shape[1], 40 if src.shape[0] % 40 == 0 else src.shape[0]

    def one(g, _):
        at = pl.ds(pl.multiple_of(g * rows, 8), rows)
        for p in range(dst.shape[0]):
            n = min(128, width - p * 128)
            dst[p, at, :n] = src[at, p * 128 : p * 128 + n]
        return 0

    lax.fori_loop(0, src.shape[0] // rows, one, 0)


def every(src, start, count, stride, width):
    parts = [src[p, pl.ds(start, count, stride=stride), :] for p in range(src.shape[0])]
    return jnp.concatenate(parts, axis=1)[:, :width]


def gather_kernel(
    nr, occ, zcuts,
    t_ref, b_ref, z_ref, l_ref,
    fp_ref, zg_ref, xz_ref,
    tp, zp, bh, bl, sib_send, sib_recv, own, z_recv, rs_recv, zs_send, zs_recv, zc, xp, xo,
    sib_s, sib_r, zz_s, zz_r, rs_s, rs_r, zs_s, zs_r, za_s, za_r, xs, xr, loc,
):
    r, c = lax.axis_index("row"), lax.axis_index("col")
    t, k = c // 2, lax.rem(c, 2)
    sib = c + 1 - 2 * k
    og = occ // nr
    va = t_ref.shape[0] // occ
    vc = z_ref.shape[0] // occ
    half = b_ref.shape[1] // 2
    blk = lax.rem(t - r + nr, nr)
    is_own = lax.rem(r + r, nr) == t
    ny = nr // 2
    y, low = t // 2, lax.rem(t, 2)
    pair = t + 1 - 2 * low

    far = r + 1 - 2 * lax.rem(r, 2)
    vir = va * nr
    pad = xo.shape[0] // 2

    barrier = pltpu.get_barrier_semaphore()
    pl.semaphore_signal(barrier, inc=1, device_id=(r, sib), device_id_type=MESH)

    pl.semaphore_signal(barrier, inc=1, device_id=(r, 2 * pair + k), device_id_type=MESH)

    def along(s):
        return 2 * lax.rem(y + 1 + s, ny) + low

    def each(count, body):
        def one(s, _):
            body(s)
            return 0

        lax.fori_loop(0, count, one, 0)

    def beside(s):
        return lax.rem(r + 2 * (s + 1), nr)

    pl.semaphore_signal(barrier, inc=1, device_id=(far, c), device_id_type=MESH)

    def greet(s):
        pl.semaphore_signal(barrier, inc=1, device_id=(r, 2 * along(s) + k), device_id_type=MESH)
        pl.semaphore_signal(barrier, inc=1, device_id=(beside(s), c), device_id_type=MESH)

    each(ny - 1, greet)

    def greet_source(s):
        @pl.when(jnp.logical_not(jnp.logical_and(is_own, s == y)))
        def _():
            pl.semaphore_signal(
                barrier, inc=1, device_id=(blk, 2 * (2 * s + low) + k), device_id_type=MESH
            )

    each(ny, greet_source)

    planes(t_ref, tp)
    planes(z_ref, zp)
    mine, other = pl.ds(pl.multiple_of(k * half, half), half), pl.ds(pl.multiple_of((1 - k) * half, half), half)
    for at, cols in ((0, other), (half, mine)):
        hi, lo = halves(b_ref[:, cols])
        bh[:, at : at + half] = hi
        bl[:, at : at + half] = lo

    first = k == 0
    kept = []
    for jj in range(og):
        z = every(zp, r * og + jj, vc, occ, z_ref.shape[1])
        z0, z1 = z[:, :half], z[:, half:]
        zs_send[jj] = jnp.where(first, z1, z0)
        kept.append(jnp.where(first, z0, z1))
        zc[jj * va : jj * va + vc, :] = kept[-1]

    @pl.when(is_own)
    def _():
        pl.semaphore_wait(barrier, nr + ny)

    @pl.when(jnp.logical_not(is_own))
    def _():
        pl.semaphore_wait(barrier, nr + ny + 1)

    z_swap = pltpu.make_async_remote_copy(
        src_ref=zs_send, dst_ref=zs_recv, send_sem=zs_s, recv_sem=zs_r,
        device_id=(r, sib), device_id_type=MESH,
    )
    z_swap.start()
    z_swap.wait()
    for jj in range(og):
        z_mine = zc[jj * va : jj * va + vc, :]
        z_sib = zs_recv[jj]
        zc[jj * va : (jj + 1) * va, :] = jnp.concatenate(
            [jnp.where(first, z_mine, z_sib), jnp.where(first, z_sib, z_mine)], axis=0
        )

    def z_push(m, src_ref, slot, peer, sem):
        lanes = pl.ds(*zcuts[m])
        return pltpu.make_async_remote_copy(
            src_ref=src_ref.at[:, lanes], dst_ref=zg_ref.at[slot, :, lanes],
            send_sem=za_s.at[m, sem], recv_sem=za_r.at[m, slot],
            device_id=(r, 2 * peer + k), device_id_type=MESH,
        )

    def z_start(m):
        z_push(m, zc, t, pair, ny - 1).start()
        each(ny - 1, lambda s: z_push(m, zc, t, along(s), s).start())

    def z_forward(m):
        z_push(m, zc, pair, pair, ny - 1).wait_recv()
        each(ny - 1, lambda s: z_push(m, zg_ref.at[pair], pair, along(s), ny + s).start())

    def z_forwarded(m):
        each(ny - 1, lambda s: z_push(m, zg_ref.at[pair], pair, along(s), ny + s).wait_send())

    z_start(0)
    zg_ref[t] = zc[...]

    def to_sibling(s):
        return pltpu.make_async_remote_copy(
            src_ref=sib_send.at[s], dst_ref=sib_recv.at[s], send_sem=sib_s.at[s], recv_sem=sib_r.at[s],
            device_id=(r, sib), device_id_type=MESH,
        )

    def owner(s):
        stays = s // ny
        side = stays * low + (1 - stays) * (1 - low)
        return 2 * lax.rem(y + 1 + lax.rem(s, ny), ny) + side

    def to_pair(s):
        return pltpu.make_async_remote_copy(
            src_ref=own.at[s], dst_ref=z_recv.at[s], send_sem=zz_s.at[s], recv_sem=zz_r.at[s],
            device_id=(r, 2 * pair + k), device_id_type=MESH,
        )

    def to_owner(s):
        ot = owner(ny + s)
        return pltpu.make_async_remote_copy(
            src_ref=own.at[ny + s], dst_ref=rs_recv.at[y], send_sem=rs_s.at[s], recv_sem=rs_r.at[y],
            device_id=(lax.rem(ot - r + nr, nr), 2 * ot + k), device_id_type=MESH,
        )

    def finish(s):
        to_sibling(s).wait_recv()
        own[s] = own[s] + sib_recv[s]

        @pl.when(s == 0)
        def _():
            to_pair(0).start()

        @pl.when(s == ny + 1)
        def _():
            to_pair(1).start()

    def step(s):
        dst = lax.rem(owner(s) - r + nr, nr)
        x = jnp.concatenate(
            [every(tp, dst * og + ii, va, occ, t_ref.shape[1]) for ii in range(og)], axis=0
        )
        xh, xl = halves(x)
        part = dot3(xh, xl, bh[...], bl[...], ((1,), (0,)))
        sib_send[s] = part[:, :half]
        own[s] = part[:, half:]
        to_sibling(s).start()

        @pl.when(s > 0)
        def _():
            finish(s - 1)

        @pl.when(s == ny)
        def _():
            z_forward(0)

    def deliver(s):
        to_pair(s).wait_recv()
        own[ny + s] = own[ny + s] + z_recv[s]
        here = jnp.logical_and(s == ny - 1, is_own)

        @pl.when(here)
        def _():
            rs_recv[y] = own[ny + s]

        @pl.when(jnp.logical_not(here))
        def _():
            to_owner(s).start()

    def x_push(m, src_ref, slot, dst, sem):
        lanes = pl.ds(*zcuts[m])
        return pltpu.make_async_remote_copy(
            src_ref=src_ref.at[:, lanes], dst_ref=xz_ref.at[slot, :, lanes],
            send_sem=xs.at[m, sem], recv_sem=xr.at[m, slot],
            device_id=(dst, c), device_id_type=MESH,
        )

    def x_forward(m):
        x_push(m, xo, far, far, ny - 1).wait_recv()
        each(ny - 1, lambda s: x_push(m, xz_ref.at[far], far, beside(s), ny + s).start())

    lh, ll = halves(l_ref[pl.ds(pl.multiple_of(t * va, 8), va), :])
    xp[...] = jnp.zeros_like(xp)

    def z_rows(m):
        def z_rest(s):
            z_push(m, zc, along(s), along(s), s).wait_recv()
            z_push(m, zc, along(s) + pair - t, pair, s).wait_recv()

        each(ny - 1, z_rest)
        at, width = zcuts[m]
        for ii in range(og):
            gh, gl = halves(zg_ref[:, ii * va : (ii + 1) * va, at : at + width].reshape(vir, width))
            x = dot3(lh, ll, gh, gl, ((1,), (0,)))
            for par in range(2):
                for p in range(width // 128):
                    xp[p, pl.ds(par * pad + ii, vc, stride=og), :] = x[
                        par * vc : (par + 1) * vc, p * 128 : (p + 1) * 128
                    ]
        for p in range(width // 128):
            xo[:, at + p * 128 : at + (p + 1) * 128] = xp[p]
        x_push(m, xo, r, far, ny - 1).start()
        each(ny - 1, lambda s: x_push(m, xo, r, beside(s), s).start())

    two = len(zcuts) > 1
    each(nr, step)
    finish(nr - 1)
    deliver(0)
    z_forwarded(0)
    if two:
        z_start(1)
    to_pair(1).wait_send()
    if ny > 2:
        to_pair(2).start()
    deliver(1)
    if two:
        z_forward(1)
    z_rows(0)
    for s in range(2, ny):
        to_pair(s).wait_send()
        if s + 1 < ny:
            to_pair(s + 1).start()
        deliver(s)
        if s == 2:
            x_forward(0)
            if two:
                z_rows(1)
    if ny < 3:
        x_forward(0)
        if two:
            z_rows(1)
    if two:
        x_forward(1)
    x_own = pltpu.make_async_copy(xo, xz_ref.at[r], loc)
    x_own.start()

    def arrived(s):
        @pl.when(jnp.logical_not(jnp.logical_and(is_own, s == y)))
        def _():
            pltpu.make_async_remote_copy(
                src_ref=own.at[0], dst_ref=rs_recv.at[s], send_sem=rs_s.at[0], recv_sem=rs_r.at[s],
                device_id=(r, sib), device_id_type=MESH,
            ).wait_recv()

    each(ny, arrived)

    def add_up(g, _):
        rows = pl.ds(pl.multiple_of(g * 8, 8), 8)
        total = rs_recv[0, rows, :]
        for s in range(1, ny):
            total = total + rs_recv[s, rows, :]
        fp_ref[rows, :] = total
        return 0

    lax.fori_loop(0, fp_ref.shape[0] // 8, add_up, 0)

    for m in range(len(zcuts)):
        z_push(m, zc, t, pair, ny - 1).wait_send()
        x_push(m, xo, r, far, ny - 1).wait_send()

        def settle(s, m=m):
            z_push(m, zc, t, along(s), s).wait_send()
            x_push(m, xo, r, beside(s), s).wait_send()
            x_push(m, xz_ref.at[far], far, beside(s), ny + s).wait_send()
            x_push(m, xo, beside(s), far, s).wait_recv()
            x_push(m, xo, lax.rem(far + 2 * (s + 1), nr), far, s).wait_recv()

        each(ny - 1, settle)
    if two:
        z_forwarded(1)
    each(nr, lambda s: to_sibling(s).wait_send())

    def sent(s):
        @pl.when(jnp.logical_not(jnp.logical_and(s == ny - 1, is_own)))
        def _():
            to_owner(s).wait_send()

    to_pair(0).wait_send()
    each(ny, sent)
    x_own.wait()


def tile_kernel(
    nr, og, vc, tiles, cuts,
    fp_ref, zg_ref, xz_ref, l_ref, r_ref, rowd_ref, cold_ref,
    out_ref,
    fg, rh, rl, yh, yl, xp, xo, xg, xh, xl, s_send, s_recv, own,
    fs, fr, xs, xr, ss, sr, os_, or_, loc,
):
    r, c = lax.axis_index("row"), lax.axis_index("col")
    t, k = c // 2, lax.rem(c, 2)
    sib = c + 1 - 2 * k
    half = fp_ref.shape[1]
    vir = r_ref.shape[0]
    va = vir // nr
    pad = xo.shape[0] // 2
    wide_pad = xh.shape[1] // nr
    blk = lax.rem(t - r + nr, nr)
    far = r + 1 - 2 * lax.rem(r, 2)
    near = nr // 2 - 1

    barrier = pltpu.get_barrier_semaphore()
    pl.semaphore_signal(barrier, inc=1, device_id=(r, sib), device_id_type=MESH)

    def greet(s, _):
        pl.semaphore_signal(barrier, inc=1, device_id=(lax.rem(r + 1 + s, nr), c), device_id_type=MESH)
        pl.semaphore_signal(
            barrier, inc=1, device_id=(r, 2 * lax.rem(t + 1 + s, nr) + k), device_id_type=MESH
        )
        return 0

    lax.fori_loop(0, nr - 1, greet, 0)

    hi, lo = halves(r_ref[...])
    rh[:vir, :] = hi
    rl[:vir, :] = lo
    hi, lo = halves(l_ref[pl.ds(pl.multiple_of(t * va, 8), va), :])
    rh[vir:, :] = hi
    rl[vir:, :] = lo
    xp[...] = jnp.zeros_like(xp)
    fg[blk] = fp_ref[...]
    pl.semaphore_wait(barrier, 2 * nr - 1)

    ny = nr // 2
    y, low = t // 2, lax.rem(t, 2)
    pair = t + 1 - 2 * low

    def along(s):
        return 2 * lax.rem(y + 1 + s, ny) + low

    def slot_of(other):
        return lax.rem(other - r + nr, nr)

    def f_push(m, src_ref, slot, peer, sem):
        at, width = cuts[m]
        cols = pl.ds(at, width)
        return pltpu.make_async_remote_copy(
            src_ref=src_ref.at[:, cols], dst_ref=fg.at[slot, :, cols],
            send_sem=fs.at[m, sem], recv_sem=fr.at[m, slot],
            device_id=(r, 2 * peer + k), device_id_type=MESH,
        )

    def each(count, body):
        def one(s, _):
            body(s)
            return 0

        lax.fori_loop(0, count, one, 0)

    def f_start(m):
        f_push(m, fp_ref, blk, pair, ny - 1).start()
        each(ny - 1, lambda s: f_push(m, fp_ref, blk, along(s), s).start())

    def f_forward(m):
        f_push(m, fp_ref, slot_of(pair), pair, ny - 1).wait_recv()
        each(
            ny - 1,
            lambda s: f_push(m, fg.at[slot_of(pair)], slot_of(pair), along(s), ny + s).start(),
        )

    def f_rest(m):
        def one(s):
            f_push(m, fp_ref, slot_of(along(s)), pair, ny - 1).wait_recv()
            f_push(m, fp_ref, slot_of(along(s) + pair - t), pair, ny - 1).wait_recv()

        each(ny - 1, one)

    last = len(cuts) - 1
    f_start(0)

    def f_forwarded(m):
        each(ny - 1, lambda s: f_push(m, fp_ref, blk, along(s), ny + s).wait_send())

    def x_push(m, src_ref, slot, dst, sem):
        return pltpu.make_async_remote_copy(
            src_ref=src_ref, dst_ref=xg.at[slot, :, pl.ds(*cuts[m])],
            send_sem=xs.at[m, sem], recv_sem=xr.at[m, slot],
            device_id=(dst, c), device_id_type=MESH,
        )

    def x_mine(m):
        return xo.at[:, pl.ds(*cuts[m])]

    def x_far(m):
        return xg.at[far, :, pl.ds(*cuts[m])]

    def beside(s):
        return lax.rem(r + 2 * (s + 1), nr)

    def x_start(m):
        x_push(m, x_mine(m), r, far, near).start()
        each(near, lambda s: x_push(m, x_mine(m), r, beside(s), s).start())

    def x_arrive(m, slot):
        x_push(m, x_mine(m), slot, far, near).wait_recv()

    def x_forward(m):
        x_arrive(m, far)
        each(near, lambda s: x_push(m, x_far(m), far, beside(s), near + 1 + s).start())

    def rotate(g_ref, fitted, at, width):
        y_at = half * fitted + at
        count = vir + va * fitted
        for ii in range(og):
            gh, gl = halves(g_ref[:, ii * va : (ii + 1) * va, at : at + width].reshape(vir, width))
            both = dot3(rh[:count], rl[:count], gh, gl, ((1,), (0,)))
            hi, lo = halves(both[:vir])
            yh[ii * vir : (ii + 1) * vir, y_at : y_at + width] = hi
            yl[ii * vir : (ii + 1) * vir, y_at : y_at + width] = lo
            if fitted:
                for par in range(2):
                    rows = both[vir + par * vc : vir + (par + 1) * vc]
                    for p in range(width // 128):
                        xp[p, pl.ds(par * pad + ii, vc, stride=og), :] = rows[:, p * 128 : (p + 1) * 128]
        if fitted:
            for p in range(width // 128):
                xo[:, at + p * 128 : at + (p + 1) * 128] = xp[p]

    def take(src, load, x_at, width):
        rows = pl.ds(pl.multiple_of(src * wide_pad, 16), pad)
        for par in range(2):
            hi, lo = halves(load(par * pad))
            xh[par, rows, x_at : x_at + width] = hi
            xl[par, rows, x_at : x_at + width] = lo

    def take_own(m):
        at, width = cuts[m]
        take(r, lambda row: xo[row : row + pad, at : at + width], at, width)

    def take_from(m, src):
        at, width = cuts[m]
        take(src, lambda row: xg[src, row : row + pad, at : at + width], at, width)

    def take_near(m, base):
        def one(s):
            src = lax.rem(base + 2 * (s + 1), nr)
            x_arrive(m, src)
            take_from(m, src)

        each(near, one)

    each(nr, lambda src: take(src, lambda row: xz_ref[src, row : row + pad, :], half, half))
    f_forward(0)
    rotate(zg_ref, 0, 0, half)
    for m, (at, width) in enumerate(cuts):
        f_forwarded(m)
        if m < last:
            f_start(m + 1)
        f_rest(m)
        rotate(fg, 1, at, width)
        x_start(m)
        if m < last:
            f_forward(m + 1)
        if m:
            x_forward(m - 1)
    x_forward(last)
    for m in range(len(cuts)):
        take_own(m)
        take_from(m, far)
        take_near(m, r)
        take_near(m, far)

    def to_sibling(n, width):
        return pltpu.make_async_remote_copy(
            src_ref=s_send.at[lax.rem(n, 2), :, pl.ds(0, width)], dst_ref=s_recv.at[n, :, pl.ds(0, width)],
            send_sem=ss.at[lax.rem(n, 2)], recv_sem=sr.at[n],
            device_id=(r, sib), device_id_type=MESH,
        )

    def to_row(n, width, s, src):
        dst = lax.rem(r + 1 + s, nr)
        cols = pl.ds(pl.multiple_of(n * WIDE, 128), width)
        return pltpu.make_async_remote_copy(
            src_ref=own.at[pl.ds(pl.multiple_of(dst * wide_pad, 8), pad), cols],
            dst_ref=out_ref.at[src, :, cols],
            send_sem=os_.at[n, s], recv_sem=or_.at[n, src],
            device_id=(dst, c), device_id_type=MESH,
        )

    def stay(n, width):
        cols = pl.ds(pl.multiple_of(n * WIDE, 128), width)
        return pltpu.make_async_copy(
            own.at[pl.ds(pl.multiple_of(r * wide_pad, 8), pad), cols], out_ref.at[r, :, cols], loc.at[n]
        )

    def tile(n, width, slot_used):
        rows = pl.ds(pl.multiple_of(n * WIDE, 128), width)
        wh, wl = yh[rows, :], yl[rows, :]

        def product(par):
            return dot3(xh[par], xl[par], wh, wl, ((1,), (1,)))

        @pl.when(slot_used)
        def _():
            to_sibling(n - 2, WIDE).wait_send()

        s_send[lax.rem(n, 2), :, 0:width] = product(1 - k)
        to_sibling(n, width).start()
        own[:, rows] = product(k)
        to_sibling(n, width).wait_recv()
        reps = width // 128

        def close(g, _):
            at = pl.ds(pl.multiple_of(g * wide_pad, 8), wide_pad)
            rowd = rowd_ref[at, :]
            for m in range(reps):
                cols = pl.ds(pl.multiple_of(n * WIDE + m * 128, 128), 128)
                here = own[at, cols] + s_recv[n, at, m * 128 : (m + 1) * 128]
                own[at, cols] = here / (rowd + cold_ref[0:1, cols])
            return 0

        lax.fori_loop(0, nr, close, 0)

        def send(s, _):
            to_row(n, width, s, r).start()
            return 0

        lax.fori_loop(0, nr - 1, send, 0)
        stay(n, width).start()

    tail = yh.shape[0] - (tiles - 1) * WIDE

    def full(n, _):
        tile(n, WIDE, n > 1)
        return 0

    lax.fori_loop(0, tiles - 1, full, 0)
    tile(jnp.int32(tiles - 1), tail, tiles > 2)

    def settle(n, width):
        def one(s, _):
            src = lax.rem(r + 1 + s, nr)
            to_row(n, width, s, src).wait()
            return 0

        lax.fori_loop(0, nr - 1, one, 0)
        stay(n, width).wait()

    def settle_full(n, _):
        settle(n, WIDE)
        return 0

    lax.fori_loop(0, tiles - 1, settle_full, 0)
    settle(jnp.int32(tiles - 1), tail)
    to_sibling(jnp.int32(tiles - 2), WIDE).wait_send()
    to_sibling(jnp.int32(tiles - 1), tail).wait_send()
    for m in range(len(cuts)):
        x_push(m, x_mine(m), r, far, near).wait_send()
        each(near, lambda s, m=m: x_push(m, x_mine(m), r, beside(s), s).wait_send())
        each(near, lambda s, m=m: x_push(m, x_far(m), far, beside(s), near + 1 + s).wait_send())
    for m in range(len(cuts)):
        f_push(m, fp_ref, blk, pair, ny - 1).wait_send()
        each(ny - 1, lambda s, m=m: f_push(m, fp_ref, blk, along(s), s).wait_send())


def lay_kernel(nr, og, vir, occ, in_ref, out_ref, op):
    count, wide = op.shape[0], in_ref.shape[2]
    for src in range(nr):
        for jj in range(og):
            for p in range(count):
                start = jj * vir + p * 128
                n = min(128, wide - start)
                v = in_ref[src, :, start : start + n]
                if n < 128:
                    v = jnp.concatenate([v, jnp.zeros((8, 128 - n), F32)], axis=1)
                op[p, pl.ds(src * og + jj, 8, stride=occ), :] = v
    for p in range(count):
        n = min(128, vir - p * 128)
        out_ref[:, p * 128 : p * 128 + n] = op[p, :, :n]


def shards(amplitudes, aux_left, aux_right, left_rotation, right_rotation, occ_energy, vir_energy):
    nr, nc = lax.axis_size("row"), lax.axis_size("col")
    occ, vir = occ_energy.shape[0], vir_energy.shape[0]
    naux = aux_left.shape[1]
    half = naux // 2
    og, va, vc = occ // nr, vir // nr, vir // nc
    piece = og * va
    rows = vc * og
    pad, wide_pad = up(rows, 8), up(rows, 16)
    dma = pltpu.SemaphoreType.DMA
    vmem = pl.BlockSpec(memory_space=pltpu.VMEM)
    hbm = pl.BlockSpec(memory_space=pl.ANY)
    limit = 60 * 1024 * 1024

    cols = og * vir
    first = up(half * 3 // 5, 128)
    zcuts = [(0, first), (first, half - first)] if first < half else [(0, half)]
    fp, zg, xz = pl.pallas_call(
        functools.partial(gather_kernel, nr, occ, zcuts),
        out_shape=[
            jax.ShapeDtypeStruct((piece, half), F32),
            jax.ShapeDtypeStruct((nr, piece, half), F32),
            jax.ShapeDtypeStruct((nr, 2 * pad, half), F32),
        ],
        in_specs=[vmem] * 4,
        out_specs=[vmem, vmem, hbm],
        scratch_shapes=[
            pltpu.VMEM((up(amplitudes.shape[1], 128) // 128, amplitudes.shape[0], 128), F32),
            pltpu.VMEM((up(naux, 128) // 128, aux_right.shape[0], 128), F32),
            pltpu.VMEM((aux_left.shape[0], naux), BF16),
            pltpu.VMEM((aux_left.shape[0], naux), BF16),
            pltpu.VMEM((nr, piece, half), F32),
            pltpu.VMEM((nr, piece, half), F32),
            pltpu.VMEM((nr, piece, half), F32),
            pltpu.VMEM((nr // 2, piece, half), F32),
            pltpu.VMEM((nr // 2, piece, half), F32),
            pltpu.VMEM((og, vc, half), F32),
            pltpu.VMEM((og, vc, half), F32),
            pltpu.VMEM((piece, half), F32),
            pltpu.VMEM((half // 128, 2 * pad, 128), F32),
            pltpu.VMEM((2 * pad, half), F32),
            dma((nr,)), dma((nr,)), dma((nr,)), dma((nr,)), dma((nr,)), dma((nr,)), dma, dma,
            dma((2, nr)), dma((2, nr)), dma((2, nr)), dma((2, nr)), dma,
        ],
        compiler_params=pltpu.CompilerParams(collective_id=0, has_side_effects=True, vmem_limit_bytes=limit),
        name="fit_gather",
    )(amplitudes, aux_left, aux_right, left_rotation)

    cols_pad = up(cols, 128)
    tiles = up(cols_pad, WIDE) // WIDE
    cuts = [(at, min(256, half - at)) for at in range(0, half, 256)]
    r, c = lax.axis_index("row"), lax.axis_index("col")
    vir_here = lax.dynamic_slice_in_dim(vir_energy, c * vc, vc)
    occ_here = lax.dynamic_slice_in_dim(occ_energy, r * og, og)
    rowd = (vir_here[None, :, None] - occ_energy.reshape(nr, 1, og)).reshape(nr, rows)
    rowd = jnp.pad(rowd, ((0, 0), (0, wide_pad - rows)), constant_values=1.0).reshape(nr * wide_pad, 1)
    rowd = jnp.broadcast_to(rowd, (nr * wide_pad, 128))
    cold = (vir_energy[None, :] - occ_here[:, None]).reshape(1, cols)
    cold = jnp.pad(cold, ((0, 0), (0, cols_pad - cols)), constant_values=1.0)
    cold = jnp.broadcast_to(cold, (8, cols_pad))

    moved = pl.pallas_call(
        functools.partial(tile_kernel, nr, og, vc, tiles, cuts),
        out_shape=jax.ShapeDtypeStruct((nr, pad, cols_pad), F32),
        in_specs=[vmem] * 7,
        out_specs=hbm,
        scratch_shapes=[
            pltpu.VMEM((nr, piece, half), F32),
            pltpu.VMEM((vir + va, vir), BF16),
            pltpu.VMEM((vir + va, vir), BF16),
            pltpu.VMEM((cols_pad, naux), BF16),
            pltpu.VMEM((cols_pad, naux), BF16),
            pltpu.VMEM((half // 128, 2 * pad, 128), F32),
            pltpu.VMEM((2 * pad, half), F32),
            pltpu.VMEM((nr, 2 * pad, half), F32),
            pltpu.VMEM((2, nr * wide_pad, naux), BF16),
            pltpu.VMEM((2, nr * wide_pad, naux), BF16),
            pltpu.VMEM((2, nr * wide_pad, WIDE), F32),
            pltpu.VMEM((tiles, nr * wide_pad, WIDE), F32),
            pltpu.VMEM((nr * wide_pad, cols_pad), F32),
            dma((len(cuts), nr)), dma((len(cuts), nr)),
            dma((len(cuts), nr)), dma((len(cuts), nr)), dma((2,)), dma((tiles,)),
            dma((tiles, nr)), dma((tiles, nr)), dma((tiles,)),
        ],
        compiler_params=pltpu.CompilerParams(collective_id=1, has_side_effects=True, vmem_limit_bytes=limit),
        name="tile_exchange",
    )(fp, zg, xz, left_rotation, right_rotation, rowd, cold)

    out = pl.pallas_call(
        functools.partial(lay_kernel, nr, og, vir, occ),
        grid=(pad // 8,),
        out_shape=jax.ShapeDtypeStruct((rows * occ, vir), F32),
        in_specs=[pl.BlockSpec((nr, 8, cols_pad), lambda g: (0, g, 0))],
        out_specs=pl.BlockSpec((8 * occ, vir), lambda g: (g, 0)),
        scratch_shapes=[pltpu.VMEM((up(vir, 128) // 128, 8 * occ, 128), F32)],
        compiler_params=pltpu.CompilerParams(vmem_limit_bytes=limit),
        name="lay_out",
    )(moved)
    return out.reshape(vc, og, occ, vir)


def solution(mesh):
    placed = (P("row", "col"), P("col", None), P("col", None), P(), P(), P(), P())
    return jax.shard_map(
        shards, mesh=mesh, in_specs=placed, out_specs=P("col", "row", None, None), check_vma=False
    )
```

```python
import functools

import jax
import jax.numpy as jnp
from jax import lax
from jax.experimental import pallas as pl
from jax.experimental.pallas import tpu as pltpu
from jax.sharding import PartitionSpec as P

MESH = pl.DeviceIdType.MESH
F32 = jnp.float32
BF16 = jnp.bfloat16
WIDE = 256


def halves(x):
    hi = x.astype(BF16)
    return hi, (x - hi.astype(F32)).astype(BF16)


def dot3(xh, xl, yh, yl, dims):
    def dot(a, b):
        return lax.dot_general(a, b, (dims, ((), ())), preferred_element_type=F32)

    return dot(xl, yh) + dot(xh, yl) + dot(xh, yh)


def up(n, unit):
    return -(-n // unit) * unit


def planes(src, dst):
    width, rows = src.shape[1], 40 if src.shape[0] % 40 == 0 else src.shape[0]

    def one(g, _):
        at = pl.ds(pl.multiple_of(g * rows, 8), rows)
        for p in range(dst.shape[0]):
            n = min(128, width - p * 128)
            dst[p, at, :n] = src[at, p * 128 : p * 128 + n]
        return 0

    lax.fori_loop(0, src.shape[0] // rows, one, 0)


def turned(src, dst):
    depth, width = src.shape
    for p in range(dst.shape[0]):
        n = min(128, depth - p * 128)

        def one(g, _, p=p, n=n):
            at = pl.ds(pl.multiple_of(g * 128, 128), 128)
            dst[p, at, :n] = src[p * 128 : p * 128 + n, at].T
            return 0

        lax.fori_loop(0, width // 128, one, 0)
        at = width // 128 * 128
        if at < width:
            dst[p, at:, :n] = src[p * 128 : p * 128 + n, at:].T


def every(src, start, count, stride, width):
    parts = [src[p, pl.ds(start, count, stride=stride), :] for p in range(src.shape[0])]
    return jnp.concatenate(parts, axis=1)[:, :width]


def gather_kernel(
    nr, occ, zcuts,
    t_ref, b_ref, z_ref, l_ref,
    fp_ref, zg_ref, xz_ref,
    tp, zp, bh, bl, sib_send, sib_recv, own, z_recv, rs_recv, fsum, zs_send, zs_recv, zc, xp, xo,
    sib_s, sib_r, zz_s, zz_r, rs_s, rs_r, hop_s, hop_r, zs_s, zs_r, za_s, za_r, xs, xr, loc,
):
    r, c = lax.axis_index("row"), lax.axis_index("col")
    t, k = c // 2, lax.rem(c, 2)
    sib = c + 1 - 2 * k
    og = occ // nr
    va = t_ref.shape[1] // occ
    vc = z_ref.shape[0] // occ
    half = b_ref.shape[1] // 2
    blk = lax.rem(t - r + nr, nr)
    is_own = lax.rem(r + r, nr) == t
    ny = nr // 2
    y, low = t // 2, lax.rem(t, 2)
    pair = t + 1 - 2 * low

    far = r + 1 - 2 * lax.rem(r, 2)
    vir = va * nr
    pad = xo.shape[0] // 2

    barrier = pltpu.get_barrier_semaphore()
    pl.semaphore_signal(barrier, inc=1, device_id=(r, sib), device_id_type=MESH)

    pl.semaphore_signal(barrier, inc=1, device_id=(r, 2 * pair + k), device_id_type=MESH)

    def along(s):
        return 2 * lax.rem(y + 1 + s, ny) + low

    def each(count, body):
        def one(s, _):
            body(s)
            return 0

        lax.fori_loop(0, count, one, 0)

    def beside(s):
        return lax.rem(r + 2 * (s + 1), nr)

    pl.semaphore_signal(barrier, inc=1, device_id=(far, c), device_id_type=MESH)

    def greet(s):
        pl.semaphore_signal(barrier, inc=1, device_id=(r, 2 * along(s) + k), device_id_type=MESH)
        pl.semaphore_signal(barrier, inc=1, device_id=(beside(s), c), device_id_type=MESH)

    each(ny - 1, greet)

    @pl.when(jnp.logical_not(is_own))
    def _():
        pl.semaphore_signal(barrier, inc=1, device_id=(blk, c), device_id_type=MESH)

    planes(z_ref, zp)
    first = k == 0
    kept = []
    for jj in range(og):
        z = every(zp, r * og + jj, vc, occ, z_ref.shape[1])
        z0, z1 = z[:, :half], z[:, half:]
        zs_send[jj] = jnp.where(first, z1, z0)
        kept.append(jnp.where(first, z0, z1))
        zc[jj * va : jj * va + vc, :] = kept[-1]

    @pl.when(is_own)
    def _():
        pl.semaphore_wait(barrier, nr + 1)

    @pl.when(jnp.logical_not(is_own))
    def _():
        pl.semaphore_wait(barrier, nr + 2)

    z_swap = pltpu.make_async_remote_copy(
        src_ref=zs_send, dst_ref=zs_recv, send_sem=zs_s, recv_sem=zs_r,
        device_id=(r, sib), device_id_type=MESH,
    )
    z_swap.start()
    mine, other = pl.ds(pl.multiple_of(k * half, half), half), pl.ds(pl.multiple_of((1 - k) * half, half), half)
    for at, cols in ((0, other), (half, mine)):
        hi, lo = halves(b_ref[:, cols])
        bh[:, at : at + half] = hi
        bl[:, at : at + half] = lo

    z_swap.wait()
    for jj in range(og):
        z_mine = zc[jj * va : jj * va + vc, :]
        z_sib = zs_recv[jj]
        zc[jj * va : (jj + 1) * va, :] = jnp.concatenate(
            [jnp.where(first, z_mine, z_sib), jnp.where(first, z_sib, z_mine)], axis=0
        )

    def z_push(m, src_ref, slot, peer, sem):
        lanes = pl.ds(*zcuts[m])
        return pltpu.make_async_remote_copy(
            src_ref=src_ref.at[:, lanes], dst_ref=zg_ref.at[slot, :, lanes],
            send_sem=za_s.at[m, sem], recv_sem=za_r.at[m, slot],
            device_id=(r, 2 * peer + k), device_id_type=MESH,
        )

    def z_start(m):
        z_push(m, zc, t, pair, ny - 1).start()
        each(ny - 1, lambda s: z_push(m, zc, t, along(s), s).start())

    def z_forward(m):
        z_push(m, zc, pair, pair, ny - 1).wait_recv()
        each(ny - 1, lambda s: z_push(m, zg_ref.at[pair], pair, along(s), ny + s).start())

    def z_forwarded(m):
        each(ny - 1, lambda s: z_push(m, zg_ref.at[pair], pair, along(s), ny + s).wait_send())

    z_start(0)
    zg_ref[t] = zc[...]
    turned(t_ref, tp)

    def to_sibling(s):
        return pltpu.make_async_remote_copy(
            src_ref=sib_send.at[s], dst_ref=sib_recv.at[s], send_sem=sib_s.at[s], recv_sem=sib_r.at[s],
            device_id=(r, sib), device_id_type=MESH,
        )

    def owner(s):
        stays = s // ny
        side = stays * low + (1 - stays) * (1 - low)
        return 2 * lax.rem(y + 1 + lax.rem(s, ny), ny) + side

    def to_pair(s):
        return pltpu.make_async_remote_copy(
            src_ref=own.at[s], dst_ref=z_recv.at[s], send_sem=zz_s.at[s], recv_sem=zz_r.at[s],
            device_id=(r, 2 * pair + k), device_id_type=MESH,
        )

    def to_owner(s):
        ot = owner(ny + s)
        return pltpu.make_async_remote_copy(
            src_ref=own.at[ny + s], dst_ref=rs_recv.at[y], send_sem=rs_s.at[s], recv_sem=rs_r.at[y],
            device_id=(r, 2 * ot + k), device_id_type=MESH,
        )

    def finish(s):
        to_sibling(s).wait_recv()
        own[s] = own[s] + sib_recv[s]

        @pl.when(s == 0)
        def _():
            to_pair(0).start()

        @pl.when(s == ny + 1)
        def _():
            to_pair(1).start()

    def step(s):
        dst = lax.rem(owner(s) - r + nr, nr)
        x = jnp.concatenate(
            [every(tp, dst * og + ii, va, occ, t_ref.shape[0]) for ii in range(og)], axis=0
        )
        xh, xl = halves(x)
        part = dot3(xh, xl, bh[...], bl[...], ((1,), (0,)))
        sib_send[s] = part[:, :half]
        own[s] = part[:, half:]
        to_sibling(s).start()

        @pl.when(s > 0)
        def _():
            finish(s - 1)

        @pl.when(s == ny)
        def _():
            z_forward(0)

    def deliver(s):
        to_pair(s).wait_recv()
        own[ny + s] = own[ny + s] + z_recv[s]
        if s < ny - 1:
            to_owner(s).start()
        else:
            rs_recv[y] = own[ny + s]

    def x_push(m, src_ref, slot, dst, sem):
        lanes = pl.ds(*zcuts[m])
        return pltpu.make_async_remote_copy(
            src_ref=src_ref.at[:, lanes], dst_ref=xz_ref.at[slot, :, lanes],
            send_sem=xs.at[m, sem], recv_sem=xr.at[m, slot],
            device_id=(dst, c), device_id_type=MESH,
        )

    def x_forward(m):
        x_push(m, xo, far, far, ny - 1).wait_recv()
        each(ny - 1, lambda s: x_push(m, xz_ref.at[far], far, beside(s), ny + s).start())

    lh, ll = halves(l_ref[pl.ds(pl.multiple_of(t * va, 8), va), :])
    xp[...] = jnp.zeros_like(xp)

    def z_rows(m):
        def z_rest(s):
            z_push(m, zc, along(s), along(s), s).wait_recv()
            z_push(m, zc, along(s) + pair - t, pair, s).wait_recv()

        each(ny - 1, z_rest)
        at, width = zcuts[m]
        for ii in range(og):
            gh, gl = halves(zg_ref[:, ii * va : (ii + 1) * va, at : at + width].reshape(vir, width))
            x = dot3(lh, ll, gh, gl, ((1,), (0,)))
            for par in range(2):
                for p in range(width // 128):
                    xp[p, pl.ds(par * pad + ii, vc, stride=og), :] = x[
                        par * vc : (par + 1) * vc, p * 128 : (p + 1) * 128
                    ]
        for p in range(width // 128):
            xo[:, at + p * 128 : at + (p + 1) * 128] = xp[p]
        x_push(m, xo, r, far, ny - 1).start()
        each(ny - 1, lambda s: x_push(m, xo, r, beside(s), s).start())

    two = len(zcuts) > 1
    each(nr, step)
    finish(nr - 1)
    deliver(0)
    z_forwarded(0)
    if two:
        z_start(1)
    to_pair(1).wait_send()
    if ny > 2:
        to_pair(2).start()
    deliver(1)
    if two:
        z_forward(1)
    z_rows(0)
    for s in range(2, ny):
        to_pair(s).wait_send()
        if s + 1 < ny:
            to_pair(s + 1).start()
        deliver(s)
        if s == 2:
            x_forward(0)
            if two:
                z_rows(1)
    if ny < 3:
        x_forward(0)
        if two:
            z_rows(1)
    if two:
        x_forward(1)
    x_own = pltpu.make_async_copy(xo, xz_ref.at[r], loc)
    x_own.start()

    def arrived(s):
        pltpu.make_async_remote_copy(
            src_ref=own.at[0], dst_ref=rs_recv.at[lax.rem(y + 1 + s, ny)], send_sem=rs_s.at[0],
            recv_sem=rs_r.at[lax.rem(y + 1 + s, ny)],
            device_id=(r, sib), device_id_type=MESH,
        ).wait_recv()

    each(ny - 1, arrived)

    def add_up(g):
        rows = pl.ds(pl.multiple_of(g * 8, 8), 8)
        total = rs_recv[0, rows, :]
        for s in range(1, ny):
            total = total + rs_recv[s, rows, :]
        fsum[rows, :] = total

    each(fsum.shape[0] // 8, add_up)
    hop = pltpu.make_async_remote_copy(
        src_ref=fsum, dst_ref=fp_ref, send_sem=hop_s, recv_sem=hop_r,
        device_id=(blk, c), device_id_type=MESH,
    )

    @pl.when(is_own)
    def _():
        fp_ref[...] = fsum[...]

    @pl.when(jnp.logical_not(is_own))
    def _():
        hop.start()

    for m in range(len(zcuts)):
        z_push(m, zc, t, pair, ny - 1).wait_send()
        x_push(m, xo, r, far, ny - 1).wait_send()

        def settle(s, m=m):
            z_push(m, zc, t, along(s), s).wait_send()
            x_push(m, xo, r, beside(s), s).wait_send()
            x_push(m, xz_ref.at[far], far, beside(s), ny + s).wait_send()
            x_push(m, xo, beside(s), far, s).wait_recv()
            x_push(m, xo, lax.rem(far + 2 * (s + 1), nr), far, s).wait_recv()

        each(ny - 1, settle)
    if two:
        z_forwarded(1)
    each(nr, lambda s: to_sibling(s).wait_send())

    each(ny - 1, lambda s: to_owner(s).wait_send())

    @pl.when(jnp.logical_not(is_own))
    def _():
        hop.wait()

    to_pair(0).wait_send()
    x_own.wait()


def tile_kernel(
    nr, og, vc, tiles, cuts,
    fp_ref, zg_ref, xz_ref, l_ref, r_ref, rowd_ref, cold_ref,
    out_ref,
    fg, rh, rl, yh, yl, xp, xo, xg, xh, xl, s_send, s_recv, own,
    fs, fr, xs, xr, ss, sr, os_, or_, loc,
):
    r, c = lax.axis_index("row"), lax.axis_index("col")
    t, k = c // 2, lax.rem(c, 2)
    sib = c + 1 - 2 * k
    half = fp_ref.shape[1]
    vir = r_ref.shape[0]
    va = vir // nr
    pad = xo.shape[0] // 2
    wide_pad = xh.shape[1] // nr
    blk = lax.rem(t - r + nr, nr)
    far = r + 1 - 2 * lax.rem(r, 2)
    near = nr // 2 - 1

    barrier = pltpu.get_barrier_semaphore()
    pl.semaphore_signal(barrier, inc=1, device_id=(r, sib), device_id_type=MESH)

    def greet(s, _):
        pl.semaphore_signal(barrier, inc=1, device_id=(lax.rem(r + 1 + s, nr), c), device_id_type=MESH)
        pl.semaphore_signal(
            barrier, inc=1, device_id=(r, 2 * lax.rem(t + 1 + s, nr) + k), device_id_type=MESH
        )
        return 0

    lax.fori_loop(0, nr - 1, greet, 0)

    hi, lo = halves(r_ref[...])
    rh[:vir, :] = hi
    rl[:vir, :] = lo
    hi, lo = halves(l_ref[pl.ds(pl.multiple_of(t * va, 8), va), :])
    rh[vir:, :] = hi
    rl[vir:, :] = lo
    xp[...] = jnp.zeros_like(xp)
    fg[blk] = fp_ref[...]
    pl.semaphore_wait(barrier, 2 * nr - 1)

    ny = nr // 2
    y, low = t // 2, lax.rem(t, 2)
    pair = t + 1 - 2 * low

    def along(s):
        return 2 * lax.rem(y + 1 + s, ny) + low

    def slot_of(other):
        return lax.rem(other - r + nr, nr)

    def f_push(m, src_ref, slot, peer, sem):
        at, width = cuts[m]
        cols = pl.ds(at, width)
        return pltpu.make_async_remote_copy(
            src_ref=src_ref.at[:, cols], dst_ref=fg.at[slot, :, cols],
            send_sem=fs.at[m, sem], recv_sem=fr.at[m, slot],
            device_id=(r, 2 * peer + k), device_id_type=MESH,
        )

    def each(count, body):
        def one(s, _):
            body(s)
            return 0

        lax.fori_loop(0, count, one, 0)

    def f_start(m):
        f_push(m, fp_ref, blk, pair, ny - 1).start()
        each(ny - 1, lambda s: f_push(m, fp_ref, blk, along(s), s).start())

    def f_forward(m):
        f_push(m, fp_ref, slot_of(pair), pair, ny - 1).wait_recv()
        each(
            ny - 1,
            lambda s: f_push(m, fg.at[slot_of(pair)], slot_of(pair), along(s), ny + s).start(),
        )

    def f_rest(m):
        def one(s):
            f_push(m, fp_ref, slot_of(along(s)), pair, ny - 1).wait_recv()
            f_push(m, fp_ref, slot_of(along(s) + pair - t), pair, ny - 1).wait_recv()

        each(ny - 1, one)

    last = len(cuts) - 1
    f_start(0)

    def f_forwarded(m):
        each(ny - 1, lambda s: f_push(m, fp_ref, blk, along(s), ny + s).wait_send())

    def x_push(m, src_ref, slot, dst, sem):
        return pltpu.make_async_remote_copy(
            src_ref=src_ref, dst_ref=xg.at[slot, :, pl.ds(*cuts[m])],
            send_sem=xs.at[m, sem], recv_sem=xr.at[m, slot],
            device_id=(dst, c), device_id_type=MESH,
        )

    def x_mine(m):
        return xo.at[:, pl.ds(*cuts[m])]

    def x_far(m):
        return xg.at[far, :, pl.ds(*cuts[m])]

    def beside(s):
        return lax.rem(r + 2 * (s + 1), nr)

    def x_start(m):
        x_push(m, x_mine(m), r, far, near).start()
        each(near, lambda s: x_push(m, x_mine(m), r, beside(s), s).start())

    def x_arrive(m, slot):
        x_push(m, x_mine(m), slot, far, near).wait_recv()

    def x_forward(m):
        x_arrive(m, far)
        each(near, lambda s: x_push(m, x_far(m), far, beside(s), near + 1 + s).start())

    def rotate(g_ref, fitted, at, width):
        y_at = half * fitted + at
        count = vir + va * fitted
        for ii in range(og):
            gh, gl = halves(g_ref[:, ii * va : (ii + 1) * va, at : at + width].reshape(vir, width))
            both = dot3(rh[:count], rl[:count], gh, gl, ((1,), (0,)))
            hi, lo = halves(both[:vir])
            yh[ii * vir : (ii + 1) * vir, y_at : y_at + width] = hi
            yl[ii * vir : (ii + 1) * vir, y_at : y_at + width] = lo
            if fitted:
                for par in range(2):
                    rows = both[vir + par * vc : vir + (par + 1) * vc]
                    for p in range(width // 128):
                        xp[p, pl.ds(par * pad + ii, vc, stride=og), :] = rows[:, p * 128 : (p + 1) * 128]
        if fitted:
            for p in range(width // 128):
                xo[:, at + p * 128 : at + (p + 1) * 128] = xp[p]

    def take(src, load, x_at, width):
        rows = pl.ds(pl.multiple_of(src * wide_pad, 16), pad)
        for par in range(2):
            hi, lo = halves(load(par * pad))
            xh[par, rows, x_at : x_at + width] = hi
            xl[par, rows, x_at : x_at + width] = lo

    def take_own(m):
        at, width = cuts[m]
        take(r, lambda row: xo[row : row + pad, at : at + width], at, width)

    def take_from(m, src):
        at, width = cuts[m]
        take(src, lambda row: xg[src, row : row + pad, at : at + width], at, width)

    def take_near(m, base):
        def one(s):
            src = lax.rem(base + 2 * (s + 1), nr)
            x_arrive(m, src)
            take_from(m, src)

        each(near, one)

    each(nr, lambda src: take(src, lambda row: xz_ref[src, row : row + pad, :], half, half))
    f_forward(0)
    rotate(zg_ref, 0, 0, half)
    for m, (at, width) in enumerate(cuts):
        f_forwarded(m)
        if m < last:
            f_start(m + 1)
        f_rest(m)
        rotate(fg, 1, at, width)
        x_start(m)
        if m < last:
            f_forward(m + 1)
        if m:
            x_forward(m - 1)
    x_forward(last)
    for m in range(len(cuts)):
        take_own(m)
        take_from(m, far)
        take_near(m, r)
        take_near(m, far)

    def to_sibling(n, width):
        return pltpu.make_async_remote_copy(
            src_ref=s_send.at[lax.rem(n, 2), :, pl.ds(0, width)], dst_ref=s_recv.at[n, :, pl.ds(0, width)],
            send_sem=ss.at[lax.rem(n, 2)], recv_sem=sr.at[n],
            device_id=(r, sib), device_id_type=MESH,
        )

    def to_row(n, width, s, src):
        dst = lax.rem(r + 1 + s, nr)
        cols = pl.ds(pl.multiple_of(n * WIDE, 128), width)
        return pltpu.make_async_remote_copy(
            src_ref=own.at[pl.ds(pl.multiple_of(dst * wide_pad, 8), pad), cols],
            dst_ref=out_ref.at[src, :, cols],
            send_sem=os_.at[n, s], recv_sem=or_.at[n, src],
            device_id=(dst, c), device_id_type=MESH,
        )

    def stay(n, width):
        cols = pl.ds(pl.multiple_of(n * WIDE, 128), width)
        return pltpu.make_async_copy(
            own.at[pl.ds(pl.multiple_of(r * wide_pad, 8), pad), cols], out_ref.at[r, :, cols], loc.at[n]
        )

    def tile(n, width, slot_used):
        rows = pl.ds(pl.multiple_of(n * WIDE, 128), width)
        wh, wl = yh[rows, :], yl[rows, :]

        def product(par):
            return dot3(xh[par], xl[par], wh, wl, ((1,), (1,)))

        @pl.when(slot_used)
        def _():
            to_sibling(n - 2, WIDE).wait_send()

        s_send[lax.rem(n, 2), :, 0:width] = product(1 - k)
        to_sibling(n, width).start()
        own[:, rows] = product(k)
        to_sibling(n, width).wait_recv()
        reps = width // 128

        def close(g, _):
            at = pl.ds(pl.multiple_of(g * wide_pad, 8), wide_pad)
            rowd = rowd_ref[at, :]
            for m in range(reps):
                cols = pl.ds(pl.multiple_of(n * WIDE + m * 128, 128), 128)
                here = own[at, cols] + s_recv[n, at, m * 128 : (m + 1) * 128]
                own[at, cols] = here / (rowd + cold_ref[0:1, cols])
            return 0

        lax.fori_loop(0, nr, close, 0)

        def send(s, _):
            to_row(n, width, s, r).start()
            return 0

        lax.fori_loop(0, nr - 1, send, 0)
        stay(n, width).start()

    tail = yh.shape[0] - (tiles - 1) * WIDE

    def full(n, _):
        tile(n, WIDE, n > 1)
        return 0

    lax.fori_loop(0, tiles - 1, full, 0)
    tile(jnp.int32(tiles - 1), tail, tiles > 2)

    def settle(n, width):
        def one(s, _):
            src = lax.rem(r + 1 + s, nr)
            to_row(n, width, s, src).wait()
            return 0

        lax.fori_loop(0, nr - 1, one, 0)
        stay(n, width).wait()

    def settle_full(n, _):
        settle(n, WIDE)
        return 0

    lax.fori_loop(0, tiles - 1, settle_full, 0)
    settle(jnp.int32(tiles - 1), tail)
    to_sibling(jnp.int32(tiles - 2), WIDE).wait_send()
    to_sibling(jnp.int32(tiles - 1), tail).wait_send()
    for m in range(len(cuts)):
        x_push(m, x_mine(m), r, far, near).wait_send()
        each(near, lambda s, m=m: x_push(m, x_mine(m), r, beside(s), s).wait_send())
        each(near, lambda s, m=m: x_push(m, x_far(m), far, beside(s), near + 1 + s).wait_send())
    for m in range(len(cuts)):
        f_push(m, fp_ref, blk, pair, ny - 1).wait_send()
        each(ny - 1, lambda s, m=m: f_push(m, fp_ref, blk, along(s), s).wait_send())


def lay_kernel(nr, og, vir, occ, in_ref, out_ref, op):
    count, wide = op.shape[0], in_ref.shape[2]
    for src in range(nr):
        for jj in range(og):
            for p in range(count):
                start = jj * vir + p * 128
                n = min(128, wide - start)
                v = in_ref[src, :, start : start + n]
                if n < 128:
                    v = jnp.concatenate([v, jnp.zeros((8, 128 - n), F32)], axis=1)
                op[p, pl.ds(src * og + jj, 8, stride=occ), :] = v
    for p in range(count):
        n = min(128, vir - p * 128)
        out_ref[:, p * 128 : p * 128 + n] = op[p, :, :n]


def shards(amplitudes, aux_left, aux_right, left_rotation, right_rotation, occ_energy, vir_energy):
    nr, nc = lax.axis_size("row"), lax.axis_size("col")
    occ, vir = occ_energy.shape[0], vir_energy.shape[0]
    naux = aux_left.shape[1]
    half = naux // 2
    og, va, vc = occ // nr, vir // nr, vir // nc
    piece = og * va
    rows = vc * og
    pad, wide_pad = up(rows, 8), up(rows, 16)
    dma = pltpu.SemaphoreType.DMA
    vmem = pl.BlockSpec(memory_space=pltpu.VMEM)
    hbm = pl.BlockSpec(memory_space=pl.ANY)
    limit = 60 * 1024 * 1024

    cols = og * vir
    first = up(half * 3 // 5, 128)
    zcuts = [(0, first), (first, half - first)] if first < half else [(0, half)]
    fp, zg, xz = pl.pallas_call(
        functools.partial(gather_kernel, nr, occ, zcuts),
        out_shape=[
            jax.ShapeDtypeStruct((piece, half), F32),
            jax.ShapeDtypeStruct((nr, piece, half), F32),
            jax.ShapeDtypeStruct((nr, 2 * pad, half), F32),
        ],
        in_specs=[vmem] * 4,
        out_specs=[vmem, vmem, hbm],
        scratch_shapes=[
            pltpu.VMEM((up(amplitudes.shape[1], 128) // 128, amplitudes.shape[0], 128), F32),
            pltpu.VMEM((up(naux, 128) // 128, aux_right.shape[0], 128), F32),
            pltpu.VMEM((aux_left.shape[0], naux), BF16),
            pltpu.VMEM((aux_left.shape[0], naux), BF16),
            pltpu.VMEM((nr, piece, half), F32),
            pltpu.VMEM((nr, piece, half), F32),
            pltpu.VMEM((nr, piece, half), F32),
            pltpu.VMEM((nr // 2, piece, half), F32),
            pltpu.VMEM((nr // 2, piece, half), F32),
            pltpu.VMEM((piece, half), F32),
            pltpu.VMEM((og, vc, half), F32),
            pltpu.VMEM((og, vc, half), F32),
            pltpu.VMEM((piece, half), F32),
            pltpu.VMEM((half // 128, 2 * pad, 128), F32),
            pltpu.VMEM((2 * pad, half), F32),
            dma((nr,)), dma((nr,)), dma((nr,)), dma((nr,)), dma((nr,)), dma((nr,)), dma, dma, dma, dma,
            dma((2, nr)), dma((2, nr)), dma((2, nr)), dma((2, nr)), dma,
        ],
        compiler_params=pltpu.CompilerParams(collective_id=0, has_side_effects=True, vmem_limit_bytes=limit),
        name="fit_gather",
    )(amplitudes.T, aux_left, aux_right, left_rotation)

    cols_pad = up(cols, 128)
    tiles = up(cols_pad, WIDE) // WIDE
    cuts = [(at, min(256, half - at)) for at in range(0, half, 256)]
    r, c = lax.axis_index("row"), lax.axis_index("col")
    vir_here = lax.dynamic_slice_in_dim(vir_energy, c * vc, vc)
    occ_here = lax.dynamic_slice_in_dim(occ_energy, r * og, og)
    rowd = (vir_here[None, :, None] - occ_energy.reshape(nr, 1, og)).reshape(nr, rows)
    rowd = jnp.pad(rowd, ((0, 0), (0, wide_pad - rows)), constant_values=1.0).reshape(nr * wide_pad, 1)
    rowd = jnp.broadcast_to(rowd, (nr * wide_pad, 128))
    cold = (vir_energy[None, :] - occ_here[:, None]).reshape(1, cols)
    cold = jnp.pad(cold, ((0, 0), (0, cols_pad - cols)), constant_values=1.0)
    cold = jnp.broadcast_to(cold, (8, cols_pad))

    moved = pl.pallas_call(
        functools.partial(tile_kernel, nr, og, vc, tiles, cuts),
        out_shape=jax.ShapeDtypeStruct((nr, pad, cols_pad), F32),
        in_specs=[vmem] * 7,
        out_specs=hbm,
        scratch_shapes=[
            pltpu.VMEM((nr, piece, half), F32),
            pltpu.VMEM((vir + va, vir), BF16),
            pltpu.VMEM((vir + va, vir), BF16),
            pltpu.VMEM((cols_pad, naux), BF16),
            pltpu.VMEM((cols_pad, naux), BF16),
            pltpu.VMEM((half // 128, 2 * pad, 128), F32),
            pltpu.VMEM((2 * pad, half), F32),
            pltpu.VMEM((nr, 2 * pad, half), F32),
            pltpu.VMEM((2, nr * wide_pad, naux), BF16),
            pltpu.VMEM((2, nr * wide_pad, naux), BF16),
            pltpu.VMEM((2, nr * wide_pad, WIDE), F32),
            pltpu.VMEM((tiles, nr * wide_pad, WIDE), F32),
            pltpu.VMEM((nr * wide_pad, cols_pad), F32),
            dma((len(cuts), nr)), dma((len(cuts), nr)),
            dma((len(cuts), nr)), dma((len(cuts), nr)), dma((2,)), dma((tiles,)),
            dma((tiles, nr)), dma((tiles, nr)), dma((tiles,)),
        ],
        compiler_params=pltpu.CompilerParams(collective_id=1, has_side_effects=True, vmem_limit_bytes=limit),
        name="tile_exchange",
    )(fp, zg, xz, left_rotation, right_rotation, rowd, cold)

    out = pl.pallas_call(
        functools.partial(lay_kernel, nr, og, vir, occ),
        grid=(pad // 8,),
        out_shape=jax.ShapeDtypeStruct((rows * occ, vir), F32),
        in_specs=[pl.BlockSpec((nr, 8, cols_pad), lambda g: (0, g, 0))],
        out_specs=pl.BlockSpec((8 * occ, vir), lambda g: (g, 0)),
        scratch_shapes=[pltpu.VMEM((up(vir, 128) // 128, 8 * occ, 128), F32)],
        compiler_params=pltpu.CompilerParams(vmem_limit_bytes=limit),
        name="lay_out",
    )(moved)
    return out.reshape(vc, og, occ, vir)


def solution(mesh):
    placed = (P("row", "col"), P("col", None), P("col", None), P(), P(), P(), P())
    return jax.shard_map(
        shards, mesh=mesh, in_specs=placed, out_specs=P("col", "row", None, None), check_vma=False
    )
```

```python
import functools

import jax
import jax.numpy as jnp
from jax import lax
from jax.experimental import pallas as pl
from jax.experimental.pallas import tpu as pltpu
from jax.sharding import PartitionSpec as P

MESH = pl.DeviceIdType.MESH
F32 = jnp.float32
BF16 = jnp.bfloat16
WIDE = 256


def halves(x):
    hi = x.astype(BF16)
    return hi, (x - hi.astype(F32)).astype(BF16)


def dot3(xh, xl, yh, yl, dims):
    def dot(a, b):
        return lax.dot_general(a, b, (dims, ((), ())), preferred_element_type=F32)

    return dot(xl, yh) + dot(xh, yl) + dot(xh, yh)


def up(n, unit):
    return -(-n // unit) * unit


def planes(src, dst):
    width, rows = src.shape[1], 40 if src.shape[0] % 40 == 0 else src.shape[0]

    def one(g, _):
        at = pl.ds(pl.multiple_of(g * rows, 8), rows)
        for p in range(dst.shape[0]):
            n = min(128, width - p * 128)
            dst[p, at, :n] = src[at, p * 128 : p * 128 + n]
        return 0

    lax.fori_loop(0, src.shape[0] // rows, one, 0)


def turned(src, dst):
    depth, width = src.shape
    for p in range(dst.shape[0]):
        n = min(128, depth - p * 128)

        def one(g, _, p=p, n=n):
            at = pl.ds(pl.multiple_of(g * 128, 128), 128)
            dst[p, at, :n] = src[p * 128 : p * 128 + n, at].T
            return 0

        lax.fori_loop(0, width // 128, one, 0)
        at = width // 128 * 128
        if at < width:
            dst[p, at:, :n] = src[p * 128 : p * 128 + n, at:].T


def every(src, start, count, stride, width):
    parts = [src[p, pl.ds(start, count, stride=stride), :] for p in range(src.shape[0])]
    return jnp.concatenate(parts, axis=1)[:, :width]


def gather_kernel(
    nr, occ, zcuts,
    t_hbm, b_hbm, z_ref, l_ref,
    fp_ref, zg_ref, xz_ref,
    t_ref, b_ref, tp, zp, bh, bl, sib_send, sib_recv, own, z_recv, rs_recv, fsum, zs_send, zs_recv, zc, xp, xo,
    sib_s, sib_r, zz_s, zz_r, rs_s, rs_r, hop_s, hop_r, zs_s, zs_r, za_s, za_r, xs, xr, loc, load,
):
    b_load = pltpu.make_async_copy(b_hbm, b_ref, load.at[0])
    t_load = pltpu.make_async_copy(t_hbm, t_ref, load.at[1])
    b_load.start()
    t_load.start()
    r, c = lax.axis_index("row"), lax.axis_index("col")
    t, k = c // 2, lax.rem(c, 2)
    sib = c + 1 - 2 * k
    og = occ // nr
    va = t_ref.shape[1] // occ
    vc = z_ref.shape[0] // occ
    half = b_ref.shape[1] // 2
    blk = lax.rem(t - r + nr, nr)
    is_own = lax.rem(r + r, nr) == t
    ny = nr // 2
    y, low = t // 2, lax.rem(t, 2)
    pair = t + 1 - 2 * low

    far = r + 1 - 2 * lax.rem(r, 2)
    vir = va * nr
    pad = xo.shape[0] // 2

    barrier = pltpu.get_barrier_semaphore()
    pl.semaphore_signal(barrier, inc=1, device_id=(r, sib), device_id_type=MESH)

    pl.semaphore_signal(barrier, inc=1, device_id=(r, 2 * pair + k), device_id_type=MESH)

    def along(s):
        return 2 * lax.rem(y + 1 + s, ny) + low

    def each(count, body):
        def one(s, _):
            body(s)
            return 0

        lax.fori_loop(0, count, one, 0)

    def beside(s):
        return lax.rem(r + 2 * (s + 1), nr)

    pl.semaphore_signal(barrier, inc=1, device_id=(far, c), device_id_type=MESH)

    def greet(s):
        pl.semaphore_signal(barrier, inc=1, device_id=(r, 2 * along(s) + k), device_id_type=MESH)
        pl.semaphore_signal(barrier, inc=1, device_id=(beside(s), c), device_id_type=MESH)

    each(ny - 1, greet)

    @pl.when(jnp.logical_not(is_own))
    def _():
        pl.semaphore_signal(barrier, inc=1, device_id=(blk, c), device_id_type=MESH)

    planes(z_ref, zp)
    first = k == 0
    kept = []
    for jj in range(og):
        z = every(zp, r * og + jj, vc, occ, z_ref.shape[1])
        z0, z1 = z[:, :half], z[:, half:]
        zs_send[jj] = jnp.where(first, z1, z0)
        kept.append(jnp.where(first, z0, z1))
        zc[jj * va : jj * va + vc, :] = kept[-1]

    @pl.when(is_own)
    def _():
        pl.semaphore_wait(barrier, nr + 1)

    @pl.when(jnp.logical_not(is_own))
    def _():
        pl.semaphore_wait(barrier, nr + 2)

    z_swap = pltpu.make_async_remote_copy(
        src_ref=zs_send, dst_ref=zs_recv, send_sem=zs_s, recv_sem=zs_r,
        device_id=(r, sib), device_id_type=MESH,
    )
    z_swap.start()
    b_load.wait()
    mine, other = pl.ds(pl.multiple_of(k * half, half), half), pl.ds(pl.multiple_of((1 - k) * half, half), half)
    for at, cols in ((0, other), (half, mine)):
        hi, lo = halves(b_ref[:, cols])
        bh[:, at : at + half] = hi
        bl[:, at : at + half] = lo

    z_swap.wait()
    for jj in range(og):
        z_mine = zc[jj * va : jj * va + vc, :]
        z_sib = zs_recv[jj]
        zc[jj * va : (jj + 1) * va, :] = jnp.concatenate(
            [jnp.where(first, z_mine, z_sib), jnp.where(first, z_sib, z_mine)], axis=0
        )

    def z_push(m, src_ref, slot, peer, sem):
        lanes = pl.ds(*zcuts[m])
        return pltpu.make_async_remote_copy(
            src_ref=src_ref.at[:, lanes], dst_ref=zg_ref.at[slot, :, lanes],
            send_sem=za_s.at[m, sem], recv_sem=za_r.at[m, slot],
            device_id=(r, 2 * peer + k), device_id_type=MESH,
        )

    def z_start(m):
        z_push(m, zc, t, pair, ny - 1).start()
        each(ny - 1, lambda s: z_push(m, zc, t, along(s), s).start())

    def z_forward(m):
        z_push(m, zc, pair, pair, ny - 1).wait_recv()
        each(ny - 1, lambda s: z_push(m, zg_ref.at[pair], pair, along(s), ny + s).start())

    def z_forwarded(m):
        each(ny - 1, lambda s: z_push(m, zg_ref.at[pair], pair, along(s), ny + s).wait_send())

    z_start(0)
    zg_ref[t] = zc[...]
    t_load.wait()
    turned(t_ref, tp)

    def to_sibling(s):
        return pltpu.make_async_remote_copy(
            src_ref=sib_send.at[s], dst_ref=sib_recv.at[s], send_sem=sib_s.at[s], recv_sem=sib_r.at[s],
            device_id=(r, sib), device_id_type=MESH,
        )

    def owner(s):
        stays = s // ny
        side = stays * low + (1 - stays) * (1 - low)
        return 2 * lax.rem(y + 1 + lax.rem(s, ny), ny) + side

    def to_pair(s):
        return pltpu.make_async_remote_copy(
            src_ref=own.at[s], dst_ref=z_recv.at[s], send_sem=zz_s.at[s], recv_sem=zz_r.at[s],
            device_id=(r, 2 * pair + k), device_id_type=MESH,
        )

    def to_owner(s):
        ot = owner(ny + s)
        return pltpu.make_async_remote_copy(
            src_ref=own.at[ny + s], dst_ref=rs_recv.at[y], send_sem=rs_s.at[s], recv_sem=rs_r.at[y],
            device_id=(r, 2 * ot + k), device_id_type=MESH,
        )

    def finish(s):
        to_sibling(s).wait_recv()
        own[s] = own[s] + sib_recv[s]

        @pl.when(s == 0)
        def _():
            to_pair(0).start()

        @pl.when(s == ny + 1)
        def _():
            to_pair(1).start()

    def step(s):
        dst = lax.rem(owner(s) - r + nr, nr)
        x = jnp.concatenate(
            [every(tp, dst * og + ii, va, occ, t_ref.shape[0]) for ii in range(og)], axis=0
        )
        xh, xl = halves(x)
        part = dot3(xh, xl, bh[...], bl[...], ((1,), (0,)))
        sib_send[s] = part[:, :half]
        own[s] = part[:, half:]
        to_sibling(s).start()

        @pl.when(s > 0)
        def _():
            finish(s - 1)

        @pl.when(s == ny)
        def _():
            z_forward(0)

    def deliver(s):
        to_pair(s).wait_recv()
        own[ny + s] = own[ny + s] + z_recv[s]
        if s < ny - 1:
            to_owner(s).start()
        else:
            rs_recv[y] = own[ny + s]

    def x_push(m, src_ref, slot, dst, sem):
        lanes = pl.ds(*zcuts[m])
        return pltpu.make_async_remote_copy(
            src_ref=src_ref.at[:, lanes], dst_ref=xz_ref.at[slot, :, lanes],
            send_sem=xs.at[m, sem], recv_sem=xr.at[m, slot],
            device_id=(dst, c), device_id_type=MESH,
        )

    def x_forward(m):
        x_push(m, xo, far, far, ny - 1).wait_recv()
        each(ny - 1, lambda s: x_push(m, xz_ref.at[far], far, beside(s), ny + s).start())

    lh, ll = halves(l_ref[pl.ds(pl.multiple_of(t * va, 8), va), :])
    xp[...] = jnp.zeros_like(xp)

    def z_rows(m):
        def z_rest(s):
            z_push(m, zc, along(s), along(s), s).wait_recv()
            z_push(m, zc, along(s) + pair - t, pair, s).wait_recv()

        each(ny - 1, z_rest)
        at, width = zcuts[m]
        for ii in range(og):
            gh, gl = halves(zg_ref[:, ii * va : (ii + 1) * va, at : at + width].reshape(vir, width))
            x = dot3(lh, ll, gh, gl, ((1,), (0,)))
            for par in range(2):
                for p in range(width // 128):
                    xp[p, pl.ds(par * pad + ii, vc, stride=og), :] = x[
                        par * vc : (par + 1) * vc, p * 128 : (p + 1) * 128
                    ]
        for p in range(width // 128):
            xo[:, at + p * 128 : at + (p + 1) * 128] = xp[p]
        x_push(m, xo, r, far, ny - 1).start()
        each(ny - 1, lambda s: x_push(m, xo, r, beside(s), s).start())

    two = len(zcuts) > 1
    each(nr, step)
    finish(nr - 1)
    deliver(0)
    z_forwarded(0)
    if two:
        z_start(1)
    to_pair(1).wait_send()
    if ny > 2:
        to_pair(2).start()
    deliver(1)
    if two:
        z_forward(1)
    z_rows(0)
    for s in range(2, ny):
        to_pair(s).wait_send()
        if s + 1 < ny:
            to_pair(s + 1).start()
        deliver(s)
        if s == 2:
            x_forward(0)
            if two:
                z_rows(1)
    if ny < 3:
        x_forward(0)
        if two:
            z_rows(1)
    if two:
        x_forward(1)
    x_own = pltpu.make_async_copy(xo, xz_ref.at[r], loc)
    x_own.start()

    def arrived(s):
        pltpu.make_async_remote_copy(
            src_ref=own.at[0], dst_ref=rs_recv.at[lax.rem(y + 1 + s, ny)], send_sem=rs_s.at[0],
            recv_sem=rs_r.at[lax.rem(y + 1 + s, ny)],
            device_id=(r, sib), device_id_type=MESH,
        ).wait_recv()

    each(ny - 1, arrived)

    def add_up(g):
        rows = pl.ds(pl.multiple_of(g * 8, 8), 8)
        total = rs_recv[0, rows, :]
        for s in range(1, ny):
            total = total + rs_recv[s, rows, :]
        fsum[rows, :] = total

    each(fsum.shape[0] // 8, add_up)
    hop = pltpu.make_async_remote_copy(
        src_ref=fsum, dst_ref=fp_ref, send_sem=hop_s, recv_sem=hop_r,
        device_id=(blk, c), device_id_type=MESH,
    )

    @pl.when(is_own)
    def _():
        fp_ref[...] = fsum[...]

    @pl.when(jnp.logical_not(is_own))
    def _():
        hop.start()

    for m in range(len(zcuts)):
        z_push(m, zc, t, pair, ny - 1).wait_send()
        x_push(m, xo, r, far, ny - 1).wait_send()

        def settle(s, m=m):
            z_push(m, zc, t, along(s), s).wait_send()
            x_push(m, xo, r, beside(s), s).wait_send()
            x_push(m, xz_ref.at[far], far, beside(s), ny + s).wait_send()
            x_push(m, xo, beside(s), far, s).wait_recv()
            x_push(m, xo, lax.rem(far + 2 * (s + 1), nr), far, s).wait_recv()

        each(ny - 1, settle)
    if two:
        z_forwarded(1)
    each(nr, lambda s: to_sibling(s).wait_send())

    each(ny - 1, lambda s: to_owner(s).wait_send())

    @pl.when(jnp.logical_not(is_own))
    def _():
        hop.wait()

    to_pair(0).wait_send()
    x_own.wait()


def tile_kernel(
    nr, og, vc, tiles, cuts,
    fp_ref, zg_hbm, xz_hbm, l_ref, r_ref, rowd_ref, cold_ref,
    out_ref,
    zg_ref, xz_ref, fg, rh, rl, yh, yl, xp, xo, xg, xh, xl, s_send, s_recv, own,
    fs, fr, xs, xr, ss, sr, os_, or_, loc, load,
):
    x_load = pltpu.make_async_copy(xz_hbm, xz_ref, load.at[0])
    z_load = pltpu.make_async_copy(zg_hbm, zg_ref, load.at[1])
    x_load.start()
    z_load.start()
    r, c = lax.axis_index("row"), lax.axis_index("col")
    t, k = c // 2, lax.rem(c, 2)
    sib = c + 1 - 2 * k
    half = fp_ref.shape[1]
    vir = r_ref.shape[0]
    va = vir // nr
    pad = xo.shape[0] // 2
    wide_pad = xh.shape[1] // nr
    blk = lax.rem(t - r + nr, nr)
    far = r + 1 - 2 * lax.rem(r, 2)
    near = nr // 2 - 1

    barrier = pltpu.get_barrier_semaphore()
    pl.semaphore_signal(barrier, inc=1, device_id=(r, sib), device_id_type=MESH)

    def greet(s, _):
        pl.semaphore_signal(barrier, inc=1, device_id=(lax.rem(r + 1 + s, nr), c), device_id_type=MESH)
        pl.semaphore_signal(
            barrier, inc=1, device_id=(r, 2 * lax.rem(t + 1 + s, nr) + k), device_id_type=MESH
        )
        return 0

    lax.fori_loop(0, nr - 1, greet, 0)

    pl.semaphore_wait(barrier, 2 * nr - 1)

    ny = nr // 2
    y, low = t // 2, lax.rem(t, 2)
    pair = t + 1 - 2 * low

    def along(s):
        return 2 * lax.rem(y + 1 + s, ny) + low

    def slot_of(other):
        return lax.rem(other - r + nr, nr)

    def f_push(m, src_ref, slot, peer, sem):
        at, width = cuts[m]
        cols = pl.ds(at, width)
        return pltpu.make_async_remote_copy(
            src_ref=src_ref.at[:, cols], dst_ref=fg.at[slot, :, cols],
            send_sem=fs.at[m, sem], recv_sem=fr.at[m, slot],
            device_id=(r, 2 * peer + k), device_id_type=MESH,
        )

    def each(count, body):
        def one(s, _):
            body(s)
            return 0

        lax.fori_loop(0, count, one, 0)

    def f_start(m):
        f_push(m, fp_ref, blk, pair, ny - 1).start()
        each(ny - 1, lambda s: f_push(m, fp_ref, blk, along(s), s).start())

    def f_forward(m):
        f_push(m, fp_ref, slot_of(pair), pair, ny - 1).wait_recv()
        each(
            ny - 1,
            lambda s: f_push(m, fg.at[slot_of(pair)], slot_of(pair), along(s), ny + s).start(),
        )

    def f_rest(m):
        def one(s):
            f_push(m, fp_ref, slot_of(along(s)), pair, ny - 1).wait_recv()
            f_push(m, fp_ref, slot_of(along(s) + pair - t), pair, ny - 1).wait_recv()

        each(ny - 1, one)

    last = len(cuts) - 1
    f_start(0)

    hi, lo = halves(r_ref[...])
    rh[:vir, :] = hi
    rl[:vir, :] = lo
    hi, lo = halves(l_ref[pl.ds(pl.multiple_of(t * va, 8), va), :])
    rh[vir:, :] = hi
    rl[vir:, :] = lo
    xp[...] = jnp.zeros_like(xp)
    fg[blk] = fp_ref[...]
    def f_forwarded(m):
        each(ny - 1, lambda s: f_push(m, fp_ref, blk, along(s), ny + s).wait_send())

    def x_push(m, src_ref, slot, dst, sem):
        return pltpu.make_async_remote_copy(
            src_ref=src_ref, dst_ref=xg.at[slot, :, pl.ds(*cuts[m])],
            send_sem=xs.at[m, sem], recv_sem=xr.at[m, slot],
            device_id=(dst, c), device_id_type=MESH,
        )

    def x_mine(m):
        return xo.at[:, pl.ds(*cuts[m])]

    def x_far(m):
        return xg.at[far, :, pl.ds(*cuts[m])]

    def beside(s):
        return lax.rem(r + 2 * (s + 1), nr)

    def x_start(m):
        x_push(m, x_mine(m), r, far, near).start()
        each(near, lambda s: x_push(m, x_mine(m), r, beside(s), s).start())

    def x_arrive(m, slot):
        x_push(m, x_mine(m), slot, far, near).wait_recv()

    def x_forward(m):
        x_arrive(m, far)
        each(near, lambda s: x_push(m, x_far(m), far, beside(s), near + 1 + s).start())

    def rotate(g_ref, fitted, at, width):
        y_at = half * fitted + at
        count = vir + va * fitted
        for ii in range(og):
            gh, gl = halves(g_ref[:, ii * va : (ii + 1) * va, at : at + width].reshape(vir, width))
            both = dot3(rh[:count], rl[:count], gh, gl, ((1,), (0,)))
            hi, lo = halves(both[:vir])
            yh[ii * vir : (ii + 1) * vir, y_at : y_at + width] = hi
            yl[ii * vir : (ii + 1) * vir, y_at : y_at + width] = lo
            if fitted:
                for par in range(2):
                    rows = both[vir + par * vc : vir + (par + 1) * vc]
                    for p in range(width // 128):
                        xp[p, pl.ds(par * pad + ii, vc, stride=og), :] = rows[:, p * 128 : (p + 1) * 128]
        if fitted:
            for p in range(width // 128):
                xo[:, at + p * 128 : at + (p + 1) * 128] = xp[p]

    def take(src, load, x_at, width):
        rows = pl.ds(pl.multiple_of(src * wide_pad, 16), pad)
        for par in range(2):
            hi, lo = halves(load(par * pad))
            xh[par, rows, x_at : x_at + width] = hi
            xl[par, rows, x_at : x_at + width] = lo

    def take_own(m):
        at, width = cuts[m]
        take(r, lambda row: xo[row : row + pad, at : at + width], at, width)

    def take_from(m, src):
        at, width = cuts[m]
        take(src, lambda row: xg[src, row : row + pad, at : at + width], at, width)

    def take_near(m, base):
        def one(s):
            src = lax.rem(base + 2 * (s + 1), nr)
            x_arrive(m, src)
            take_from(m, src)

        each(near, one)

    x_load.wait()
    each(nr, lambda src: take(src, lambda row: xz_ref[src, row : row + pad, :], half, half))
    f_forward(0)
    z_load.wait()
    rotate(zg_ref, 0, 0, half)
    for m, (at, width) in enumerate(cuts):
        f_forwarded(m)
        if m < last:
            f_start(m + 1)
        f_rest(m)
        rotate(fg, 1, at, width)
        x_start(m)
        if m < last:
            f_forward(m + 1)
        if m:
            x_forward(m - 1)
    x_forward(last)
    for m in range(len(cuts)):
        take_own(m)
        take_from(m, far)
        take_near(m, r)
        take_near(m, far)

    def to_sibling(n, width):
        return pltpu.make_async_remote_copy(
            src_ref=s_send.at[lax.rem(n, 2), :, pl.ds(0, width)], dst_ref=s_recv.at[n, :, pl.ds(0, width)],
            send_sem=ss.at[lax.rem(n, 2)], recv_sem=sr.at[n],
            device_id=(r, sib), device_id_type=MESH,
        )

    def to_row(n, width, s, src):
        dst = lax.rem(r + 1 + s, nr)
        cols = pl.ds(pl.multiple_of(n * WIDE, 128), width)
        return pltpu.make_async_remote_copy(
            src_ref=own.at[pl.ds(pl.multiple_of(dst * wide_pad, 8), pad), cols],
            dst_ref=out_ref.at[src, :, cols],
            send_sem=os_.at[n, s], recv_sem=or_.at[n, src],
            device_id=(dst, c), device_id_type=MESH,
        )

    def stay(n, width):
        cols = pl.ds(pl.multiple_of(n * WIDE, 128), width)
        return pltpu.make_async_copy(
            own.at[pl.ds(pl.multiple_of(r * wide_pad, 8), pad), cols], out_ref.at[r, :, cols], loc.at[n]
        )

    def tile(n, width, slot_used):
        rows = pl.ds(pl.multiple_of(n * WIDE, 128), width)
        wh, wl = yh[rows, :], yl[rows, :]

        def product(par):
            return dot3(xh[par], xl[par], wh, wl, ((1,), (1,)))

        @pl.when(slot_used)
        def _():
            to_sibling(n - 2, WIDE).wait_send()

        s_send[lax.rem(n, 2), :, 0:width] = product(1 - k)
        to_sibling(n, width).start()
        own[:, rows] = product(k)
        to_sibling(n, width).wait_recv()
        reps = width // 128

        def close(g, _):
            at = pl.ds(pl.multiple_of(g * wide_pad, 8), wide_pad)
            rowd = rowd_ref[at, :]
            for m in range(reps):
                cols = pl.ds(pl.multiple_of(n * WIDE + m * 128, 128), 128)
                here = own[at, cols] + s_recv[n, at, m * 128 : (m + 1) * 128]
                own[at, cols] = here / (rowd + cold_ref[0:1, cols])
            return 0

        lax.fori_loop(0, nr, close, 0)

        def send(s, _):
            to_row(n, width, s, r).start()
            return 0

        lax.fori_loop(0, nr - 1, send, 0)
        stay(n, width).start()

    tail = yh.shape[0] - (tiles - 1) * WIDE

    def full(n, _):
        tile(n, WIDE, n > 1)
        return 0

    lax.fori_loop(0, tiles - 1, full, 0)
    tile(jnp.int32(tiles - 1), tail, tiles > 2)

    def settle(n, width):
        def one(s, _):
            src = lax.rem(r + 1 + s, nr)
            to_row(n, width, s, src).wait()
            return 0

        lax.fori_loop(0, nr - 1, one, 0)
        stay(n, width).wait()

    def settle_full(n, _):
        settle(n, WIDE)
        return 0

    lax.fori_loop(0, tiles - 1, settle_full, 0)
    settle(jnp.int32(tiles - 1), tail)
    to_sibling(jnp.int32(tiles - 2), WIDE).wait_send()
    to_sibling(jnp.int32(tiles - 1), tail).wait_send()
    for m in range(len(cuts)):
        x_push(m, x_mine(m), r, far, near).wait_send()
        each(near, lambda s, m=m: x_push(m, x_mine(m), r, beside(s), s).wait_send())
        each(near, lambda s, m=m: x_push(m, x_far(m), far, beside(s), near + 1 + s).wait_send())
    for m in range(len(cuts)):
        f_push(m, fp_ref, blk, pair, ny - 1).wait_send()
        each(ny - 1, lambda s, m=m: f_push(m, fp_ref, blk, along(s), s).wait_send())


def lay_kernel(nr, og, vir, occ, in_ref, out_ref):
    wide = in_ref.shape[2]
    for at in range(0, vir, 128):
        keep = min(128, vir - at)
        parts = []
        for src in range(nr):
            for jj in range(og):
                start = jj * vir + at
                n = min(128, wide - start)
                v = in_ref[src, :, start : start + n]
                if n < 128:
                    v = jnp.concatenate([v, jnp.zeros((8, 128 - n), F32)], axis=1)
                parts.append(v)
        turned_rows = jnp.swapaxes(jnp.stack(parts, axis=0), 0, 1)
        out_ref[:, at : at + keep] = turned_rows.reshape(8 * occ, 128)[:, :keep]


def shards(amplitudes, aux_left, aux_right, left_rotation, right_rotation, occ_energy, vir_energy):
    nr, nc = lax.axis_size("row"), lax.axis_size("col")
    occ, vir = occ_energy.shape[0], vir_energy.shape[0]
    naux = aux_left.shape[1]
    half = naux // 2
    og, va, vc = occ // nr, vir // nr, vir // nc
    piece = og * va
    rows = vc * og
    pad, wide_pad = up(rows, 8), up(rows, 16)
    dma = pltpu.SemaphoreType.DMA
    vmem = pl.BlockSpec(memory_space=pltpu.VMEM)
    hbm = pl.BlockSpec(memory_space=pl.ANY)
    limit = 60 * 1024 * 1024

    cols = og * vir
    first = up(half * 3 // 5, 128)
    zcuts = [(0, first), (first, half - first)] if first < half else [(0, half)]
    fp, zg, xz = pl.pallas_call(
        functools.partial(gather_kernel, nr, occ, zcuts),
        out_shape=[
            jax.ShapeDtypeStruct((piece, half), F32),
            jax.ShapeDtypeStruct((nr, piece, half), F32),
            jax.ShapeDtypeStruct((nr, 2 * pad, half), F32),
        ],
        in_specs=[hbm, hbm, vmem, vmem],
        out_specs=[vmem, vmem, hbm],
        scratch_shapes=[
            pltpu.VMEM(amplitudes.shape[::-1], F32),
            pltpu.VMEM(aux_left.shape, F32),
            pltpu.VMEM((up(amplitudes.shape[1], 128) // 128, amplitudes.shape[0], 128), F32),
            pltpu.VMEM((up(naux, 128) // 128, aux_right.shape[0], 128), F32),
            pltpu.VMEM((aux_left.shape[0], naux), BF16),
            pltpu.VMEM((aux_left.shape[0], naux), BF16),
            pltpu.VMEM((nr, piece, half), F32),
            pltpu.VMEM((nr, piece, half), F32),
            pltpu.VMEM((nr, piece, half), F32),
            pltpu.VMEM((nr // 2, piece, half), F32),
            pltpu.VMEM((nr // 2, piece, half), F32),
            pltpu.VMEM((piece, half), F32),
            pltpu.VMEM((og, vc, half), F32),
            pltpu.VMEM((og, vc, half), F32),
            pltpu.VMEM((piece, half), F32),
            pltpu.VMEM((half // 128, 2 * pad, 128), F32),
            pltpu.VMEM((2 * pad, half), F32),
            dma((nr,)), dma((nr,)), dma((nr,)), dma((nr,)), dma((nr,)), dma((nr,)), dma, dma, dma, dma,
            dma((2, nr)), dma((2, nr)), dma((2, nr)), dma((2, nr)), dma, dma((2,)),
        ],
        compiler_params=pltpu.CompilerParams(collective_id=0, has_side_effects=True, vmem_limit_bytes=limit),
        name="fit_gather",
    )(amplitudes.T, aux_left, aux_right, left_rotation)

    cols_pad = up(cols, 128)
    tiles = up(cols_pad, WIDE) // WIDE
    cuts = [(at, min(256, half - at)) for at in range(0, half, 256)]
    r, c = lax.axis_index("row"), lax.axis_index("col")
    vir_here = lax.dynamic_slice_in_dim(vir_energy, c * vc, vc)
    occ_here = lax.dynamic_slice_in_dim(occ_energy, r * og, og)
    rowd = (vir_here[None, :, None] - occ_energy.reshape(nr, 1, og)).reshape(nr, rows)
    rowd = jnp.pad(rowd, ((0, 0), (0, wide_pad - rows)), constant_values=1.0).reshape(nr * wide_pad, 1)
    rowd = jnp.broadcast_to(rowd, (nr * wide_pad, 128))
    cold = (vir_energy[None, :] - occ_here[:, None]).reshape(1, cols)
    cold = jnp.pad(cold, ((0, 0), (0, cols_pad - cols)), constant_values=1.0)
    cold = jnp.broadcast_to(cold, (8, cols_pad))

    moved = pl.pallas_call(
        functools.partial(tile_kernel, nr, og, vc, tiles, cuts),
        out_shape=jax.ShapeDtypeStruct((nr, pad, cols_pad), F32),
        in_specs=[vmem, hbm, hbm] + [vmem] * 4,
        out_specs=hbm,
        scratch_shapes=[
            pltpu.VMEM((nr, piece, half), F32),
            pltpu.VMEM((nr, 2 * pad, half), F32),
            pltpu.VMEM((nr, piece, half), F32),
            pltpu.VMEM((vir + va, vir), BF16),
            pltpu.VMEM((vir + va, vir), BF16),
            pltpu.VMEM((cols_pad, naux), BF16),
            pltpu.VMEM((cols_pad, naux), BF16),
            pltpu.VMEM((half // 128, 2 * pad, 128), F32),
            pltpu.VMEM((2 * pad, half), F32),
            pltpu.VMEM((nr, 2 * pad, half), F32),
            pltpu.VMEM((2, nr * wide_pad, naux), BF16),
            pltpu.VMEM((2, nr * wide_pad, naux), BF16),
            pltpu.VMEM((2, nr * wide_pad, WIDE), F32),
            pltpu.VMEM((tiles, nr * wide_pad, WIDE), F32),
            pltpu.VMEM((nr * wide_pad, cols_pad), F32),
            dma((len(cuts), nr)), dma((len(cuts), nr)),
            dma((len(cuts), nr)), dma((len(cuts), nr)), dma((2,)), dma((tiles,)),
            dma((tiles, nr)), dma((tiles, nr)), dma((tiles,)), dma((2,)),
        ],
        compiler_params=pltpu.CompilerParams(collective_id=1, has_side_effects=True, vmem_limit_bytes=limit),
        name="tile_exchange",
    )(fp, zg, xz, left_rotation, right_rotation, rowd, cold)

    out = pl.pallas_call(
        functools.partial(lay_kernel, nr, og, vir, occ),
        grid=(pad // 8,),
        out_shape=jax.ShapeDtypeStruct((rows * occ, vir), F32),
        in_specs=[pl.BlockSpec((nr, 8, cols_pad), lambda g: (0, g, 0))],
        out_specs=pl.BlockSpec((8 * occ, vir), lambda g: (g, 0)),
        compiler_params=pltpu.CompilerParams(vmem_limit_bytes=limit),
        name="lay_out",
    )(moved)
    return out.reshape(vc, og, occ, vir)


def solution(mesh):
    placed = (P("row", "col"), P("col", None), P("col", None), P(), P(), P(), P())
    return jax.shard_map(
        shards, mesh=mesh, in_specs=placed, out_specs=P("col", "row", None, None), check_vma=False
    )
```

```python
import functools

import jax
import jax.numpy as jnp
from jax import lax
from jax.experimental import pallas as pl
from jax.experimental.pallas import tpu as pltpu
from jax.sharding import PartitionSpec as P

MESH = pl.DeviceIdType.MESH
F32 = jnp.float32
BF16 = jnp.bfloat16
WIDE = 256


def halves(x):
    hi = x.astype(BF16)
    return hi, (x - hi.astype(F32)).astype(BF16)


def dot3(xh, xl, yh, yl, dims):
    def dot(a, b):
        return lax.dot_general(a, b, (dims, ((), ())), preferred_element_type=F32)

    return dot(xl, yh) + dot(xh, yl) + dot(xh, yh)


def up(n, unit):
    return -(-n // unit) * unit


def planes(src, dst):
    width, rows = src.shape[1], 40 if src.shape[0] % 40 == 0 else src.shape[0]

    def one(g, _):
        at = pl.ds(pl.multiple_of(g * rows, 8), rows)
        for p in range(dst.shape[0]):
            n = min(128, width - p * 128)
            dst[p, at, :n] = src[at, p * 128 : p * 128 + n]
        return 0

    lax.fori_loop(0, src.shape[0] // rows, one, 0)


def turned(src, dst):
    depth, width = src.shape
    for p in range(dst.shape[0]):
        n = min(128, depth - p * 128)

        def one(g, _, p=p, n=n):
            at = pl.ds(pl.multiple_of(g * 128, 128), 128)
            dst[p, at, :n] = src[p * 128 : p * 128 + n, at].T
            return 0

        lax.fori_loop(0, width // 128, one, 0)
        at = width // 128 * 128
        if at < width:
            dst[p, at:, :n] = src[p * 128 : p * 128 + n, at:].T


def every(src, start, count, stride, width):
    parts = [src[p, pl.ds(start, count, stride=stride), :] for p in range(src.shape[0])]
    return jnp.concatenate(parts, axis=1)[:, :width]


def gather_kernel(
    nr, occ, zcuts,
    t_hbm, b_hbm, z_ref, l_ref,
    fp_ref, zg_ref, xz_ref,
    t_ref, b_ref, tp, zp, bh, bl, sib_send, sib_recv, own, z_recv, rs_recv, fsum, zs_send, zs_recv, zc, xp, xo,
    sib_s, sib_r, zz_s, zz_r, rs_s, rs_r, hop_s, hop_r, zs_s, zs_r, za_s, za_r, xs, xr, loc, load,
):
    b_load = pltpu.make_async_copy(b_hbm, b_ref, load.at[0])
    t_load = pltpu.make_async_copy(t_hbm, t_ref, load.at[1])
    b_load.start()
    t_load.start()
    r, c = lax.axis_index("row"), lax.axis_index("col")
    t, k = c // 2, lax.rem(c, 2)
    sib = c + 1 - 2 * k
    og = occ // nr
    va = t_ref.shape[1] // occ
    vc = z_ref.shape[0] // occ
    half = b_ref.shape[1] // 2
    blk = lax.rem(t - r + nr, nr)
    is_own = lax.rem(r + r, nr) == t
    ny = nr // 2
    y, low = t // 2, lax.rem(t, 2)
    pair = t + 1 - 2 * low

    far = r + 1 - 2 * lax.rem(r, 2)
    vir = va * nr
    pad = xo.shape[0] // 2

    barrier = pltpu.get_barrier_semaphore()
    pl.semaphore_signal(barrier, inc=1, device_id=(r, sib), device_id_type=MESH)

    pl.semaphore_signal(barrier, inc=1, device_id=(r, 2 * pair + k), device_id_type=MESH)

    def along(s):
        return 2 * lax.rem(y + 1 + s, ny) + low

    def each(count, body):
        def one(s, _):
            body(s)
            return 0

        lax.fori_loop(0, count, one, 0)

    def beside(s):
        return lax.rem(r + 2 * (s + 1), nr)

    pl.semaphore_signal(barrier, inc=1, device_id=(far, c), device_id_type=MESH)

    def greet(s):
        pl.semaphore_signal(barrier, inc=1, device_id=(r, 2 * along(s) + k), device_id_type=MESH)
        pl.semaphore_signal(barrier, inc=1, device_id=(beside(s), c), device_id_type=MESH)

    each(ny - 1, greet)

    @pl.when(jnp.logical_not(is_own))
    def _():
        pl.semaphore_signal(barrier, inc=1, device_id=(blk, c), device_id_type=MESH)

    planes(z_ref, zp)
    first = k == 0
    kept = []
    for jj in range(og):
        z = every(zp, r * og + jj, vc, occ, z_ref.shape[1])
        z0, z1 = z[:, :half], z[:, half:]
        zs_send[jj] = jnp.where(first, z1, z0)
        kept.append(jnp.where(first, z0, z1))
        zc[jj * va : jj * va + vc, :] = kept[-1]

    @pl.when(is_own)
    def _():
        pl.semaphore_wait(barrier, nr + 1)

    @pl.when(jnp.logical_not(is_own))
    def _():
        pl.semaphore_wait(barrier, nr + 2)

    z_swap = pltpu.make_async_remote_copy(
        src_ref=zs_send, dst_ref=zs_recv, send_sem=zs_s, recv_sem=zs_r,
        device_id=(r, sib), device_id_type=MESH,
    )
    z_swap.start()
    b_load.wait()
    mine, other = pl.ds(pl.multiple_of(k * half, half), half), pl.ds(pl.multiple_of((1 - k) * half, half), half)
    for at, cols in ((0, other), (half, mine)):
        hi, lo = halves(b_ref[:, cols])
        bh[:, at : at + half] = hi
        bl[:, at : at + half] = lo

    z_swap.wait()
    for jj in range(og):
        z_mine = zc[jj * va : jj * va + vc, :]
        z_sib = zs_recv[jj]
        zc[jj * va : (jj + 1) * va, :] = jnp.concatenate(
            [jnp.where(first, z_mine, z_sib), jnp.where(first, z_sib, z_mine)], axis=0
        )

    def z_push(m, src_ref, slot, peer, sem):
        lanes = pl.ds(*zcuts[m])
        return pltpu.make_async_remote_copy(
            src_ref=src_ref.at[:, lanes], dst_ref=zg_ref.at[slot, :, lanes],
            send_sem=za_s.at[m, sem], recv_sem=za_r.at[m, slot],
            device_id=(r, 2 * peer + k), device_id_type=MESH,
        )

    def z_start(m):
        z_push(m, zc, t, pair, ny - 1).start()
        each(ny - 1, lambda s: z_push(m, zc, t, along(s), s).start())

    def z_forward(m):
        z_push(m, zc, pair, pair, ny - 1).wait_recv()
        each(ny - 1, lambda s: z_push(m, zg_ref.at[pair], pair, along(s), ny + s).start())

    def z_forwarded(m):
        each(ny - 1, lambda s: z_push(m, zg_ref.at[pair], pair, along(s), ny + s).wait_send())

    z_start(0)
    zg_ref[t] = zc[...]
    t_load.wait()
    turned(t_ref, tp)

    def to_sibling(s):
        return pltpu.make_async_remote_copy(
            src_ref=sib_send.at[s], dst_ref=sib_recv.at[s], send_sem=sib_s.at[s], recv_sem=sib_r.at[s],
            device_id=(r, sib), device_id_type=MESH,
        )

    def owner(s):
        stays = s // ny
        side = stays * low + (1 - stays) * (1 - low)
        return 2 * lax.rem(y + 1 + lax.rem(s, ny), ny) + side

    def to_pair(s):
        return pltpu.make_async_remote_copy(
            src_ref=own.at[s], dst_ref=z_recv.at[s], send_sem=zz_s.at[s], recv_sem=zz_r.at[s],
            device_id=(r, 2 * pair + k), device_id_type=MESH,
        )

    def to_owner(s):
        ot = owner(ny + s)
        return pltpu.make_async_remote_copy(
            src_ref=own.at[ny + s], dst_ref=rs_recv.at[y], send_sem=rs_s.at[s], recv_sem=rs_r.at[y],
            device_id=(r, 2 * ot + k), device_id_type=MESH,
        )

    def finish(s):
        to_sibling(s).wait_recv()
        own[s] = own[s] + sib_recv[s]

        @pl.when(s == 0)
        def _():
            to_pair(0).start()

        @pl.when(s == ny + 1)
        def _():
            to_pair(1).start()

    def step(s):
        dst = lax.rem(owner(s) - r + nr, nr)
        x = jnp.concatenate(
            [every(tp, dst * og + ii, va, occ, t_ref.shape[0]) for ii in range(og)], axis=0
        )
        xh, xl = halves(x)
        part = dot3(xh, xl, bh[...], bl[...], ((1,), (0,)))
        sib_send[s] = part[:, :half]
        own[s] = part[:, half:]
        to_sibling(s).start()

        @pl.when(s > 0)
        def _():
            finish(s - 1)

        @pl.when(s == ny)
        def _():
            z_forward(0)

    def deliver(s):
        to_pair(s).wait_recv()
        own[ny + s] = own[ny + s] + z_recv[s]
        if s < ny - 1:
            to_owner(s).start()
        else:
            rs_recv[y] = own[ny + s]

    def x_push(m, src_ref, slot, dst, sem):
        lanes = pl.ds(*zcuts[m])
        return pltpu.make_async_remote_copy(
            src_ref=src_ref.at[:, lanes], dst_ref=xz_ref.at[slot, :, lanes],
            send_sem=xs.at[m, sem], recv_sem=xr.at[m, slot],
            device_id=(dst, c), device_id_type=MESH,
        )

    def x_forward(m):
        x_push(m, xo, far, far, ny - 1).wait_recv()
        each(ny - 1, lambda s: x_push(m, xz_ref.at[far], far, beside(s), ny + s).start())

    lh, ll = halves(l_ref[pl.ds(pl.multiple_of(t * va, 8), va), :])
    xp[...] = jnp.zeros_like(xp)

    def z_rows(m):
        def z_rest(s):
            z_push(m, zc, along(s), along(s), s).wait_recv()
            z_push(m, zc, along(s) + pair - t, pair, s).wait_recv()

        each(ny - 1, z_rest)
        at, width = zcuts[m]
        for ii in range(og):
            gh, gl = halves(zg_ref[:, ii * va : (ii + 1) * va, at : at + width].reshape(vir, width))
            x = dot3(lh, ll, gh, gl, ((1,), (0,)))
            for par in range(2):
                for p in range(width // 128):
                    xp[p, pl.ds(par * pad + ii, vc, stride=og), :] = x[
                        par * vc : (par + 1) * vc, p * 128 : (p + 1) * 128
                    ]
        for p in range(width // 128):
            xo[:, at + p * 128 : at + (p + 1) * 128] = xp[p]
        x_push(m, xo, r, far, ny - 1).start()
        each(ny - 1, lambda s: x_push(m, xo, r, beside(s), s).start())

    two = len(zcuts) > 1
    each(nr, step)
    finish(nr - 1)
    deliver(0)
    z_forwarded(0)
    if two:
        z_start(1)
    to_pair(1).wait_send()
    if ny > 2:
        to_pair(2).start()
    deliver(1)
    if two:
        z_forward(1)
    z_rows(0)
    for s in range(2, ny):
        to_pair(s).wait_send()
        if s + 1 < ny:
            to_pair(s + 1).start()
        deliver(s)
        if s == 2:
            x_forward(0)
            if two:
                z_rows(1)
    if ny < 3:
        x_forward(0)
        if two:
            z_rows(1)
    if two:
        x_forward(1)
    x_own = pltpu.make_async_copy(xo, xz_ref.at[r], loc)
    x_own.start()

    def arrived(s):
        pltpu.make_async_remote_copy(
            src_ref=own.at[0], dst_ref=rs_recv.at[lax.rem(y + 1 + s, ny)], send_sem=rs_s.at[0],
            recv_sem=rs_r.at[lax.rem(y + 1 + s, ny)],
            device_id=(r, sib), device_id_type=MESH,
        ).wait_recv()

    each(ny - 1, arrived)

    def add_up(g):
        rows = pl.ds(pl.multiple_of(g * 8, 8), 8)
        total = rs_recv[0, rows, :]
        for s in range(1, ny):
            total = total + rs_recv[s, rows, :]
        fsum[rows, :] = total

    each(fsum.shape[0] // 8, add_up)
    hop = pltpu.make_async_remote_copy(
        src_ref=fsum, dst_ref=fp_ref, send_sem=hop_s, recv_sem=hop_r,
        device_id=(blk, c), device_id_type=MESH,
    )

    @pl.when(is_own)
    def _():
        fp_ref[...] = fsum[...]

    @pl.when(jnp.logical_not(is_own))
    def _():
        hop.start()

    for m in range(len(zcuts)):
        z_push(m, zc, t, pair, ny - 1).wait_send()
        x_push(m, xo, r, far, ny - 1).wait_send()

        def settle(s, m=m):
            z_push(m, zc, t, along(s), s).wait_send()
            x_push(m, xo, r, beside(s), s).wait_send()
            x_push(m, xz_ref.at[far], far, beside(s), ny + s).wait_send()
            x_push(m, xo, beside(s), far, s).wait_recv()
            x_push(m, xo, lax.rem(far + 2 * (s + 1), nr), far, s).wait_recv()

        each(ny - 1, settle)
    if two:
        z_forwarded(1)
    each(nr, lambda s: to_sibling(s).wait_send())

    each(ny - 1, lambda s: to_owner(s).wait_send())

    @pl.when(jnp.logical_not(is_own))
    def _():
        hop.wait()

    to_pair(0).wait_send()
    x_own.wait()


def tile_kernel(
    nr, og, vc, tiles, cuts,
    fp_ref, zg_hbm, xz_hbm, l_ref, r_ref, rowd_ref, cold_ref,
    out_ref,
    zg_ref, xz_ref, fg, rh, rl, yh, yl, xp, xo, xg, xh, xl, s_send, s_recv, own,
    fs, fr, xs, xr, ss, sr, os_, or_, loc, load,
):
    x_load = pltpu.make_async_copy(xz_hbm, xz_ref, load.at[0])
    z_load = pltpu.make_async_copy(zg_hbm, zg_ref, load.at[1])
    x_load.start()
    z_load.start()
    r, c = lax.axis_index("row"), lax.axis_index("col")
    t, k = c // 2, lax.rem(c, 2)
    sib = c + 1 - 2 * k
    half = fp_ref.shape[1]
    vir = r_ref.shape[0]
    va = vir // nr
    pad = xo.shape[0] // 2
    wide_pad = xh.shape[1] // nr
    blk = lax.rem(t - r + nr, nr)
    far = r + 1 - 2 * lax.rem(r, 2)
    near = nr // 2 - 1

    barrier = pltpu.get_barrier_semaphore()
    pl.semaphore_signal(barrier, inc=1, device_id=(r, sib), device_id_type=MESH)

    def greet(s, _):
        pl.semaphore_signal(barrier, inc=1, device_id=(lax.rem(r + 1 + s, nr), c), device_id_type=MESH)
        pl.semaphore_signal(
            barrier, inc=1, device_id=(r, 2 * lax.rem(t + 1 + s, nr) + k), device_id_type=MESH
        )
        return 0

    lax.fori_loop(0, nr - 1, greet, 0)

    pl.semaphore_wait(barrier, 2 * nr - 1)

    ny = nr // 2
    y, low = t // 2, lax.rem(t, 2)
    pair = t + 1 - 2 * low

    def along(s):
        return 2 * lax.rem(y + 1 + s, ny) + low

    def slot_of(other):
        return lax.rem(other - r + nr, nr)

    def f_push(m, src_ref, slot, peer, sem):
        at, width = cuts[m]
        cols = pl.ds(at, width)
        return pltpu.make_async_remote_copy(
            src_ref=src_ref.at[:, cols], dst_ref=fg.at[slot, :, cols],
            send_sem=fs.at[m, sem], recv_sem=fr.at[m, slot],
            device_id=(r, 2 * peer + k), device_id_type=MESH,
        )

    def each(count, body):
        def one(s, _):
            body(s)
            return 0

        lax.fori_loop(0, count, one, 0)

    def f_start(m):
        f_push(m, fp_ref, blk, pair, ny - 1).start()
        each(ny - 1, lambda s: f_push(m, fp_ref, blk, along(s), s).start())

    def f_forward(m):
        f_push(m, fp_ref, slot_of(pair), pair, ny - 1).wait_recv()
        each(
            ny - 1,
            lambda s: f_push(m, fg.at[slot_of(pair)], slot_of(pair), along(s), ny + s).start(),
        )

    def f_rest(m):
        def one(s):
            f_push(m, fp_ref, slot_of(along(s)), pair, ny - 1).wait_recv()
            f_push(m, fp_ref, slot_of(along(s) + pair - t), pair, ny - 1).wait_recv()

        each(ny - 1, one)

    last = len(cuts) - 1
    f_start(0)

    hi, lo = halves(r_ref[...])
    rh[:vir, :] = hi
    rl[:vir, :] = lo
    hi, lo = halves(l_ref[pl.ds(pl.multiple_of(t * va, 8), va), :])
    rh[vir:, :] = hi
    rl[vir:, :] = lo
    xp[...] = jnp.zeros_like(xp)
    fg[blk] = fp_ref[...]
    def f_forwarded(m):
        each(ny - 1, lambda s: f_push(m, fp_ref, blk, along(s), ny + s).wait_send())

    def x_push(m, src_ref, slot, dst, sem):
        return pltpu.make_async_remote_copy(
            src_ref=src_ref, dst_ref=xg.at[slot, :, pl.ds(*cuts[m])],
            send_sem=xs.at[m, sem], recv_sem=xr.at[m, slot],
            device_id=(dst, c), device_id_type=MESH,
        )

    def x_mine(m):
        return xo.at[:, pl.ds(*cuts[m])]

    def x_far(m):
        return xg.at[far, :, pl.ds(*cuts[m])]

    def beside(s):
        return lax.rem(r + 2 * (s + 1), nr)

    def x_start(m):
        x_push(m, x_mine(m), r, far, near).start()
        each(near, lambda s: x_push(m, x_mine(m), r, beside(s), s).start())

    def x_arrive(m, slot):
        x_push(m, x_mine(m), slot, far, near).wait_recv()

    def x_forward(m):
        x_arrive(m, far)
        each(near, lambda s: x_push(m, x_far(m), far, beside(s), near + 1 + s).start())

    def rotate(g_ref, fitted, at, width):
        y_at = half * fitted + at
        count = vir + va * fitted
        for ii in range(og):
            gh, gl = halves(g_ref[:, ii * va : (ii + 1) * va, at : at + width].reshape(vir, width))
            both = dot3(rh[:count], rl[:count], gh, gl, ((1,), (0,)))
            hi, lo = halves(both[:vir])
            yh[ii * vir : (ii + 1) * vir, y_at : y_at + width] = hi
            yl[ii * vir : (ii + 1) * vir, y_at : y_at + width] = lo
            if fitted:
                for par in range(2):
                    rows = both[vir + par * vc : vir + (par + 1) * vc]
                    for p in range(width // 128):
                        xp[p, pl.ds(par * pad + ii, vc, stride=og), :] = rows[:, p * 128 : (p + 1) * 128]
        if fitted:
            for p in range(width // 128):
                xo[:, at + p * 128 : at + (p + 1) * 128] = xp[p]

    def take(src, load, x_at, width):
        rows = pl.ds(pl.multiple_of(src * wide_pad, 16), pad)
        for par in range(2):
            hi, lo = halves(load(par * pad))
            xh[par, rows, x_at : x_at + width] = hi
            xl[par, rows, x_at : x_at + width] = lo

    def take_own(m):
        at, width = cuts[m]
        take(r, lambda row: xo[row : row + pad, at : at + width], at, width)

    def take_from(m, src):
        at, width = cuts[m]
        take(src, lambda row: xg[src, row : row + pad, at : at + width], at, width)

    def take_near(m, base):
        def one(s):
            src = lax.rem(base + 2 * (s + 1), nr)
            x_arrive(m, src)
            take_from(m, src)

        each(near, one)

    x_load.wait()
    each(nr, lambda src: take(src, lambda row: xz_ref[src, row : row + pad, :], half, half))
    f_forward(0)
    z_load.wait()
    rotate(zg_ref, 0, 0, half)
    for m, (at, width) in enumerate(cuts):
        f_forwarded(m)
        if m < last:
            f_start(m + 1)
        f_rest(m)
        rotate(fg, 1, at, width)
        x_start(m)
        if m < last:
            f_forward(m + 1)
        if m:
            x_forward(m - 1)
    x_forward(last)
    for m in range(len(cuts)):
        take_own(m)
        take_from(m, far)
        take_near(m, r)
        take_near(m, far)

    def to_sibling(n, width):
        return pltpu.make_async_remote_copy(
            src_ref=s_send.at[lax.rem(n, 2), :, pl.ds(0, width)], dst_ref=s_recv.at[n, :, pl.ds(0, width)],
            send_sem=ss.at[lax.rem(n, 2)], recv_sem=sr.at[n],
            device_id=(r, sib), device_id_type=MESH,
        )

    def to_row(n, width, s, src):
        dst = lax.rem(r + 1 + s, nr)
        cols = pl.ds(pl.multiple_of(n * WIDE, 128), width)
        return pltpu.make_async_remote_copy(
            src_ref=own.at[pl.ds(pl.multiple_of(dst * wide_pad, 8), pad), cols],
            dst_ref=out_ref.at[src, :, cols],
            send_sem=os_.at[n, s], recv_sem=or_.at[n, src],
            device_id=(dst, c), device_id_type=MESH,
        )

    def stay(n, width):
        cols = pl.ds(pl.multiple_of(n * WIDE, 128), width)
        return pltpu.make_async_copy(
            own.at[pl.ds(pl.multiple_of(r * wide_pad, 8), pad), cols], out_ref.at[r, :, cols], loc.at[n]
        )

    def tile(n, width, slot_used):
        rows = pl.ds(pl.multiple_of(n * WIDE, 128), width)
        wh, wl = yh[rows, :], yl[rows, :]

        def product(par):
            return dot3(xh[par], xl[par], wh, wl, ((1,), (1,)))

        @pl.when(slot_used)
        def _():
            to_sibling(n - 2, WIDE).wait_send()

        s_send[lax.rem(n, 2), :, 0:width] = product(1 - k)
        to_sibling(n, width).start()
        own[:, rows] = product(k)
        to_sibling(n, width).wait_recv()
        reps = width // 128

        def close(g, _):
            at = pl.ds(pl.multiple_of(g * wide_pad, 8), wide_pad)
            rowd = rowd_ref[at, :]
            for m in range(reps):
                cols = pl.ds(pl.multiple_of(n * WIDE + m * 128, 128), 128)
                here = own[at, cols] + s_recv[n, at, m * 128 : (m + 1) * 128]
                own[at, cols] = here / (rowd + cold_ref[0:1, cols])
            return 0

        lax.fori_loop(0, nr, close, 0)

        def send(s, _):
            to_row(n, width, s, r).start()
            return 0

        lax.fori_loop(0, nr - 1, send, 0)
        stay(n, width).start()

    tail = yh.shape[0] - (tiles - 1) * WIDE

    def full(n, _):
        tile(n, WIDE, n > 1)
        return 0

    lax.fori_loop(0, tiles - 1, full, 0)
    tile(jnp.int32(tiles - 1), tail, tiles > 2)

    def settle(n, width):
        def one(s, _):
            src = lax.rem(r + 1 + s, nr)
            to_row(n, width, s, src).wait()
            return 0

        lax.fori_loop(0, nr - 1, one, 0)
        stay(n, width).wait()

    def settle_full(n, _):
        settle(n, WIDE)
        return 0

    lax.fori_loop(0, tiles - 1, settle_full, 0)
    settle(jnp.int32(tiles - 1), tail)
    to_sibling(jnp.int32(tiles - 2), WIDE).wait_send()
    to_sibling(jnp.int32(tiles - 1), tail).wait_send()
    for m in range(len(cuts)):
        x_push(m, x_mine(m), r, far, near).wait_send()
        each(near, lambda s, m=m: x_push(m, x_mine(m), r, beside(s), s).wait_send())
        each(near, lambda s, m=m: x_push(m, x_far(m), far, beside(s), near + 1 + s).wait_send())
    for m in range(len(cuts)):
        f_push(m, fp_ref, blk, pair, ny - 1).wait_send()
        each(ny - 1, lambda s, m=m: f_push(m, fp_ref, blk, along(s), s).wait_send())


def lay_kernel(nr, og, vir, occ, in_ref, out_ref):
    wide = in_ref.shape[2]

    def group(g, _):
        rows = pl.ds(pl.multiple_of(g * 8, 8), 8)
        outs = pl.ds(pl.multiple_of(g * 8 * occ, 8), 8 * occ)
        for at in range(0, vir, 128):
            keep = min(128, vir - at)
            parts = []
            for src in range(nr):
                for jj in range(og):
                    start = jj * vir + at
                    n = min(128, wide - start)
                    v = in_ref[src, rows, start : start + n]
                    if n < 128:
                        v = jnp.concatenate([v, jnp.zeros((8, 128 - n), F32)], axis=1)
                    parts.append(v)
            turned_rows = jnp.swapaxes(jnp.stack(parts, axis=0), 0, 1)
            out_ref[outs, at : at + keep] = turned_rows.reshape(8 * occ, 128)[:, :keep]
        return 0

    lax.fori_loop(0, in_ref.shape[1] // 8, group, 0)


def shards(amplitudes, aux_left, aux_right, left_rotation, right_rotation, occ_energy, vir_energy):
    nr, nc = lax.axis_size("row"), lax.axis_size("col")
    occ, vir = occ_energy.shape[0], vir_energy.shape[0]
    naux = aux_left.shape[1]
    half = naux // 2
    og, va, vc = occ // nr, vir // nr, vir // nc
    piece = og * va
    rows = vc * og
    pad, wide_pad = up(rows, 8), up(rows, 16)
    dma = pltpu.SemaphoreType.DMA
    vmem = pl.BlockSpec(memory_space=pltpu.VMEM)
    hbm = pl.BlockSpec(memory_space=pl.ANY)
    limit = 60 * 1024 * 1024

    cols = og * vir
    first = up(half * 3 // 5, 128)
    zcuts = [(0, first), (first, half - first)] if first < half else [(0, half)]
    fp, zg, xz = pl.pallas_call(
        functools.partial(gather_kernel, nr, occ, zcuts),
        out_shape=[
            jax.ShapeDtypeStruct((piece, half), F32),
            jax.ShapeDtypeStruct((nr, piece, half), F32),
            jax.ShapeDtypeStruct((nr, 2 * pad, half), F32),
        ],
        in_specs=[hbm, hbm, vmem, vmem],
        out_specs=[vmem, vmem, hbm],
        scratch_shapes=[
            pltpu.VMEM(amplitudes.shape[::-1], F32),
            pltpu.VMEM(aux_left.shape, F32),
            pltpu.VMEM((up(amplitudes.shape[1], 128) // 128, amplitudes.shape[0], 128), F32),
            pltpu.VMEM((up(naux, 128) // 128, aux_right.shape[0], 128), F32),
            pltpu.VMEM((aux_left.shape[0], naux), BF16),
            pltpu.VMEM((aux_left.shape[0], naux), BF16),
            pltpu.VMEM((nr, piece, half), F32),
            pltpu.VMEM((nr, piece, half), F32),
            pltpu.VMEM((nr, piece, half), F32),
            pltpu.VMEM((nr // 2, piece, half), F32),
            pltpu.VMEM((nr // 2, piece, half), F32),
            pltpu.VMEM((piece, half), F32),
            pltpu.VMEM((og, vc, half), F32),
            pltpu.VMEM((og, vc, half), F32),
            pltpu.VMEM((piece, half), F32),
            pltpu.VMEM((half // 128, 2 * pad, 128), F32),
            pltpu.VMEM((2 * pad, half), F32),
            dma((nr,)), dma((nr,)), dma((nr,)), dma((nr,)), dma((nr,)), dma((nr,)), dma, dma, dma, dma,
            dma((2, nr)), dma((2, nr)), dma((2, nr)), dma((2, nr)), dma, dma((2,)),
        ],
        compiler_params=pltpu.CompilerParams(collective_id=0, has_side_effects=True, vmem_limit_bytes=limit),
        name="fit_gather",
    )(amplitudes.T, aux_left, aux_right, left_rotation)

    cols_pad = up(cols, 128)
    tiles = up(cols_pad, WIDE) // WIDE
    cuts = [(at, min(256, half - at)) for at in range(0, half, 256)]
    r, c = lax.axis_index("row"), lax.axis_index("col")
    vir_here = lax.dynamic_slice_in_dim(vir_energy, c * vc, vc)
    occ_here = lax.dynamic_slice_in_dim(occ_energy, r * og, og)
    rowd = (vir_here[None, :, None] - occ_energy.reshape(nr, 1, og)).reshape(nr, rows)
    rowd = jnp.pad(rowd, ((0, 0), (0, wide_pad - rows)), constant_values=1.0).reshape(nr * wide_pad, 1)
    rowd = jnp.broadcast_to(rowd, (nr * wide_pad, 128))
    cold = (vir_energy[None, :] - occ_here[:, None]).reshape(1, cols)
    cold = jnp.pad(cold, ((0, 0), (0, cols_pad - cols)), constant_values=1.0)
    cold = jnp.broadcast_to(cold, (8, cols_pad))

    moved = pl.pallas_call(
        functools.partial(tile_kernel, nr, og, vc, tiles, cuts),
        out_shape=jax.ShapeDtypeStruct((nr, pad, cols_pad), F32),
        in_specs=[vmem, hbm, hbm] + [vmem] * 4,
        out_specs=hbm,
        scratch_shapes=[
            pltpu.VMEM((nr, piece, half), F32),
            pltpu.VMEM((nr, 2 * pad, half), F32),
            pltpu.VMEM((nr, piece, half), F32),
            pltpu.VMEM((vir + va, vir), BF16),
            pltpu.VMEM((vir + va, vir), BF16),
            pltpu.VMEM((cols_pad, naux), BF16),
            pltpu.VMEM((cols_pad, naux), BF16),
            pltpu.VMEM((half // 128, 2 * pad, 128), F32),
            pltpu.VMEM((2 * pad, half), F32),
            pltpu.VMEM((nr, 2 * pad, half), F32),
            pltpu.VMEM((2, nr * wide_pad, naux), BF16),
            pltpu.VMEM((2, nr * wide_pad, naux), BF16),
            pltpu.VMEM((2, nr * wide_pad, WIDE), F32),
            pltpu.VMEM((tiles, nr * wide_pad, WIDE), F32),
            pltpu.VMEM((nr * wide_pad, cols_pad), F32),
            dma((len(cuts), nr)), dma((len(cuts), nr)),
            dma((len(cuts), nr)), dma((len(cuts), nr)), dma((2,)), dma((tiles,)),
            dma((tiles, nr)), dma((tiles, nr)), dma((tiles,)), dma((2,)),
        ],
        compiler_params=pltpu.CompilerParams(collective_id=1, has_side_effects=True, vmem_limit_bytes=limit),
        name="tile_exchange",
    )(fp, zg, xz, left_rotation, right_rotation, rowd, cold)

    out = pl.pallas_call(
        functools.partial(lay_kernel, nr, og, vir, occ),
        grid=(pl.cdiv(pad, 24),),
        out_shape=jax.ShapeDtypeStruct((rows * occ, vir), F32),
        in_specs=[pl.BlockSpec((nr, 24, cols_pad), lambda g: (0, g, 0))],
        out_specs=pl.BlockSpec((24 * occ, vir), lambda g: (g, 0)),
        compiler_params=pltpu.CompilerParams(vmem_limit_bytes=limit),
        name="lay_out",
    )(moved)
    return out.reshape(vc, og, occ, vir)


def solution(mesh):
    placed = (P("row", "col"), P("col", None), P("col", None), P(), P(), P(), P())
    return jax.shard_map(
        shards, mesh=mesh, in_specs=placed, out_specs=P("col", "row", None, None), check_vma=False
    )
```
